32 devices in a mesh: gx: 8 (over z, x), gy: 4 (over y, core).
Axes of the slice: x: 2, y: 2, z: 4, core: 2. Of those that a mesh axis runs over, the one named last changes fastest.
Arguments:
- control: float32 [2, 32, 256, 1024], P(None, None, 'gx', 'gy'), may hold values from -6 to 6
- band_roots: float32 [16, 32, 32], replicated, may hold values from -1 to 1
Outputs:
- increment: float32 [2, 32, 256, 1024], P(None, None, 'gx', 'gy')
The draws below stay inside these ranges and needn't reach their ends.
All inputs are finite; a program needn't handle non-finite values.
Results may differ from the reference program's by a relative error of at most 0.000053.
Values sent between devices are 32-bit elements; how exact they have to be, the bound alone decides.
No kernel may reach another device: no remote copies, remote signals or barrier semaphores. Data moves between devices by JAX's collectives and lax.ppermute only.
A program may use at most 64 MiB of HBM per device.

```python
import jax
import jax.numpy as jnp
from jax import lax

L = 32
LEVELS = 5
BANDS = 16
NV = 2
NX = 256
NY = 1024


def block_scale(key, extent, cuts, least, largest):
    def one(position, shards_of):
        draws = jax.random.uniform(jax.random.fold_in(jax.random.fold_in(key, 6), position), (shards_of,), jnp.float32, least / len(cuts), largest / len(cuts))
        return jnp.repeat(jnp.exp(draws), extent[position] // shards_of).reshape((-1,) + (1,) * (len(extent) - position - 1))

    factor_of = one(*cuts[0])
    for cut in cuts[1:]:
        factor_of = factor_of * one(*cut)
    return factor_of


def bell_draw(key, shape, scale, most, shards=(), kind=jnp.bfloat16):
    loudness = block_scale(key, shape, shards, -0.22, 0.18) if shards else 1.0
    drawn = jax.random.normal(key, shape, jnp.float32) * scale * loudness
    return jnp.minimum(jnp.maximum(drawn, -most), most).astype(kind)


def setup_inputs(seed: int = 0) -> dict:
    keys = jax.random.split(jax.random.key(seed), 3)
    return {
        "control": bell_draw(keys[0], (NV, L, NX, NY), 1.0, 6.0, ((2, 8), (3, 4)), jnp.float32),
        "band_roots": bell_draw(keys[1], (BANDS, L, L), L ** -0.5, 1.0, (), jnp.float32),
    }


def slab_of(source, begin_at, end_at, stride, dimension):
    return lax.slice_in_dim(source, begin_at, end_at, stride, dimension)


def alternate(even_part, odd_part, dimension):
    joined = jnp.stack([even_part, odd_part], dimension + 1)
    shape_out = list(even_part.shape)
    shape_out[dimension] = shape_out[dimension] * 2
    return joined.reshape(shape_out)


def forward_lift(signal, dimension):
    length = signal.shape[dimension]
    half_len = length // 2
    even_part = slab_of(signal, 0, length, 2, dimension)
    odd_part = slab_of(signal, 1, length, 2, dimension)
    edge = jnp.zeros_like(slab_of(even_part, 0, 1, 1, dimension))
    after_part = jnp.concatenate([slab_of(even_part, 1, half_len, 1, dimension), edge], dimension)
    detail = odd_part - 0.5 * (even_part + after_part)
    before = jnp.concatenate([edge, slab_of(detail, 0, half_len - 1, 1, dimension)], dimension)
    smooth = even_part + 0.25 * (before + detail)
    return smooth, detail


def inverse_lift(smooth, detail, dimension):
    half_len = smooth.shape[dimension]
    edge = jnp.zeros_like(slab_of(detail, 0, 1, 1, dimension))
    before = jnp.concatenate([edge, slab_of(detail, 0, half_len - 1, 1, dimension)], dimension)
    even_part = smooth - 0.25 * (before + detail)
    after_part = jnp.concatenate([slab_of(even_part, 1, half_len, 1, dimension), edge], dimension)
    odd_part = detail + 0.5 * (even_part + after_part)
    return alternate(even_part, odd_part, dimension)


def vertical(band_roots, band_index, coeffs):
    return jnp.einsum("lm,nmxy->nlxy", band_roots[band_index], coeffs, precision=lax.Precision.HIGHEST)


def analyse(signal):
    vectors = signal.shape[0]
    smooth, detail = forward_lift(signal, 2)
    stacked = jnp.concatenate([smooth, detail], 0)
    upper, lower = forward_lift(stacked, 3)
    return upper[:vectors], (lower[:vectors], upper[vectors:], lower[vectors:])


def synthesise(coarse, band_list):
    vectors = coarse.shape[0]
    rows_smooth = jnp.concatenate([coarse, band_list[1]], 0)
    rows_detail = jnp.concatenate([band_list[0], band_list[2]], 0)
    both = inverse_lift(rows_smooth, rows_detail, 3)
    return inverse_lift(both[:vectors], both[vectors:], 2)


def reference(control, band_roots):
    def descend(signal, level_now):
        if level_now == LEVELS:
            return vertical(band_roots, 3 * LEVELS, signal)
        coarse, band_list = analyse(signal)
        band_list = tuple(vertical(band_roots, 3 * level_now + offset, member) for offset, member in enumerate(band_list))
        return synthesise(descend(coarse, level_now + 1), band_list)

    return descend(control, 0)
```

```python
from functools import lru_cache, partial

import jax
import jax.numpy as jnp
import numpy as np
from jax import lax
from jax.experimental import pallas as pl
from jax.experimental.pallas import tpu as pltpu
from jax.sharding import PartitionSpec as P

LEVELS = 5
HALO = 2 ** (LEVELS + 1)
TILE = 128
BF = jnp.bfloat16
F32 = jnp.float32


def lift_np(signal):
    even, odd = signal[0::2], signal[1::2]
    zero = np.zeros_like(even[:1])
    detail = odd - 0.5 * (even + np.concatenate([even[1:], zero]))
    return even + 0.25 * (np.concatenate([zero, detail[:-1]]) + detail), detail


def unlift_np(smooth, detail):
    zero = np.zeros_like(smooth[:1])
    even = smooth - 0.25 * (np.concatenate([zero, detail[:-1]]) + detail)
    odd = detail + 0.5 * (even + np.concatenate([even[1:], zero]))
    return np.stack([even, odd], 1).reshape(2 * even.shape[0], -1)


def lane_plan(ny):
    place, lane = {}, 0
    spans = {}
    for k in list(range(3, LEVELS + 1)) + [1, 2]:
        n = ny >> k
        first = lane
        for kind, lo in (("s", 0), ("d", -1)):
            start = lane
            for i in range(lo, n + 1):
                if k <= 2 and 0 <= i < n:
                    place[k, kind, i] = (f"m{k}", i + (n if kind == "d" else 0))
                else:
                    place[k, kind, i] = ("c", lane)
                    lane += 1
            spans[k, kind] = (start, lane)
        spans[k] = (first, lane)
    assert lane <= TILE
    return place, spans


@lru_cache(None)
def y_matrices(ny, below, above):
    place, _ = lane_plan(ny)
    off = ny if below else 0
    size = off + ny + (ny if above else 0)
    width = {"m1": ny, "m2": ny // 2, "c": TILE}
    ana = {a: np.zeros((ny + 2 * HALO, w)) for a, w in width.items()}
    syn = {a: np.zeros((w, ny)) for a, w in width.items()}
    s = np.eye(size)
    for k in range(1, LEVELS + 1):
        s, d = lift_np(s)
        for kind, mat in (("s", s), ("d", d)):
            n, o = size >> k, off >> k
            for i in range(0 if kind == "s" else -1, (ny >> k) + 1):
                if not 0 <= o + i < n:
                    continue
                arr, lane = place[k, kind, i]
                row = mat[o + i]
                ana[arr][:ny, lane] = row[off : off + ny]
                if below:
                    ana[arr][ny : ny + HALO, lane] = row[off - HALO : off]
                if above:
                    ana[arr][ny + HALO :, lane] = row[off + ny : off + ny + HALO]
                unit = np.zeros((n, 1))
                unit[o + i] = 1.0
                zero = np.zeros_like(unit)
                back = unlift_np(unit, zero) if kind == "s" else unlift_np(zero, unit)
                for _ in range(k - 1):
                    back = unlift_np(back, np.zeros_like(back))
                syn[arr][lane] = back[off : off + ny, 0]
    return ana, syn


def split_np(mat):
    hi = mat.astype(np.float32).astype(jnp.bfloat16)
    lo = (mat - hi.astype(np.float64)).astype(np.float32).astype(jnp.bfloat16)
    return hi, lo


@lru_cache(None)
def y_constants(ny, count):
    if count == 1:
        kinds = [(False, False)]
    else:
        kinds = [(False, True), (True, True), (True, False)]
    a_hi, a_lo, s_hi = [], [], []
    for below, above in kinds:
        ana, syn = y_matrices(ny, below, above)
        hi, lo = split_np(np.concatenate([ana["m1"], ana["m2"], ana["c"]], 1))
        width = ny + ny // 2
        assert not np.any(lo[:, :width].astype(np.float32))
        shi, slo = split_np(np.concatenate([syn["m1"], syn["m2"], syn["c"]], 0))
        assert not np.any(slo.astype(np.float32))
        a_hi.append(hi)
        a_lo.append(lo[:, width:])
        s_hi.append(shi)
    return np.stack(a_hi), np.stack(a_lo), np.stack(s_hi)


@lru_cache(None)
def row_plan(nx):
    ranges, low, high = {}, 0, nx - 1
    for k in range(1, LEVELS + 1):
        n = nx >> k
        d_low, d_high = (low - 2 + 1) // 2, high // 2
        s_low, s_high = d_low, max(high // 2, d_high + 1)
        ranges[k, "d"], ranges[k, "s"] = (d_low, d_high), (s_low, s_high)
        assert d_low == -1 and s_low == -1 and d_high <= n and s_high <= n + 1
        low, high = s_low, s_high
    first, total = {}, 0
    for key, (a, b) in ranges.items():
        first[key] = total
        total += b - a + 1
    need, count = {}, 0
    for k in range(1, LEVELS + 1):
        n = nx >> k
        for kind, a in (("d", -1), ("s", 0)):
            need[k, kind] = (count, a, n)
            count += n - a + 1
    return ranges, first, total, need, count


def split(value):
    hi = value.astype(BF)
    return hi, (value - hi.astype(F32)).astype(BF)


def dot(a, b):
    return jnp.dot(a, b, preferred_element_type=F32)


def lanes():
    return lax.broadcasted_iota(jnp.int32, (1, TILE), 1)


def in_span(span):
    lane = lanes()
    return (lane >= span[0]) & (lane < span[1])


def pack_kernel(x_ref, up_ref, down_ref):
    half = x_ref.shape[1] // 2
    ny = x_ref.shape[2]
    low_half = lax.broadcasted_iota(jnp.int32, (1, 1, TILE), 2) < HALO
    last = x_ref[:, :, ny - TILE :]
    up_ref[...] = jnp.where(low_half, pltpu.roll(last[:, :half], HALO, 2), last[:, half:])
    first = x_ref[:, :, :TILE]
    down_ref[...] = jnp.where(low_half, first[:, :half], pltpu.roll(first[:, half:], HALO, 2))


def analyse_rows(nx, edge_ref, x_refs, lo_ref, hi_ref, rows, xh, xl):
    ranges, first, _, _, _ = row_plan(nx)
    g = x_refs[0].shape[0] // nx
    half = nx // 2
    low_half = lanes() < HALO
    not_first, not_last = edge_ref[0], edge_ref[1]

    def raw(i):
        a = lo_ref[pl.ds(i % half, g, stride=half), :]
        b = hi_ref[pl.ds(i % half, g, stride=half), :]
        if i < half:
            b = pltpu.roll(b, HALO, 1)
        else:
            a = pltpu.roll(a, HALO, 1)
        own = [ref[pl.ds(i, g, stride=nx), :] for ref in x_refs]
        return jnp.concatenate(own + [jnp.where(low_half, a, b)], 1)

    low, high = 0, nx - 1
    fetch = raw
    for k in range(1, LEVELS + 1):
        n = nx >> k
        (d_low, d_high), (s_low, s_high) = ranges[k, "d"], ranges[k, "s"]

        def get(i, low=low, high=high, fetch=fetch):
            return fetch(i) if low <= i <= high else None

        def add(*terms):
            terms = [t for t in terms if t is not None]
            return None if not terms else terms[0] if len(terms) == 1 else terms[0] + terms[1]

        before = None
        after = None
        for i in range(s_low, s_high + 1):
            even = after if i > s_low else get(2 * i)
            detail = None
            after = get(2 * i + 2)
            if d_low <= i <= d_high:
                mid, pair = get(2 * i + 1), add(even, after)
                detail = -0.5 * pair if mid is None else mid if pair is None else mid - 0.5 * pair
                if i < 0:
                    detail = detail * not_first
                h, l = split(detail)
                xh[first[k, "d"] + i - d_low] = h
                xl[first[k, "d"] + i - d_low] = l
            pair = add(before, detail)
            smooth = even if pair is None else 0.25 * pair if even is None else even + 0.25 * pair
            if i >= n:
                smooth = smooth * not_last
            r = first[k, "s"] + i - s_low
            rows[r] = smooth
            h, l = split(smooth)
            xh[r] = h
            xl[r] = l
            before = detail
        low, high = s_low, s_high
        base = first[k, "s"] - s_low
        fetch = lambda i, base=base: rows[base + i]


def y_rows(xh, xl, r, count, a_ref, columns, lo_ref=None):
    g, w = xh.shape[1], xh.shape[2]
    hi = xh[r : r + count].reshape(count * g, w)
    lo = xl[r : r + count].reshape(count * g, w)
    mat = a_ref[0, :, columns]
    out = dot(hi, mat) + dot(lo, mat)
    if lo_ref is not None:
        out = out + dot(hi, lo_ref[0])
    return out.reshape(count, g, out.shape[1])


def send_kernel(nx, far, edge_ref, var_ref, xa_ref, xb_ref, lo_ref, hi_ref, a_ref, alo_ref, *rest):
    if far:
        up_ref, down_ref, up2_ref, down2_ref, rows, xh, xl = rest
    else:
        up_ref, down_ref, rows, xh, xl = rest
    ny = 2 * TILE
    _, spans = lane_plan(ny)
    ranges, first, _, _, _ = row_plan(nx)
    analyse_rows(nx, edge_ref, (xa_ref, xb_ref), lo_ref, hi_ref, rows, xh, xl)
    m1, m1d = slice(0, ny), slice(ny // 2, ny)
    m2, c = slice(ny, ny + ny // 2), slice(ny + ny // 2, ny + ny // 2 + TILE)

    def place(ref, tile, value):
        for t in range(value.shape[1] // TILE):
            ref[tile + t] = value[:, t * TILE : (t + 1) * TILE]

    def row(k, kind, i):
        return first[k, kind] + i - ranges[k, kind][0]

    n1, n2 = nx >> 1, nx >> 2
    place(up_ref, 0, y_rows(xh, xl, row(1, "d", n1 - 1), 1, a_ref, m1)[0])
    two = y_rows(xh, xl, row(2, "d", n2 - 1), 2, a_ref, m2)
    up_ref[2], up_ref[3] = two[0], two[1]
    up_ref[4] = y_rows(xh, xl, row(2, "s", n2), 1, a_ref, m2)[0]
    two = y_rows(xh, xl, row(1, "d", -1), 2, a_ref, m1)
    place(down_ref, 0, two[0])
    place(down_ref, 2, two[1])
    down_ref[4] = y_rows(xh, xl, row(1, "s", 0), 1, a_ref, m1d)[0]
    two = y_rows(xh, xl, row(2, "d", -1), 2, a_ref, m2)
    down_ref[5], down_ref[6] = two[0], two[1]
    down_ref[7] = y_rows(xh, xl, row(2, "s", 0), 1, a_ref, m2)[0]

    acc = [jnp.zeros(up_ref.shape[1:], F32)] * 6
    for k in range(1, LEVELS + 1):
        n, here = nx >> k, in_span(spans[k])

        def edges(kind, i, count, k=k):
            return y_rows(xh, xl, row(k, kind, i), count, a_ref, c, alo_ref)

        if k == 1:
            top = [edges("d", n - 1, 1)[0], None]
            ends = None
        else:
            top = edges("d", n - 1, 2)
            ends = edges("s", n, 1)[0]
        bottom = edges("d", -1, 2)
        begin = edges("s", 0, 1)[0]
        new = [top[0], top[1], ends, bottom[0], bottom[1], begin]
        acc = [a if v is None else jnp.where(here, v, a) for a, v in zip(acc, new)]
    for t in range(3):
        up_ref[5 + t] = acc[t]
        down_ref[8 + t] = acc[3 + t]
    if far:
        here = in_span(spans[LEVELS])
        up2_ref[...] = jnp.where(here, acc[1], 0.0)
        down2_ref[...] = jnp.where(here, acc[3], 0.0)


def weigh(r_ref, bands, value):
    m = r_ref.shape[1]
    vectors = value.shape[0] // m
    hi, lo = split(value)
    out = [[] for _ in bands]
    mats = [r_ref[b] for b in bands]
    mat = mats[0] if len(mats) == 1 else jnp.concatenate(mats, 0)
    for v in range(vectors):
        part = slice(v * m, (v + 1) * m)
        rhs = jnp.concatenate([hi[part], hi[part], lo[part]], 0)
        res = dot(mat, rhs)
        for j in range(len(bands)):
            out[j].append(res[j * m : (j + 1) * m])
    return [jnp.concatenate(o, 0) for o in out]


def band_of(k, kind, y_kind):
    if kind == "s":
        return 3 * LEVELS if y_kind == "s" else 3 * (k - 1)
    return 3 * (k - 1) + (1 if y_kind == "s" else 2)


def weigh_c(r_ref, spans, kind, levels, value):
    which = [
        (k, y_kind)
        for k in levels
        for y_kind in ("s", "d")
        if kind == "d" or y_kind == "d" or k == LEVELS
    ]
    res = weigh(r_ref, [band_of(k, kind, y_kind) for k, y_kind in which], value)
    out = jnp.zeros_like(value)
    for (k, y_kind), r in zip(which, res):
        out = jnp.where(in_span(spans[k, y_kind]), r, out)
    return out


def weigh_m2(r_ref, kind, value):
    lane_d = lanes() >= TILE // 2 if value.shape[1] == TILE else None
    if kind == "s":
        return jnp.where(lane_d, weigh(r_ref, [band_of(2, "s", "d")], value)[0], 0.0)
    a, b = weigh(r_ref, [band_of(2, "d", "s"), band_of(2, "d", "d")], value)
    return jnp.where(lane_d, b, a)


def y_back(parts, s_ref):
    out = None
    for (hi, lo), rows in parts:
        mat = s_ref[0, rows, :]
        term = dot(hi, mat) + dot(lo, mat)
        out = term if out is None else out + term
    return out


def local_kernel(nx, edge_ref, var_ref, xa_ref, xb_ref, lo_ref, hi_ref, a_ref, alo_ref, s_ref, r_ref,
                 v_ref, rows, xh, xl, y1d, y1s, y2, cc, wh1d, wl1d, wh1s, wl1s, wh2, wl2, whc, wlc):
    ny = 2 * TILE
    _, spans = lane_plan(ny)
    ranges, first, _, need, _ = row_plan(nx)
    g = xh.shape[1]
    analyse_rows(nx, edge_ref, (xa_ref, xb_ref), lo_ref, hi_ref, rows, xh, xl)
    m1, m1d = slice(0, ny), slice(ny // 2, ny)
    m2, c = slice(ny, ny + ny // 2), slice(ny + ny // 2, ny + ny // 2 + TILE)
    n1, n2 = nx >> 1, nx >> 2

    def span_rows(k, kind):
        _, a, b = need[k, kind]
        low, high = ranges[k, kind]
        b = min(b, high)
        return first[k, kind] + a - low, b - a + 1

    r, n = span_rows(1, "d")
    y1d[0:n] = y_rows(xh, xl, r, n, a_ref, m1)
    count1d = n
    r, n = span_rows(1, "s")
    y1s[0:n] = y_rows(xh, xl, r, n, a_ref, m1d)
    r, n2d = span_rows(2, "d")
    y2[0:n2d] = y_rows(xh, xl, r, n2d, a_ref, m2)
    r, n2s = span_rows(2, "s")
    y2[n2d : n2d + n2s] = y_rows(xh, xl, r, n2s, a_ref, m2)
    slots_d = count1d
    slots_s = n1 + 1
    for kind, base in (("d", 0), ("s", slots_d)):
        for k in range(1, LEVELS + 1):
            r, n = span_rows(k, kind)
            res = y_rows(xh, xl, r, n, a_ref, c, alo_ref)
            if k == 1:
                cc[base : base + n] = res
            else:
                here = in_span(spans[k])
                cc[base : base + n] = jnp.where(here, res, cc[base : base + n])

    half = ny // 2

    def body1d(i, _):
        a = y1d[i]
        ws = weigh(r_ref, [band_of(1, "d", "s")], a[:, :half])[0]
        wd = weigh(r_ref, [band_of(1, "d", "d")], a[:, half:])[0]
        w = jnp.concatenate([ws, wd], 1)
        wh1d[i], wl1d[i] = split(w)
        return 0

    lax.fori_loop(0, count1d, body1d, 0)

    def body1s(i, _):
        wh1s[i], wl1s[i] = split(weigh(r_ref, [band_of(1, "s", "d")], y1s[i])[0])
        return 0

    lax.fori_loop(0, n1 + 1, body1s, 0)
    for i in range(n2d + n2s):
        wh2[i], wl2[i] = split(weigh_m2(r_ref, "d" if i < n2d else "s", y2[i]))
    for kind, base, slots, low in (("d", 0, slots_d, -1), ("s", slots_d, slots_s, 0)):
        for j in range(slots):
            levels = [k for k in range(1, LEVELS + 1) if j + low <= nx >> k]
            whc[base + j], wlc[base + j] = split(weigh_c(r_ref, spans, kind, levels, cc[base + j]))

    rm1, rm1d = slice(0, ny), slice(half, ny)
    rm2, rc = slice(ny, ny + half), slice(ny + half, ny + half + TILE)
    for kind, base in (("d", 0), ("s", slots_d)):
        for k in range(1, LEVELS + 1):
            at, _, _ = need[k, kind]
            _, n = span_rows(k, kind)
            here = in_span(spans[k])

            def masked(ref):
                val = ref[base : base + n].reshape(n * g, TILE)
                return jnp.where(here, val, jnp.zeros_like(val))

            parts = [((masked(whc), masked(wlc)), rc)]
            if k == 1:
                hi, lo = (wh1d, wl1d) if kind == "d" else (wh1s, wl1s)
                w = hi.shape[2]
                pair = tuple(ref[0:n].reshape(n * g, w) for ref in (hi, lo))
                parts.append((pair, rm1 if kind == "d" else rm1d))
            if k == 2:
                o = 0 if kind == "d" else n2d
                parts.append((tuple(ref[o : o + n].reshape(n * g, half) for ref in (wh2, wl2)), rm2))
            v_ref[at : at + n] = y_back(parts, s_ref).reshape(n, g, ny)
    at, _, _ = need[1, "d"]
    v_ref[at + count1d] = jnp.zeros((g, ny), F32)


def final_kernel(nx, far, edge_ref, var_ref, v_ref, up_ref, down_ref, *rest):
    if far:
        up2_ref, down2_ref, s_ref, r_ref, out_ref, wc_h, wc_l, rows, oa_ref, ob_ref, sem = rest
    else:
        s_ref, r_ref, out_ref, wc_h, wc_l, rows, oa_ref, ob_ref, sem = rest
    g, ny = v_ref.shape[1], v_ref.shape[2]
    _, spans = lane_plan(ny)
    _, _, _, need, _ = row_plan(nx)
    half = ny // 2
    n1, n2 = nx >> 1, nx >> 2
    lane = lanes()
    lane_d = lane >= TILE // 2
    s_lanes = in_span(spans[LEVELS])
    for k in range(1, LEVELS):
        s_lanes = s_lanes | in_span(spans[k, "d"])

    def smooth_c(value):
        return jnp.where(s_lanes, 0.25 * value, 0.0)

    lev1, deep = in_span(spans[1]), ~in_span(spans[1])
    extra = {}

    def put(key, value):
        extra.setdefault(key, []).append(value)

    c_d = {-1: up_ref[5], 0: up_ref[6], "n-1": down_ref[8], "n": down_ref[9]}
    c_s = {
        0: up_ref[7] + jnp.where(lev1, smooth_c(c_d[-1]), 0.0),
        1: smooth_c(c_d[0]),
        "n-1": smooth_c(c_d["n-1"]),
        "n": down_ref[10],
    }
    if far:
        c_d[-1] = c_d[-1] + up2_ref[...]
        c_s[0] = c_s[0] + smooth_c(up2_ref[...])
        c_d["n"] = c_d["n"] + down2_ref[...]
        c_s["n"] = c_s["n"] + smooth_c(down2_ref[...])
    m1 = {
        ("d", -1): jnp.concatenate([up_ref[0], up_ref[1]], 1),
        ("d", "n-1"): jnp.concatenate([down_ref[0], down_ref[1]], 1),
        ("d", "n"): jnp.concatenate([down_ref[2], down_ref[3]], 1),
        ("s", 0): 0.25 * up_ref[1],
        ("s", "n-1"): 0.25 * down_ref[1],
        ("s", "n"): down_ref[4],
    }
    m2 = {
        ("d", -1): up_ref[2],
        ("d", 0): up_ref[3],
        ("d", "n-1"): down_ref[5],
        ("d", "n"): down_ref[6],
        ("s", 0): up_ref[4],
        ("s", 1): 0.25 * up_ref[3],
        ("s", "n-1"): 0.25 * down_ref[5],
        ("s", "n"): down_ref[7],
    }
    rm1, rm1d = slice(0, ny), slice(half, ny)
    rm2, rc = slice(ny, ny + half), slice(ny + half, ny + half + TILE)

    w1, w2 = {}, {}
    for key, value in m1.items():
        if key[0] == "d":
            ws = weigh(r_ref, [band_of(1, "d", "s")], value[:, :half])[0]
            wd = weigh(r_ref, [band_of(1, "d", "d")], value[:, half:])[0]
            w1[key] = split(jnp.concatenate([ws, wd], 1))
        else:
            w1[key] = split(weigh(r_ref, [band_of(1, "s", "d")], value)[0])
    for key, value in m2.items():
        w2[key] = split(weigh_m2(r_ref, key[0], value))
    every = list(range(1, LEVELS + 1))
    slot = 0
    where = {}
    for kind, tiles in (("d", c_d), ("s", c_s)):
        for key, value in tiles.items():
            where[kind, key] = slot
            wc_h[slot], wc_l[slot] = split(weigh_c(r_ref, spans, kind, every, value))
            slot += 1
    for k in every:
        here = in_span(spans[k])
        hi = jnp.where(here, wc_h[...].reshape(8 * g, TILE), jnp.zeros((), BF))
        lo = jnp.where(here, wc_l[...].reshape(8 * g, TILE), jnp.zeros((), BF))
        res = y_back([((hi, lo), rc)], s_ref)
        for (kind, key), j in where.items():
            if k == 1 and key in (0, 1) and (kind, key) != ("s", 0):
                continue
            part = res[j * g : (j + 1) * g]
            if k == 1:
                part = part + y_back([(w1[kind, key], rm1 if kind == "d" else rm1d)], s_ref)
            if k == 2:
                part = part + y_back([(w2[kind, key], rm2)], s_ref)
            n = nx >> k
            i = n - 1 if key == "n-1" else n if key == "n" else key
            put((k, kind, i), part)

    not_last = edge_ref[1]

    def value_of(k, kind, i):
        at, a, _ = need[k, kind]
        v = v_ref[at + i - a]
        for e in extra.get((k, kind, i), []):
            v = v + e
        return v

    coarse = None
    for k in range(LEVELS, 0, -1):
        n = nx >> k
        below = value_of(k, "d", -1)
        even_before = None
        for i in range(n + 1):
            smooth = value_of(k, "s", i)
            if coarse is not None:
                smooth = smooth + rows[coarse + i]
            detail = value_of(k, "d", i)
            even = smooth - 0.25 * (below + detail)
            if i == n:
                even = even * not_last
            if even_before is not None:
                odd = below + 0.5 * (even_before + even)
            if k > 1:
                base = level_base(nx, k)
                rows[base + 2 * i] = even
                if even_before is not None:
                    rows[base + 2 * i - 1] = odd
            else:
                for ref, cols in ((oa_ref, slice(0, TILE)), (ob_ref, slice(TILE, 2 * TILE))):
                    if i < n:
                        ref[pl.ds(2 * i, g, stride=nx), :] = even[:, cols]
                    if even_before is not None:
                        ref[pl.ds(2 * i - 1, g, stride=nx), :] = odd[:, cols]
            even_before, below = even, detail
        coarse = level_base(nx, k)
    copies = [
        pltpu.make_async_copy(ref, out_ref.at[:, pl.ds(j * TILE, TILE)], sem.at[j])
        for j, ref in enumerate((oa_ref, ob_ref))
    ]
    for copy in copies:
        copy.start()
    for copy in copies:
        copy.wait()


def level_base(nx, k):
    return sum((nx >> (j - 1)) + 1 for j in range(k + 1, LEVELS + 1))


def shift(value, axis, step):
    count = lax.axis_size(axis)
    pairs = [(i, i + step) for i in range(count) if 0 <= i + step < count]
    return lax.ppermute(value, axis, pairs)


def per_device(control, band_roots):
    vectors, m, nx, ny = control.shape
    g = vectors * m
    half = ny // 2
    gx, gy = lax.axis_size("gx"), lax.axis_size("gy")
    assert half == TILE and nx % 16 == 0
    far = (nx >> LEVELS) < 2 and gx > 2
    a_np, alo_np, s_np = y_constants(ny, gy)
    width = ny + 2 * HALO
    _, _, total, need, count = row_plan(nx)

    ix, iy = lax.axis_index("gx"), lax.axis_index("gy")
    edge = jnp.stack([ix > 0, ix < gx - 1]).astype(F32)
    which = jnp.where(iy == 0, 0, jnp.where(iy == gy - 1, 2, 1)) if gy > 1 else jnp.zeros((), jnp.int32)
    which = which.astype(jnp.int32).reshape(1)
    r_hi = lax.reduce_precision(band_roots, 8, 7)
    r_lo = band_roots - r_hi
    roots = jnp.concatenate([r_hi.astype(BF), r_lo.astype(BF), r_hi.astype(BF)], 2)

    vmem = pl.BlockSpec(memory_space=pltpu.VMEM)
    rows3 = control.reshape(g, nx, ny)
    rows2 = control.reshape(g * nx, ny)
    pack = jax.ShapeDtypeStruct((g, nx // 2, TILE), F32)
    up, down = pl.pallas_call(
        pack_kernel, out_shape=(pack, pack), in_specs=[vmem], out_specs=(vmem, vmem), name="pack"
    )(rows3)
    lo = shift(up, "gy", 1).reshape(g * nx // 2, TILE)
    hi = shift(down, "gy", -1).reshape(g * nx // 2, TILE)

    def full(shape):
        return pl.BlockSpec(shape, lambda i, e, v: (0,) * len(shape))

    def variant(shape):
        return pl.BlockSpec((1,) + shape, lambda i, e, v: (v[0], 0, 0))

    a_mat, alo_mat, s_mat = jnp.asarray(a_np), jnp.asarray(alo_np), jnp.asarray(s_np)
    a_spec, alo_spec, s_spec = (variant(t.shape[1:]) for t in (a_mat, alo_mat, s_mat))
    x_spec = [pl.BlockSpec((g * nx, TILE), lambda i, e, v, j=j: (0, j)) for j in (0, 1)]
    halo_spec = full((g * nx // 2, TILE))
    scratch = [
        pltpu.VMEM((total, g, width), F32),
        pltpu.VMEM((total, g, width), BF),
        pltpu.VMEM((total, g, width), BF),
    ]

    def call(kernel, ins, outs, scratches, name, out_specs=None):
        specs = [s for _, s in ins]
        return pl.pallas_call(
            kernel,
            out_shape=tuple(jax.ShapeDtypeStruct(s, F32) for s in outs),
            grid_spec=pltpu.PrefetchScalarGridSpec(
                num_scalar_prefetch=2,
                grid=(1,),
                in_specs=specs,
                out_specs=out_specs or tuple(full(s) for s in outs),
                scratch_shapes=scratches,
            ),
            name=name,
        )(edge, which, *[a for a, _ in ins])

    base_ins = [(rows2, x_spec[0]), (rows2, x_spec[1]), (lo, halo_spec), (hi, halo_spec), (a_mat, a_spec), (alo_mat, alo_spec)]
    tile = (g, TILE)
    sent = call(
        partial(send_kernel, nx, far),
        base_ins,
        [(8,) + tile, (11,) + tile] + ([tile, tile] if far else []),
        scratch,
        "send",
    )
    below = shift(sent[0], "gx", 1)
    above = shift(sent[1], "gx", -1)
    got = [(below, full((8,) + tile)), (above, full((11,) + tile))]
    if far:
        got += [(shift(sent[2], "gx", 2), full(tile)), (shift(sent[3], "gx", -2), full(tile))]

    n1, n2 = nx >> 1, nx >> 2
    slots = 2 * n1 + 2
    pair = lambda n, w: [pltpu.VMEM((n, g, w), BF)] * 2
    (v,) = call(
        partial(local_kernel, nx),
        base_ins + [(s_mat, s_spec), (roots, full(roots.shape))],
        [(count, g, ny)],
        scratch
        + [
            pltpu.VMEM((n1 + 1, g, ny), F32),
            pltpu.VMEM((n1 + 1, g, half), F32),
            pltpu.VMEM((2 * n2 + 3, g, half), F32),
            pltpu.VMEM((slots, g, TILE), F32),
        ]
        + pair(n1 + 1, ny)
        + pair(n1 + 1, half)
        + pair(2 * n2 + 3, half)
        + pair(slots, TILE),
        "local",
    )
    (out,) = call(
        partial(final_kernel, nx, far),
        [(v, full((count, g, ny)))] + got + [(s_mat, s_spec), (roots, full(roots.shape))],
        [(g * nx, ny)],
        pair(8, TILE)
        + [pltpu.VMEM((level_base(nx, 1), g, ny), F32)]
        + [pltpu.VMEM((g * nx, TILE), F32)] * 2
        + [pltpu.SemaphoreType.DMA((2,))],
        "final",
        (pl.BlockSpec(memory_space=pl.ANY),),
    )
    return out.reshape(control.shape)


def solution(mesh):
    in_specs = (P(None, None, "gx", "gy"), P())
    out_specs = P(None, None, "gx", "gy")
    return jax.shard_map(
        per_device, mesh=mesh, in_specs=in_specs, out_specs=out_specs, check_vma=False
    )
```

```python
from functools import lru_cache, partial

import jax
import jax.numpy as jnp
import numpy as np
from jax import lax
from jax.experimental import pallas as pl
from jax.experimental.pallas import tpu as pltpu
from jax.sharding import PartitionSpec as P

LEVELS = 5
TILE = 128
VMEM_LIMIT = 28 * 2**20
BF = jnp.bfloat16
F32 = jnp.float32


def lift_np(signal):
    even, odd = signal[0::2], signal[1::2]
    zero = np.zeros_like(even[:1])
    detail = odd - 0.5 * (even + np.concatenate([even[1:], zero]))
    return even + 0.25 * (np.concatenate([zero, detail[:-1]]) + detail), detail


def unlift_np(smooth, detail):
    zero = np.zeros_like(smooth[:1])
    even = smooth - 0.25 * (np.concatenate([zero, detail[:-1]]) + detail)
    odd = detail + 0.5 * (even + np.concatenate([even[1:], zero]))
    return np.stack([even, odd], 1).reshape(2 * even.shape[0], -1)


def lane_plan(ny):
    place, lane = {}, 0
    spans = {}
    for k in list(range(3, LEVELS + 1)) + [1, 2]:
        n = ny >> k
        first = lane
        for kind, lo in (("s", 0), ("d", -1)):
            start = lane
            for i in range(lo, n + 1):
                if k <= 2 and 0 <= i < n:
                    place[k, kind, i] = (f"m{k}", i + (n if kind == "d" else 0))
                else:
                    place[k, kind, i] = ("c", lane)
                    lane += 1
            spans[k, kind] = (start, lane)
        spans[k] = (first, lane)
    assert lane <= TILE
    return place, spans


SLOT = 16


def edge_lanes(side):
    out = []
    for k in range(1, LEVELS + 1):
        if side > 0:
            out += [(k, "d", -1)] + ([(k, "d", 0), (k, "s", 0)] if k > 1 else [])
        else:
            out += [(k, "d", -1), (k, "d", 0), (k, "s", 0)]
    assert len(out) <= SLOT
    return out


@lru_cache(None)
def y_matrices(ny, below, above):
    place, _ = lane_plan(ny)
    off = ny if below else 0
    size = off + ny + (ny if above else 0)
    width = {"m1": ny, "m2": ny // 2, "c": TILE}
    ana = {a: np.zeros((ny, w)) for a, w in width.items()}
    syn = {a: np.zeros((w, ny)) for a, w in width.items()}
    send = {side: np.zeros((ny, SLOT)) for side in (1, -1)}
    s = np.eye(size)
    for k in range(1, LEVELS + 1):
        s, d = lift_np(s)
        for kind, mat in (("s", s), ("d", d)):
            n, o, own = size >> k, off >> k, ny >> k
            for side in (1, -1):
                for lane, (level, what, i) in enumerate(edge_lanes(side)):
                    at = o + i + (own if side > 0 else 0)
                    if (level, what) == (k, kind) and 0 <= at < n:
                        send[side][:, lane] = mat[at][off : off + ny]
            for i in range(0 if kind == "s" else -1, own + 1):
                if not 0 <= o + i < n:
                    continue
                arr, lane = place[k, kind, i]
                ana[arr][:, lane] = mat[o + i][off : off + ny]
                unit = np.zeros((n, 1))
                unit[o + i] = 1.0
                zero = np.zeros_like(unit)
                back = unlift_np(unit, zero) if kind == "s" else unlift_np(zero, unit)
                for _ in range(k - 1):
                    back = unlift_np(back, np.zeros_like(back))
                syn[arr][lane] = back[off : off + ny, 0]
    return ana, syn, send


@lru_cache(None)
def y_received(ny):
    place, _ = lane_plan(ny)
    base = {"m1": 0, "m2": ny, "c": ny + ny // 2}
    mat = np.zeros((2 * SLOT, base["c"] + TILE))

    def put(row, k, kind, i, value):
        arr, lane = place[k, kind, i]
        mat[row, base[arr] + lane] += value

    for row, (k, kind, i) in enumerate(edge_lanes(1)):
        put(row, k, kind, i, 1.0)
        if kind == "d" and i == (-1 if k == 1 else 0):
            put(row, k, "s", i + 1, 0.25)
    for row, (k, kind, i) in enumerate(edge_lanes(-1)):
        n = ny >> k
        put(SLOT + row, k, kind, n + i, 1.0)
        if kind == "d" and i == -1:
            put(SLOT + row, k, "s", n - 1, 0.25)
    groups = TILE // SLOT
    return np.concatenate([np.tile(mat[:SLOT], (groups, 1)), np.tile(mat[SLOT:], (groups, 1))], 0)


def split_np(mat):
    hi = mat.astype(np.float32).astype(jnp.bfloat16)
    lo = (mat - hi.astype(np.float64)).astype(np.float32).astype(jnp.bfloat16)
    return hi, lo


@lru_cache(None)
def y_constants(ny, count):
    if count == 1:
        kinds = [(False, False)]
    else:
        kinds = [(False, True), (True, True), (True, False)]
    main, e_hi, e_lo, back = [], [], [], []
    for below, above in kinds:
        ana, syn, send = y_matrices(ny, below, above)
        hi, lo = split_np(np.concatenate([ana["m1"], ana["m2"]], 1))
        assert not np.any(lo.astype(np.float32))
        main.append(hi)
        edge = np.tile(np.concatenate([send[1], send[-1]], 1), (1, TILE // (2 * SLOT)))
        hi, lo = split_np(np.concatenate([ana["c"], edge], 1))
        e_hi.append(hi)
        e_lo.append(lo)
        hi, lo = split_np(np.concatenate([syn["m1"], syn["m2"], syn["c"]], 0))
        assert not np.any(lo.astype(np.float32))
        back.append(hi)
    return np.stack(main), np.stack(e_hi), np.stack(e_lo), np.stack(back), split_np(y_received(ny))[0]


def split(value):
    hi = value.astype(BF)
    return hi, (value - hi.astype(F32)).astype(BF)


def dot(a, b):
    return jnp.dot(a, b, preferred_element_type=F32)


def lanes():
    return lax.broadcasted_iota(jnp.int32, (1, TILE), 1)


def in_span(span):
    lane = lanes()
    return (lane >= span[0]) & (lane < span[1])


def first_kernel(nx, edge_ref, var_ref, x_ref, ehi_ref, elo_ref, xhl, yc_ref, one_ref, two_ref, xt, e3, sems):
    g, ny = xt.shape[1], xt.shape[2]
    consts = [
        pltpu.make_async_copy(ref.at[var_ref[0]], e3.at[pl.ds(j * ny, ny)], sems.at[nx + j])
        for j, ref in enumerate((ehi_ref, ehi_ref, elo_ref))
    ]
    copies = [pltpu.make_async_copy(x_ref.at[:, i], xt.at[i], sems.at[i]) for i in range(nx)]
    for copy in copies[:4] + consts + copies[4:]:
        copy.start()
    per = TILE // SLOT
    odd = var_ref[1] == 1
    for r in range(0, nx, per):
        up = down = None
        for q in range(r, r + per, 4):
            for i in range(q, q + 4):
                copies[i].wait()
                rows = slice(i * g, (i + 1) * g)
                hi, lo = split(xt[i])
                xhl[rows, 0:ny], xhl[rows, ny : 2 * ny], xhl[rows, 2 * ny : 3 * ny] = hi, lo, hi
            if q == 0:
                for copy in consts:
                    copy.wait()
            res = dot(xhl[q * g : (q + 4) * g], e3[...])
            for i in range(q, q + 4):
                part = res[(i - q) * g : (i - q + 1) * g]
                yc_ref[i] = part[:, 0:TILE]
                plain = part[:, TILE : 2 * TILE]
                turned = pltpu.roll(plain, SLOT, 1)
                group = lanes() // SLOT == i - r
                a, b = (plain, turned) if i % 2 == 0 else (turned, plain)
                up = jnp.where(group, a, 0.0 if up is None else up)
                down = jnp.where(group, b, 0.0 if down is None else down)
        one_ref[r // per] = jnp.where(odd, down, up)
        two_ref[r // per] = jnp.where(odd, up, down)


def main_kernel(nx, edge_ref, var_ref, xhl, a_ref, y_ref, a2):
    g, ny = y_ref.shape[1], a_ref.shape[1]
    a2[0:ny], a2[ny : 2 * ny] = a_ref[0], a_ref[0]
    step = 4
    for r in range(0, nx, step):
        res = dot(xhl[r * g : (r + step) * g, 0 : 2 * ny], a2[...])
        y_ref[r : r + step] = res.reshape(step, g, res.shape[1])


class Lift:
    def __init__(self, nx, raw, edge_ref, first=0, last=None):
        self.nx, self.raw = nx, raw
        self.first, self.last = first, nx - 1 if last is None else last
        self.not_first, self.not_last = edge_ref[0], edge_ref[1]
        self.known = {}

    def smooth(self, k, i):
        if k == 0:
            if not 0 <= i < self.nx:
                return None
            assert self.first <= i <= self.last
        if (k, "s", i) not in self.known:
            self.known[k, "s", i] = self.raw(i) if k == 0 else self.new_smooth(k, i)
        return self.known[k, "s", i]

    def detail(self, k, i):
        if (k, "d", i) not in self.known:
            self.known[k, "d", i] = self.new_detail(k, i)
        return self.known[k, "d", i]

    def new_detail(self, k, i):
        if not -1 <= i <= self.nx >> k:
            return None
        even, mid, after = (self.smooth(k - 1, j) for j in (2 * i, 2 * i + 1, 2 * i + 2))
        pair = plus(even, after)
        if pair is None:
            return mid
        out = -0.5 * pair if mid is None else mid - 0.5 * pair
        return out * self.not_first if i < 0 else out

    def new_smooth(self, k, i):
        if not -1 <= i <= (self.nx >> k) + 1:
            return None
        even = self.smooth(k - 1, 2 * i)
        pair = plus(self.detail(k, i - 1), self.detail(k, i))
        if pair is None:
            return even if even is None or i < self.nx >> k else even * self.not_last
        out = 0.25 * pair if even is None else even + 0.25 * pair
        return out * self.not_last if i >= self.nx >> k else out


def plus(a, b):
    return b if a is None else a if b is None else a + b


def c_slots(lift, spans, kind, low, high, s_lanes):
    out = []
    for i in range(low, high + 1):
        tile = None
        for k in range(1, LEVELS + 1):
            if i > lift.nx >> k:
                continue
            value = lift.detail(k, i) if kind == "d" else lift.smooth(k, i)
            if value is None:
                continue
            tile = jnp.where(in_span(spans[k]), value, 0.0 if tile is None else tile)
        out.append(jnp.where(s_lanes, tile, 0.0) if kind == "s" else tile)
    return out


def smooth_lanes(spans):
    ok = in_span(spans[LEVELS])
    for k in range(1, LEVELS):
        ok = ok | in_span(spans[k, "d"])
    return ok


def send_kernel(nx, far, edge_ref, var_ref, yc_ref, ym_ref, one_ref, two_ref, p_ref, *rest):
    up_ref, down_ref, cc_ref, z = rest[:4]
    rest = rest[4:]
    if far:
        up2_ref, down2_ref = rest[:2]
        rest = rest[2:]
    yc, yl, yh, p2 = rest
    g = yc.shape[1]
    mains = ym_ref.shape[2]
    ny = mains - TILE
    half = ny // 2
    _, spans = lane_plan(ny)
    n1, n2 = nx >> 1, nx >> 2
    n = 2 * TILE
    p2[0:n], p2[n : 2 * n] = p_ref[...], p_ref[...]
    per = TILE // SLOT
    group = lanes() // SLOT
    zero = jnp.zeros((g, TILE), BF)
    odd = var_ref[1] == 1
    for t in range(nx // per):
        from_below = jnp.where(odd, one_ref[t], two_ref[t])
        from_above = jnp.where(odd, two_ref[t], one_ref[t])
        pieces = split(from_below) + split(from_above)
        for i in range(per):
            here = group == i
            rows = slice((t * per + i) * g, (t * per + i + 1) * g)
            for c, j in enumerate((0, 2, 1, 3)):
                z[rows, c * TILE : (c + 1) * TILE] = jnp.where(here, pieces[j], zero)
    step = 4
    for r in range(0, nx, step):
        res = dot(z[r * g : (r + step) * g], p2[:, mains : mains + TILE])
        yc[r : r + step] = yc_ref[r : r + step] + res.reshape(step, g, TILE)
    low, high = yl.shape[0], yh.shape[0]
    yl[...] = ym_ref[0:low] + dot(z[0 : low * g], p2[:, 0:mains]).reshape(yl.shape)
    yh[...] = ym_ref[nx - high :] + dot(z[(nx - high) * g :], p2[:, 0:mains]).reshape(yh.shape)

    def place(ref, tile, value):
        for t in range(value.shape[1] // TILE):
            ref[tile + t] = value[:, t * TILE : (t + 1) * TILE]

    m1, m1d, m2 = slice(0, ny), slice(half, ny), slice(ny, ny + half)

    def lift(ref, base, columns, first, last):
        return Lift(nx, lambda i: ref[i - base, :, columns], edge_ref, first, last)

    top = nx - high
    place(up_ref, 0, lift(yh, top, m1, top, nx - 1).detail(1, n1 - 1))
    one = lift(yh, top, m2, top, nx - 1)
    up_ref[2], up_ref[3], up_ref[4] = one.detail(2, n2 - 1), one.detail(2, n2), one.smooth(2, n2)
    one = lift(yl, 0, m1, 0, low - 1)
    place(down_ref, 0, one.detail(1, -1))
    place(down_ref, 2, one.detail(1, 0))
    down_ref[4] = lift(yl, 0, m1d, 0, low - 1).smooth(1, 0)
    one = lift(yl, 0, m2, 0, low - 1)
    down_ref[5], down_ref[6], down_ref[7] = one.detail(2, -1), one.detail(2, 0), one.smooth(2, 0)

    s_lanes = smooth_lanes(spans)
    deep = Lift(nx, lambda i: yc[i], edge_ref)
    for j, tile in enumerate(c_slots(deep, spans, "d", -1, n1 - 1, s_lanes)):
        cc_ref[j] = tile
    for j, tile in enumerate(c_slots(deep, spans, "s", 0, n1, s_lanes)):
        cc_ref[n1 + 1 + j] = tile
    acc = [jnp.zeros((g, TILE), F32)] * 3
    for k in range(1, LEVELS + 1):
        n, here = nx >> k, in_span(spans[k])
        new = [deep.detail(k, n - 1)] + ([deep.detail(k, n), deep.smooth(k, n)] if k > 1 else [None] * 2)
        acc = [a if v is None else jnp.where(here, v, a) for a, v in zip(acc, new)]
    for t in range(3):
        up_ref[5 + t] = acc[t]
    down_ref[8], down_ref[9], down_ref[10] = cc_ref[0], cc_ref[1], cc_ref[n1 + 1]
    if far:
        here = in_span(spans[LEVELS])
        up2_ref[...] = jnp.where(here, deep.detail(LEVELS, nx >> LEVELS), 0.0)
        down2_ref[...] = jnp.where(here, deep.detail(LEVELS, -1), 0.0)


def weigh(r_ref, bands, value):
    m = r_ref.shape[1]
    vectors = value.shape[0] // m
    hi, lo = split(value)
    out = [[] for _ in bands]
    mats = [r_ref[b] for b in bands]
    mat = mats[0] if len(mats) == 1 else jnp.concatenate(mats, 0)
    for v in range(vectors):
        part = slice(v * m, (v + 1) * m)
        rhs = jnp.concatenate([hi[part], hi[part], lo[part]], 0)
        res = dot(mat, rhs)
        for j in range(len(bands)):
            out[j].append(res[j * m : (j + 1) * m])
    return [jnp.concatenate(o, 0) for o in out]


def band_of(k, kind, y_kind):
    if kind == "s":
        return 3 * LEVELS if y_kind == "s" else 3 * (k - 1)
    return 3 * (k - 1) + (1 if y_kind == "s" else 2)


def weigh_c(r_ref, spans, kind, levels, tiles):
    which = [
        (k, y_kind)
        for k in levels
        for y_kind in ("s", "d")
        if kind == "d" or y_kind == "d" or k == LEVELS
    ]
    value = jnp.concatenate(tiles, 1) if len(tiles) > 1 else tiles[0]
    res = weigh(r_ref, [band_of(k, kind, y_kind) for k, y_kind in which], value)
    outs = []
    for t in range(len(tiles)):
        out = jnp.zeros_like(tiles[t])
        for (k, y_kind), r in zip(which, res):
            out = jnp.where(in_span(spans[k, y_kind]), r[:, t * TILE : (t + 1) * TILE], out)
        outs.append(out)
    return outs


def weigh_m2(r_ref, kind, tiles):
    lane_d = lanes() >= TILE // 2
    value = jnp.concatenate(tiles, 1) if len(tiles) > 1 else tiles[0]
    if kind == "s":
        res = [None, weigh(r_ref, [band_of(2, "s", "d")], value)[0]]
    else:
        res = weigh(r_ref, [band_of(2, "d", "s"), band_of(2, "d", "d")], value)
    outs = []
    for t in range(len(tiles)):
        a, b = (0.0 if r is None else r[:, t * TILE : (t + 1) * TILE] for r in res)
        outs.append(jnp.where(lane_d, b, a))
    return outs


def weigh_tiles(r_ref, band, tiles):
    value = jnp.concatenate(tiles, 1) if len(tiles) > 1 else tiles[0]
    res = weigh(r_ref, [band], value)[0]
    return [res[:, t * TILE : (t + 1) * TILE] for t in range(len(tiles))]


def groups(low, high, size):
    return [list(range(i, min(i + size, high + 1))) for i in range(low, high + 1, size)]


def weighted_plan(nx):
    n2 = nx >> 2
    plan, at = {}, 0
    for name, count in ((("m2", "d"), n2 + 2), (("m2", "s"), n2 + 1), (("c", "d"), n2 + 2), (("c", "s"), n2 + 1)):
        plan[name] = at
        at += count
    return plan, at


def pairs_into(ref, row, g, tiles):
    rows, width = slice(row * g, (row + 1) * g), len(tiles) * TILE
    for t, tile in enumerate(tiles):
        if tile is None:
            continue
        cols = slice(t * TILE, (t + 1) * TILE)
        ref[rows, cols], ref[rows, width + t * TILE : width + (t + 1) * TILE] = split(tile)


def stack_back(s_ref, out, spans_of_rows):
    at = 0
    for a, b in spans_of_rows * 2:
        out[at : at + b - a] = s_ref[0, a:b]
        at += b - a


def first_level_rows(ny):
    half, c = ny // 2, (ny + ny // 2, ny + ny // 2 + TILE)
    return [(0, ny), c], [(half, ny), c]


def local_kernel(nx, edge_ref, var_ref, ym_ref, z, cc_ref, p_ref, s_ref, r_ref,
                 vd_ref, vs_ref, w_ref, y, p2, zd, zs, sd, ss):
    g, mains = y.shape[1], y.shape[2]
    ny = mains - TILE
    _, spans = lane_plan(ny)
    n1, n2 = nx >> 1, nx >> 2
    plan, _ = weighted_plan(nx)
    n = 2 * TILE
    p2[0:n], p2[n : 2 * n] = p_ref[:, 0:mains], p_ref[:, 0:mains]
    rows_d, rows_s = first_level_rows(ny)
    stack_back(s_ref, sd, rows_d)
    stack_back(s_ref, ss, rows_s)
    step = 4
    for r in range(0, nx, step):
        res = dot(z[r * g : (r + step) * g], p2[...])
        y[r : r + step] = ym_ref[r : r + step] + res.reshape(step, g, mains)

    def lift(columns):
        return Lift(nx, lambda i: y[i, :, columns], edge_ref)

    a, b, m2 = (lift(slice(t * TILE, (t + 1) * TILE)) for t in range(3))

    def store(name, low, some, tiles):
        for i, tile in zip(some, tiles):
            w_ref[plan[name] + i - low] = tile

    here = in_span(spans[1])

    def weighed_c(kind, low, some):
        base = 0 if kind == "d" else n1 + 1
        out = {}
        by_levels = {}
        for i in some:
            by_levels.setdefault(tuple(k for k in range(1, LEVELS + 1) if i <= nx >> k), []).append(i)
        for levels, part in by_levels.items():
            tiles = weigh_c(r_ref, spans, kind, list(levels), [cc_ref[base + i - low] for i in part])
            for i, tile in zip(part, tiles):
                if i <= n2:
                    w_ref[plan["c", kind] + i - low] = tile
                out[i] = jnp.where(here, tile, 0.0) if i <= n2 else tile
        return [out[i] for i in some]

    for some in groups(-1, n1 - 1, 4):
        ta = weigh_tiles(r_ref, band_of(1, "d", "s"), [a.detail(1, i) for i in some])
        tb = weigh_tiles(r_ref, band_of(1, "d", "d"), [b.detail(1, i) for i in some])
        tc = weighed_c("d", -1, some)
        for i, tiles in zip(some, zip(ta, tb, tc)):
            pairs_into(zd, i + 1, g, tiles)
        first, count = some[0] + 1, len(some)
        vd_ref[first : first + count] = dot(zd[first * g : (first + count) * g], sd[...]).reshape(count, g, ny)
    for some in groups(0, n1, 4):
        tb = weigh_tiles(r_ref, band_of(1, "s", "d"), [b.smooth(1, i) for i in some])
        tc = weighed_c("s", 0, some)
        for i, tiles in zip(some, zip(tb, tc)):
            pairs_into(zs, i, g, tiles)
        first, count = some[0], len(some)
        vs_ref[first : first + count] = dot(zs[first * g : (first + count) * g], ss[...]).reshape(count, g, ny)
    for some in groups(-1, n2, 4):
        store(("m2", "d"), -1, some, weigh_m2(r_ref, "d", [m2.detail(2, i) for i in some]))
    for some in groups(0, n2, 4):
        store(("m2", "s"), 0, some, weigh_m2(r_ref, "s", [m2.smooth(2, i) for i in some]))


def final_kernel(nx, far, edge_ref, var_ref, vd_ref, vs_ref, w_ref, up_ref, down_ref, *rest):
    if far:
        up2_ref, down2_ref = rest[:2]
        rest = rest[2:]
    s_ref, r_ref, out_ref, sd, ss, sdeep, zd, zs, zdeep, rows, ot, sem = rest
    g, ny = ot.shape[1], ot.shape[2]
    _, spans = lane_plan(ny)
    plan, _ = weighted_plan(nx)
    half = ny // 2
    n1, n2 = nx >> 1, nx >> 2
    rows_d, rows_s = first_level_rows(ny)
    stack_back(s_ref, sd, rows_d)
    stack_back(s_ref, ss, rows_s)
    stack_back(s_ref, sdeep, [(ny, ny + half + TILE)])
    s_lanes = smooth_lanes(spans)
    lev1 = in_span(spans[1])

    def smooth_c(value):
        return jnp.where(s_lanes, 0.25 * value, 0.0)

    c_d = {-1: up_ref[5], 0: up_ref[6], "n-1": down_ref[8], "n": down_ref[9]}
    c_s = {
        0: up_ref[7] + jnp.where(lev1, smooth_c(c_d[-1]), 0.0),
        1: smooth_c(c_d[0]),
        "n-1": smooth_c(c_d["n-1"]),
        "n": down_ref[10],
    }
    if far:
        c_d[-1] = c_d[-1] + up2_ref[...]
        c_s[0] = c_s[0] + smooth_c(up2_ref[...])
        c_d["n"] = c_d["n"] + down2_ref[...]
        c_s["n"] = c_s["n"] + smooth_c(down2_ref[...])
    every = list(range(1, LEVELS + 1))
    got = {}

    def keep(name, keys, tiles):
        for key, tile in zip(keys, tiles):
            got[name, key] = tile

    for kind, tiles in (("d", c_d), ("s", c_s)):
        keep(("c", kind), list(tiles), weigh_c(r_ref, spans, kind, every, list(tiles.values())))
    keys = [-1, "n-1", "n"]
    ta = weigh_tiles(r_ref, band_of(1, "d", "s"), [up_ref[0], down_ref[0], down_ref[2]])
    tb = weigh_tiles(r_ref, band_of(1, "d", "d"), [up_ref[1], down_ref[1], down_ref[3]])
    for j, key in enumerate(keys):
        pairs_into(zd, j, g, [ta[j], tb[j], jnp.where(lev1, got[("c", "d"), key], 0.0)])
    more_d = dot(zd[...], sd[...])
    tb = weigh_tiles(r_ref, band_of(1, "s", "d"), [0.25 * up_ref[1], 0.25 * down_ref[1], down_ref[4]])
    for j, key in enumerate([0, "n-1", "n"]):
        pairs_into(zs, j, g, [tb[j], jnp.where(lev1, got[("c", "s"), key], 0.0)])
    more_s = dot(zs[...], ss[...])
    keep(("m2", "d"), [-1, 0, "n-1", "n"], weigh_m2(r_ref, "d", [up_ref[2], up_ref[3], down_ref[5], down_ref[6]]))
    keep(("m2", "s"), [0, 1, "n-1", "n"],
         weigh_m2(r_ref, "s", [up_ref[4], 0.25 * up_ref[3], 0.25 * down_ref[5], down_ref[7]]))

    def value_of(array, kind, k, i):
        n, low = nx >> k, -1 if kind == "d" else 0
        v = w_ref[plan[array, kind] + i - low]
        for key, at in ((-1, -1), (0, 0), (1, 1), ("n-1", n - 1), ("n", n)):
            if at == i and ((array, kind), key) in got:
                v = v + got[(array, kind), key]
        return jnp.where(in_span(spans[k]), v, 0.0) if array == "c" else v

    not_last = edge_ref[1]

    def unlift(n, smooth, detail, emit):
        below, before = detail(-1), None
        for i in range(n + 1):
            here = detail(i)
            even = smooth(i) - 0.25 * (below + here)
            if i == n:
                even = even * not_last
            if i > 0:
                emit(2 * i - 1, below + 0.5 * (before + even))
            emit(2 * i, even)
            below, before = here, even

    for k in range(LEVELS, 1, -1):
        base = level_base(nx, k)

        def smooth_deep(i, k=k, base=base):
            v = value_of("c", "s", k, i)
            return v if k == LEVELS else v + rows[base + i]

        if k > 2:
            def emit(i, value, base=level_base(nx, k - 1)):
                rows[base + i] = value
        else:
            def emit(i, value):
                r = slice(i * g, (i + 1) * g)
                zdeep[r, TILE : 2 * TILE], zdeep[r, 3 * TILE : 4 * TILE] = split(value)

        unlift(nx >> k, smooth_deep, lambda i, k=k: value_of("c", "d", k, i), emit)

    def emit_m2(i, value):
        r = slice(i * g, (i + 1) * g)
        zdeep[r, 0:TILE], zdeep[r, 2 * TILE : 3 * TILE] = split(value)

    unlift(n2, lambda i: value_of("m2", "s", 2, i), lambda i: value_of("m2", "d", 2, i), emit_m2)

    extra_d = {-1: more_d[0:g], n1 - 1: more_d[g : 2 * g], n1: more_d[2 * g :]}
    extra_s = {0: more_s[0:g], n1 - 1: more_s[g : 2 * g], n1: more_s[2 * g :]}
    step = 4
    deep = {}

    def smooth_first(i):
        if i % step == 0:
            count = min(step, n1 + 1 - i)
            res = dot(zdeep[i * g : (i + count) * g], sdeep[...])
            for j in range(count):
                deep[i + j] = res[j * g : (j + 1) * g]
        v = deep[i] + vs_ref[i]
        return v + extra_s[i] if i in extra_s else v

    def detail_first(i):
        if i == n1:
            return extra_d[i]
        v = vd_ref[i + 1]
        return v + extra_d[i] if i in extra_d else v

    copies = []

    def emit_out(i, value):
        if i < nx:
            ot[i] = value
            copies.append(pltpu.make_async_copy(ot.at[i], out_ref.at[:, i], sem.at[i]))
            copies[-1].start()

    unlift(n1, smooth_first, detail_first, emit_out)
    for copy in copies:
        copy.wait()


def level_base(nx, k):
    return sum((nx >> j) + 1 for j in range(max(k + 1, 3), LEVELS)) if k > 1 else 0


def shift(value, axis, step):
    count = lax.axis_size(axis)
    pairs = [(i, i + step) for i in range(count) if 0 <= i + step < count]
    return lax.ppermute(value, axis, pairs)


def swap(value, axis, first):
    count = lax.axis_size(axis)
    starts = range(first, count - 1, 2)
    return lax.ppermute(value, axis, [p for i in starts for p in ((i, i + 1), (i + 1, i))])


def per_device(control, band_roots):
    vectors, m, nx, ny = control.shape
    g = vectors * m
    half = ny // 2
    gx, gy = lax.axis_size("gx"), lax.axis_size("gy")
    per = TILE // SLOT
    assert half == TILE and nx % (2 * per) == 0
    far = (nx >> LEVELS) < 2 and gx > 2
    consts = y_constants(ny, gy)
    main_mat, ehi_mat, elo_mat, s_mat, p_mat = (jnp.asarray(t) for t in consts)
    n1, n2 = nx >> 1, nx >> 2
    mains = ny + half

    ix, iy = lax.axis_index("gx"), lax.axis_index("gy")
    edge = jnp.stack([ix > 0, ix < gx - 1]).astype(F32)
    which = jnp.where(iy == 0, 0, jnp.where(iy == gy - 1, 2, 1)) if gy > 1 else jnp.zeros((), jnp.int32)
    which = jnp.stack([which, iy % 2, ix % 2]).astype(jnp.int32)
    r_hi = lax.reduce_precision(band_roots, 8, 7)
    r_lo = band_roots - r_hi
    roots = jnp.concatenate([r_hi.astype(BF), r_lo.astype(BF), r_hi.astype(BF)], 2)

    hbm = pl.BlockSpec(memory_space=pl.ANY)
    vmem = pl.BlockSpec(memory_space=pltpu.VMEM)

    def variant(mat):
        shape = (1,) + mat.shape[1:]
        return mat, pl.BlockSpec(shape, lambda i, e, v: (v[0], 0, 0))

    def call(kernel, ins, outs, scratches, name, out_specs=None):
        return pl.pallas_call(
            kernel,
            out_shape=tuple(jax.ShapeDtypeStruct(*s) for s in outs),
            grid_spec=pltpu.PrefetchScalarGridSpec(
                num_scalar_prefetch=2,
                grid=(1,),
                in_specs=[s for _, s in ins],
                out_specs=out_specs or (vmem,) * len(outs),
                scratch_shapes=scratches,
            ),
            name=name,
            compiler_params=pltpu.CompilerParams(vmem_limit_bytes=VMEM_LIMIT),
        )(edge, which, *[a for a, _ in ins])

    tile = (g, TILE)
    rows3 = control.reshape(g, nx, ny)
    far_hbm = pl.BlockSpec(memory_space=pltpu.HBM)
    xhl, yc, one, two = call(
        partial(first_kernel, nx),
        [(pltpu.with_memory_space_constraint(t, pltpu.HBM), far_hbm) for t in (rows3, ehi_mat, elo_mat)],
        [((nx * g, 3 * ny), BF), ((nx,) + tile, F32), ((nx // per,) + tile, F32), ((nx // per,) + tile, F32)],
        [pltpu.VMEM((nx, g, ny), F32), pltpu.VMEM((3 * ny, 2 * TILE), BF), pltpu.SemaphoreType.DMA((nx + 3,))],
        "first",
    )
    got_one = swap(one, "gy", 0)
    got_two = swap(two, "gy", 1)
    (ym,) = call(
        partial(main_kernel, nx),
        [(xhl, vmem), variant(main_mat)],
        [((nx, g, mains), F32)],
        [pltpu.VMEM((2 * ny, mains), BF)],
        "main",
    )
    slots = 2 * n1 + 2
    sent = call(
        partial(send_kernel, nx, far),
        [(yc, vmem), (ym, vmem), (got_one, vmem), (got_two, vmem), (p_mat, vmem)],
        [((8,) + tile, F32), ((11,) + tile, F32), ((slots,) + tile, F32), ((nx * g, 4 * TILE), BF)]
        + ([(tile, F32), (tile, F32)] if far else []),
        [
            pltpu.VMEM((nx,) + tile, F32),
            pltpu.VMEM((8, g, mains), F32),
            pltpu.VMEM((8, g, mains), F32),
            pltpu.VMEM((4 * TILE, mains + TILE), BF),
        ],
        "send",
    )
    got = [(shift(sent[0], "gx", 1), vmem), (shift(sent[1], "gx", -1), vmem)]
    if far:
        got += [(shift(sent[4], "gx", 2), vmem), (shift(sent[5], "gx", -2), vmem)]

    _, count = weighted_plan(nx)
    vd, vs, w = call(
        partial(local_kernel, nx),
        [(ym, vmem), (sent[3], vmem), (sent[2], vmem), (p_mat, vmem), variant(s_mat), (roots, vmem)],
        [((n1 + 1, g, ny), F32), ((n1 + 1, g, ny), F32), ((count,) + tile, F32)],
        [
            pltpu.VMEM((nx, g, mains), F32),
            pltpu.VMEM((4 * TILE, mains), BF),
            pltpu.VMEM(((n1 + 1) * g, 6 * TILE), BF),
            pltpu.VMEM(((n1 + 1) * g, 4 * TILE), BF),
            pltpu.VMEM((6 * TILE, ny), BF),
            pltpu.VMEM((4 * TILE, ny), BF),
        ],
        "local",
    )
    (out,) = call(
        partial(final_kernel, nx, far),
        [(vd, vmem), (vs, vmem), (w, vmem)] + got + [variant(s_mat), (roots, vmem)],
        [((g, nx, ny), F32)],
        [
            pltpu.VMEM((6 * TILE, ny), BF),
            pltpu.VMEM((4 * TILE, ny), BF),
            pltpu.VMEM((4 * TILE, ny), BF),
            pltpu.VMEM((3 * g, 6 * TILE), BF),
            pltpu.VMEM((3 * g, 4 * TILE), BF),
            pltpu.VMEM(((n1 + 1) * g, 4 * TILE), BF),
            pltpu.VMEM((level_base(nx, 1) + sum((nx >> j) + 1 for j in range(2, LEVELS)),) + tile, F32),
            pltpu.VMEM((nx, g, ny), F32),
            pltpu.SemaphoreType.DMA((nx,)),
        ],
        "final",
        (hbm,),
    )
    return out.reshape(control.shape)


def solution(mesh):
    in_specs = (P(None, None, "gx", "gy"), P())
    out_specs = P(None, None, "gx", "gy")
    return jax.shard_map(
        per_device, mesh=mesh, in_specs=in_specs, out_specs=out_specs, check_vma=False
    )
```

```python
from functools import lru_cache, partial

import jax
import jax.numpy as jnp
import numpy as np
from jax import lax
from jax.experimental import pallas as pl
from jax.experimental.pallas import tpu as pltpu
from jax.sharding import PartitionSpec as P

LEVELS = 5
TILE = 128
VMEM_LIMIT = 28 * 2**20
BF = jnp.bfloat16
F32 = jnp.float32


def lift_np(signal):
    even, odd = signal[0::2], signal[1::2]
    zero = np.zeros_like(even[:1])
    detail = odd - 0.5 * (even + np.concatenate([even[1:], zero]))
    return even + 0.25 * (np.concatenate([zero, detail[:-1]]) + detail), detail


def unlift_np(smooth, detail):
    zero = np.zeros_like(smooth[:1])
    even = smooth - 0.25 * (np.concatenate([zero, detail[:-1]]) + detail)
    odd = detail + 0.5 * (even + np.concatenate([even[1:], zero]))
    return np.stack([even, odd], 1).reshape(2 * even.shape[0], -1)


def lane_plan(ny):
    place, lane = {}, 0
    spans = {}
    for k in list(range(3, LEVELS + 1)) + [1, 2]:
        n = ny >> k
        first = lane
        for kind, lo in (("s", 0), ("d", -1)):
            start = lane
            for i in range(lo, n + 1):
                if k <= 2 and 0 <= i < n:
                    place[k, kind, i] = (f"m{k}", i + (n if kind == "d" else 0))
                else:
                    place[k, kind, i] = ("c", lane)
                    lane += 1
            spans[k, kind] = (start, lane)
        spans[k] = (first, lane)
    assert lane <= TILE
    return place, spans


SLOT = 16


def edge_lanes(side):
    out = []
    for k in range(1, LEVELS + 1):
        if side > 0:
            out += [(k, "d", -1)] + ([(k, "d", 0), (k, "s", 0)] if k > 1 else [])
        else:
            out += [(k, "d", -1), (k, "d", 0), (k, "s", 0)]
    assert len(out) <= SLOT
    return out


@lru_cache(None)
def y_matrices(ny, below, above):
    place, _ = lane_plan(ny)
    off = ny if below else 0
    size = off + ny + (ny if above else 0)
    width = {"m1": ny, "m2": ny // 2, "c": TILE}
    ana = {a: np.zeros((ny, w)) for a, w in width.items()}
    syn = {a: np.zeros((w, ny)) for a, w in width.items()}
    send = {side: np.zeros((ny, SLOT)) for side in (1, -1)}
    s = np.eye(size)
    for k in range(1, LEVELS + 1):
        s, d = lift_np(s)
        for kind, mat in (("s", s), ("d", d)):
            n, o, own = size >> k, off >> k, ny >> k
            for side in (1, -1):
                for lane, (level, what, i) in enumerate(edge_lanes(side)):
                    at = o + i + (own if side > 0 else 0)
                    if (level, what) == (k, kind) and 0 <= at < n:
                        send[side][:, lane] = mat[at][off : off + ny]
            for i in range(0 if kind == "s" else -1, own + 1):
                if not 0 <= o + i < n:
                    continue
                arr, lane = place[k, kind, i]
                ana[arr][:, lane] = mat[o + i][off : off + ny]
                unit = np.zeros((n, 1))
                unit[o + i] = 1.0
                zero = np.zeros_like(unit)
                back = unlift_np(unit, zero) if kind == "s" else unlift_np(zero, unit)
                for _ in range(k - 1):
                    back = unlift_np(back, np.zeros_like(back))
                syn[arr][lane] = back[off : off + ny, 0]
    return ana, syn, send


@lru_cache(None)
def y_received(ny):
    place, _ = lane_plan(ny)
    base = {"m1": 0, "m2": ny, "c": ny + ny // 2}
    mat = np.zeros((2 * SLOT, base["c"] + TILE))

    def put(row, k, kind, i, value):
        arr, lane = place[k, kind, i]
        mat[row, base[arr] + lane] += value

    for row, (k, kind, i) in enumerate(edge_lanes(1)):
        put(row, k, kind, i, 1.0)
        if kind == "d" and i == (-1 if k == 1 else 0):
            put(row, k, "s", i + 1, 0.25)
    for row, (k, kind, i) in enumerate(edge_lanes(-1)):
        n = ny >> k
        put(SLOT + row, k, kind, n + i, 1.0)
        if kind == "d" and i == -1:
            put(SLOT + row, k, "s", n - 1, 0.25)
    groups = TILE // SLOT
    return np.concatenate([np.tile(mat[:SLOT], (groups, 1)), np.tile(mat[SLOT:], (groups, 1))], 0)


def split_np(mat):
    hi = mat.astype(np.float32).astype(jnp.bfloat16)
    lo = (mat - hi.astype(np.float64)).astype(np.float32).astype(jnp.bfloat16)
    return hi, lo


@lru_cache(None)
def y_constants(ny, count):
    if count == 1:
        kinds = [(False, False)]
    else:
        kinds = [(False, True), (True, True), (True, False)]
    main, e_hi, e_lo, back = [], [], [], []
    for below, above in kinds:
        ana, syn, send = y_matrices(ny, below, above)
        hi, lo = split_np(np.concatenate([ana["m1"], ana["m2"], np.zeros((ny, TILE))], 1))
        assert not np.any(lo.astype(np.float32))
        main.append(hi)
        edge = np.tile(np.concatenate([send[1], send[-1]], 1), (1, TILE // (2 * SLOT)))
        hi, lo = split_np(np.concatenate([ana["c"], edge], 1))
        e_hi.append(hi)
        e_lo.append(lo)
        hi, lo = split_np(np.concatenate([syn["m1"], syn["m2"], syn["c"]], 0))
        assert not np.any(lo.astype(np.float32))
        back.append(hi)
    return np.stack(main), np.stack(e_hi), np.stack(e_lo), np.stack(back), split_np(y_received(ny))[0]


def split(value):
    hi = value.astype(BF)
    return hi, (value - hi.astype(F32)).astype(BF)


def dot(a, b):
    return jnp.dot(a, b, preferred_element_type=F32)


def lanes():
    return lax.broadcasted_iota(jnp.int32, (1, TILE), 1)


def in_span(span):
    lane = lanes()
    return (lane >= span[0]) & (lane < span[1])


def first_kernel(nx, edge_ref, var_ref, x_ref, ehi_ref, elo_ref, xhl, yc_ref, one_ref, two_ref, xt, e3, sems):
    g, ny = xt.shape[1], xt.shape[3]
    consts = [
        pltpu.make_async_copy(ref.at[var_ref[0]], e3.at[pl.ds(j * ny, ny)], sems.at[nx + j])
        for j, ref in enumerate((ehi_ref, ehi_ref, elo_ref))
    ]
    per = TILE // SLOT
    copies = [
        pltpu.make_async_copy(x_ref.at[:, pl.ds(r, per)], xt.at[r // per], sems.at[r // per])
        for r in range(0, nx, per)
    ]
    for copy in copies[:1] + consts + copies[1:]:
        copy.start()
    odd = var_ref[1] == 1
    for r in range(0, nx, per):
        up = down = None
        copies[r // per].wait()
        block = jnp.swapaxes(xt[r // per], 0, 1)
        for q in range(r, r + per, 4):
            for i in range(q, q + 4):
                rows = slice(i * g, (i + 1) * g)
                hi, lo = split(block[i - r])
                xhl[rows, 0:ny], xhl[rows, ny : 2 * ny], xhl[rows, 2 * ny : 3 * ny] = hi, lo, hi
            if q == 0:
                for copy in consts:
                    copy.wait()
            res = dot(xhl[q * g : (q + 4) * g], e3[...])
            for i in range(q, q + 4):
                part = res[(i - q) * g : (i - q + 1) * g]
                yc_ref[i] = part[:, 0:TILE]
                plain = part[:, TILE : 2 * TILE]
                turned = pltpu.roll(plain, SLOT, 1)
                group = lanes() // SLOT == i - r
                a, b = (plain, turned) if i % 2 == 0 else (turned, plain)
                up = jnp.where(group, a, 0.0 if up is None else up)
                down = jnp.where(group, b, 0.0 if down is None else down)
        one_ref[r // per] = jnp.where(odd, down, up)
        two_ref[r // per] = jnp.where(odd, up, down)


def main_kernel(nx, edge_ref, var_ref, xhl, a_ref, y_ref, one_ref, two_ref, a2):
    g, ny = y_ref.shape[1], a_ref.shape[1]
    a2[0:ny], a2[ny : 2 * ny] = a_ref[0], a_ref[0]
    step = 4
    for r in range(0, nx, step):
        res = dot(xhl[r * g : (r + step) * g, 0 : 2 * ny], a2[...])
        y_ref[r : r + step] = res[:, 0 : y_ref.shape[2]].reshape(step, g, y_ref.shape[2])
    lift = Lift(nx, lambda i: y_ref[i, :, 0:ny], edge_ref)
    zero = jnp.zeros((g, TILE), F32)
    top, begin, then = lift.detail(1, (nx >> 1) - 1), lift.detail(1, -1), lift.detail(1, 0)
    row = lift.smooth(1, 0)
    up = [top[:, 0:TILE], top[:, TILE:], zero, zero, zero]
    down = [begin[:, 0:TILE], begin[:, TILE:], then[:, 0:TILE], then[:, TILE:], row[:, TILE:]]
    to_pairs(var_ref[2], up, down, one_ref, two_ref)


def to_pairs(odd, up, down, one_ref, two_ref):
    for t, (a, b) in enumerate(zip(up, down)):
        one_ref[t] = jnp.where(odd == 1, b, a)
        two_ref[t] = jnp.where(odd == 1, a, b)


def from_pairs(odd, one_ref, two_ref):
    count = one_ref.shape[0]
    below = [jnp.where(odd == 1, one_ref[t], two_ref[t]) for t in range(count)]
    above = [jnp.where(odd == 1, two_ref[t], one_ref[t]) for t in range(count)]
    return below, above


class Lift:
    def __init__(self, nx, raw, edge_ref, first=0, last=None):
        self.nx, self.raw = nx, raw
        self.first, self.last = first, nx - 1 if last is None else last
        self.not_first, self.not_last = edge_ref[0], edge_ref[1]
        self.known = {}

    def smooth(self, k, i):
        if k == 0:
            if not 0 <= i < self.nx:
                return None
            assert self.first <= i <= self.last
        if (k, "s", i) not in self.known:
            self.known[k, "s", i] = self.raw(i) if k == 0 else self.new_smooth(k, i)
        return self.known[k, "s", i]

    def detail(self, k, i):
        if (k, "d", i) not in self.known:
            self.known[k, "d", i] = self.new_detail(k, i)
        return self.known[k, "d", i]

    def new_detail(self, k, i):
        if not -1 <= i <= self.nx >> k:
            return None
        even, mid, after = (self.smooth(k - 1, j) for j in (2 * i, 2 * i + 1, 2 * i + 2))
        pair = plus(even, after)
        if pair is None:
            return mid
        out = -0.5 * pair if mid is None else mid - 0.5 * pair
        return out * self.not_first if i < 0 else out

    def new_smooth(self, k, i):
        if not -1 <= i <= (self.nx >> k) + 1:
            return None
        even = self.smooth(k - 1, 2 * i)
        pair = plus(self.detail(k, i - 1), self.detail(k, i))
        if pair is None:
            return even if even is None or i < self.nx >> k else even * self.not_last
        out = 0.25 * pair if even is None else even + 0.25 * pair
        return out * self.not_last if i >= self.nx >> k else out


def plus(a, b):
    return b if a is None else a if b is None else a + b


def c_slots(lift, spans, kind, low, high, s_lanes):
    out = []
    for i in range(low, high + 1):
        tile = None
        for k in range(1, LEVELS + 1):
            if i > lift.nx >> k:
                continue
            value = lift.detail(k, i) if kind == "d" else lift.smooth(k, i)
            if value is None:
                continue
            tile = jnp.where(in_span(spans[k]), value, 0.0 if tile is None else tile)
        out.append(jnp.where(s_lanes, tile, 0.0) if kind == "s" else tile)
    return out


def smooth_lanes(spans):
    ok = in_span(spans[LEVELS])
    for k in range(1, LEVELS):
        ok = ok | in_span(spans[k, "d"])
    return ok


def send_kernel(nx, far, edge_ref, var_ref, yc_ref, ym_ref, one_ref, two_ref, p_ref, *rest):
    to_one_ref, to_two_ref, cc_ref, z, y2_ref = rest[:5]
    rest = rest[5:]
    if far:
        far_one_ref, far_two_ref = rest[:2]
        rest = rest[2:]
    yc, yl, yh, p2 = rest
    g = yc.shape[1]
    mains = ym_ref.shape[2]
    ny = mains - TILE
    half = ny // 2
    _, spans = lane_plan(ny)
    n1, n2 = nx >> 1, nx >> 2
    n = 2 * TILE
    p2[0:n], p2[n : 2 * n] = p_ref[...], p_ref[...]
    per = TILE // SLOT
    group = lanes() // SLOT
    zero = jnp.zeros((g, TILE), BF)
    odd = var_ref[1] == 1
    for t in range(nx // per):
        from_below = jnp.where(odd, one_ref[t], two_ref[t])
        from_above = jnp.where(odd, two_ref[t], one_ref[t])
        pieces = split(from_below) + split(from_above)
        for i in range(per):
            here = group == i
            rows = slice((t * per + i) * g, (t * per + i + 1) * g)
            for c, j in enumerate((0, 2, 1, 3)):
                z[rows, c * TILE : (c + 1) * TILE] = jnp.where(here, pieces[j], zero)
    step = 4
    for r in range(0, nx, step):
        res = dot(z[r * g : (r + step) * g], p2[:, ny : mains + TILE])
        y2_ref[r : r + step] = ym_ref[r : r + step, :, ny:mains] + res[:, 0:TILE].reshape(step, g, TILE)
        yc[r : r + step] = yc_ref[r : r + step] + res[:, TILE:].reshape(step, g, TILE)
    low, high = yl.shape[0], yh.shape[0]
    yl[...] = dot(z[0 : low * g], p2[:, 0:TILE]).reshape(yl.shape)
    yh[...] = dot(z[(nx - high) * g :], p2[:, 0:TILE]).reshape(yh.shape)

    def lift(ref, base):
        return Lift(nx, lambda i: ref[i - base], edge_ref, base, base + ref.shape[0] - 1)

    second = Lift(nx, lambda i: y2_ref[i], edge_ref)
    one, two = lift(yl, 0), lift(yh, nx - high)
    fix_up = [two.detail(1, n1 - 1)]
    fix_down = [one.detail(1, -1), one.detail(1, 0), one.smooth(1, 0)]
    up = [second.detail(2, n2 - 1), second.detail(2, n2), put_fixes(second.smooth(2, n2), fix_up)]
    down = [second.detail(2, -1), second.detail(2, 0), put_fixes(second.smooth(2, 0), fix_down)]

    s_lanes = smooth_lanes(spans)
    deep = Lift(nx, lambda i: yc[i], edge_ref)
    for j, tile in enumerate(c_slots(deep, spans, "d", -1, n1 - 1, s_lanes)):
        cc_ref[j] = tile
    for j, tile in enumerate(c_slots(deep, spans, "s", 0, n1, s_lanes)):
        cc_ref[n1 + 1 + j] = tile
    acc = [jnp.zeros((g, TILE), F32)] * 3
    for k in range(1, LEVELS + 1):
        n, here = nx >> k, in_span(spans[k])
        new = [deep.detail(k, n - 1)] + ([deep.detail(k, n), deep.smooth(k, n)] if k > 1 else [None] * 2)
        acc = [a if v is None else jnp.where(here, v, a) for a, v in zip(acc, new)]
    to_pairs(var_ref[2], up + acc, down + [cc_ref[0], cc_ref[1], cc_ref[n1 + 1]], to_one_ref, to_two_ref)
    if far:
        here = in_span(spans[LEVELS])
        up = jnp.where(here, deep.detail(LEVELS, nx >> LEVELS), 0.0)
        down = jnp.where(here, deep.detail(LEVELS, -1), 0.0)
        to_pairs(var_ref[3], [up], [down], far_one_ref, far_two_ref)


def put_fixes(tile, fixes):
    lane = lanes()
    for j, fix in enumerate(fixes):
        tile = jnp.where((lane >> 1) == j, pltpu.roll(fix, 1 + 2 * j, 1), tile)
    return tile


def get_fix(tile, j):
    lane = lanes()
    turned = pltpu.roll(tile, TILE - 1 - 2 * j, 1)
    a = jnp.where((lane == 0) | (lane == TILE - 1), turned, 0.0)
    return a, jnp.where(lane == TILE - 1, 4.0 * turned, 0.0)


def weigh(r_ref, bands, value):
    m = r_ref.shape[1]
    vectors = value.shape[0] // m
    hi, lo = split(value)
    out = [[] for _ in bands]
    mats = [r_ref[b] for b in bands]
    mat = mats[0] if len(mats) == 1 else jnp.concatenate(mats, 0)
    for v in range(vectors):
        part = slice(v * m, (v + 1) * m)
        rhs = jnp.concatenate([hi[part], hi[part], lo[part]], 0)
        res = dot(mat, rhs)
        for j in range(len(bands)):
            out[j].append(res[j * m : (j + 1) * m])
    return [jnp.concatenate(o, 0) for o in out]


def band_of(k, kind, y_kind):
    if kind == "s":
        return 3 * LEVELS if y_kind == "s" else 3 * (k - 1)
    return 3 * (k - 1) + (1 if y_kind == "s" else 2)


def weigh_c(r_ref, spans, kind, levels, tiles):
    which = [
        (k, y_kind)
        for k in levels
        for y_kind in ("s", "d")
        if kind == "d" or y_kind == "d" or k == LEVELS
    ]
    value = jnp.concatenate(tiles, 1) if len(tiles) > 1 else tiles[0]
    res = weigh(r_ref, [band_of(k, kind, y_kind) for k, y_kind in which], value)
    outs = []
    for t in range(len(tiles)):
        out = jnp.zeros_like(tiles[t])
        for (k, y_kind), r in zip(which, res):
            out = jnp.where(in_span(spans[k, y_kind]), r[:, t * TILE : (t + 1) * TILE], out)
        outs.append(out)
    return outs


def weigh_m2(r_ref, kind, tiles):
    lane_d = lanes() >= TILE // 2
    value = jnp.concatenate(tiles, 1) if len(tiles) > 1 else tiles[0]
    if kind == "s":
        res = [None, weigh(r_ref, [band_of(2, "s", "d")], value)[0]]
    else:
        res = weigh(r_ref, [band_of(2, "d", "s"), band_of(2, "d", "d")], value)
    outs = []
    for t in range(len(tiles)):
        a, b = (0.0 if r is None else r[:, t * TILE : (t + 1) * TILE] for r in res)
        outs.append(jnp.where(lane_d, b, a))
    return outs


def weigh_tiles(r_ref, band, tiles):
    value = jnp.concatenate(tiles, 1) if len(tiles) > 1 else tiles[0]
    res = weigh(r_ref, [band], value)[0]
    return [res[:, t * TILE : (t + 1) * TILE] for t in range(len(tiles))]


def groups(low, high, size):
    return [list(range(i, min(i + size, high + 1))) for i in range(low, high + 1, size)]


def weighted_plan(nx):
    n2 = nx >> 2
    plan, at = {}, 0
    for name, count in ((("m2", "d"), n2 + 2), (("m2", "s"), n2 + 1), (("c", "d"), n2 + 2), (("c", "s"), n2 + 1)):
        plan[name] = at
        at += count
    return plan, at


def pairs_into(ref, row, g, tiles):
    rows, width = slice(row * g, (row + 1) * g), len(tiles) * TILE
    for t, tile in enumerate(tiles):
        if tile is None:
            continue
        cols = slice(t * TILE, (t + 1) * TILE)
        ref[rows, cols], ref[rows, width + t * TILE : width + (t + 1) * TILE] = split(tile)


def stack_back(s_ref, out, spans_of_rows):
    at = 0
    for a, b in spans_of_rows * 2:
        out[at : at + b - a] = s_ref[0, a:b]
        at += b - a


def first_level_rows(ny):
    half, c = ny // 2, (ny + ny // 2, ny + ny // 2 + TILE)
    return [(0, ny), c], [(half, ny), c]


def local_kernel(nx, edge_ref, var_ref, ym_ref, z, y2_ref, cc_ref, p_ref, s_ref, r_ref,
                 vd_ref, vs_ref, w_ref, y, p2, zd, zs, sd, ss):
    g, ny = y.shape[1], y.shape[2]
    _, spans = lane_plan(ny)
    n1, n2 = nx >> 1, nx >> 2
    plan, _ = weighted_plan(nx)
    n = 2 * TILE
    p2[0:n], p2[n : 2 * n] = p_ref[:, 0:ny], p_ref[:, 0:ny]
    rows_d, rows_s = first_level_rows(ny)
    stack_back(s_ref, sd, rows_d)
    stack_back(s_ref, ss, rows_s)
    step = 4
    for r in range(0, nx, step):
        res = dot(z[r * g : (r + step) * g], p2[...])
        y[r : r + step] = ym_ref[r : r + step, :, 0:ny] + res.reshape(step, g, ny)

    def lift(columns):
        return Lift(nx, lambda i: y[i, :, columns], edge_ref)

    a, b = (lift(slice(t * TILE, (t + 1) * TILE)) for t in range(2))
    m2 = Lift(nx, lambda i: y2_ref[i], edge_ref)

    def store(name, low, some, tiles):
        for i, tile in zip(some, tiles):
            w_ref[plan[name] + i - low] = tile

    here = in_span(spans[1])

    def weighed_c(kind, low, some):
        base = 0 if kind == "d" else n1 + 1
        out = {}
        by_levels = {}
        for i in some:
            by_levels.setdefault(tuple(k for k in range(1, LEVELS + 1) if i <= nx >> k), []).append(i)
        for levels, part in by_levels.items():
            tiles = weigh_c(r_ref, spans, kind, list(levels), [cc_ref[base + i - low] for i in part])
            for i, tile in zip(part, tiles):
                if i <= n2:
                    w_ref[plan["c", kind] + i - low] = tile
                out[i] = jnp.where(here, tile, 0.0) if i <= n2 else tile
        return [out[i] for i in some]

    for some in groups(-1, n1 - 1, 4):
        ta = weigh_tiles(r_ref, band_of(1, "d", "s"), [a.detail(1, i) for i in some])
        tb = weigh_tiles(r_ref, band_of(1, "d", "d"), [b.detail(1, i) for i in some])
        tc = weighed_c("d", -1, some)
        for i, tiles in zip(some, zip(ta, tb, tc)):
            pairs_into(zd, i + 1, g, tiles)
        first, count = some[0] + 1, len(some)
        vd_ref[first : first + count] = dot(zd[first * g : (first + count) * g], sd[...]).reshape(count, g, ny)
    for some in groups(0, n1, 4):
        tb = weigh_tiles(r_ref, band_of(1, "s", "d"), [b.smooth(1, i) for i in some])
        tc = weighed_c("s", 0, some)
        for i, tiles in zip(some, zip(tb, tc)):
            pairs_into(zs, i, g, tiles)
        first, count = some[0], len(some)
        vs_ref[first : first + count] = dot(zs[first * g : (first + count) * g], ss[...]).reshape(count, g, ny)
    for some in groups(-1, n2, 4):
        store(("m2", "d"), -1, some, weigh_m2(r_ref, "d", [m2.detail(2, i) for i in some]))
    for some in groups(0, n2, 4):
        store(("m2", "s"), 0, some, weigh_m2(r_ref, "s", [m2.smooth(2, i) for i in some]))


def final_kernel(nx, far, edge_ref, var_ref, vd_ref, vs_ref, w_ref, e_one, e_two, r_one, r_two, *rest):
    if far:
        f_one, f_two = rest[:2]
        rest = rest[2:]
    s_ref, r_ref, out_ref, sd, ss, sdeep, zd, zs, zdeep, rows, ot, sem = rest
    g, ny = ot.shape[1], ot.shape[3]
    _, spans = lane_plan(ny)
    plan, _ = weighted_plan(nx)
    half = ny // 2
    n1, n2 = nx >> 1, nx >> 2
    rows_d, rows_s = first_level_rows(ny)
    stack_back(s_ref, sd, rows_d)
    stack_back(s_ref, ss, rows_s)
    stack_back(s_ref, sdeep, [(ny, ny + half + TILE)])
    s_lanes = smooth_lanes(spans)
    lev1 = in_span(spans[1])

    def smooth_c(value):
        return jnp.where(s_lanes, 0.25 * value, 0.0)

    below, above = from_pairs(var_ref[2], r_one, r_two)
    first_below, first_above = from_pairs(var_ref[2], e_one, e_two)
    c_d = {-1: below[3], 0: below[4], "n-1": above[3], "n": above[4]}
    c_s = {
        0: below[5] + jnp.where(lev1, smooth_c(c_d[-1]), 0.0),
        1: smooth_c(c_d[0]),
        "n-1": smooth_c(c_d["n-1"]),
        "n": above[5],
    }
    if far:
        (far_below,), (far_above,) = from_pairs(var_ref[3], f_one, f_two)
        c_d[-1] = c_d[-1] + far_below
        c_s[0] = c_s[0] + smooth_c(far_below)
        c_d["n"] = c_d["n"] + far_above
        c_s["n"] = c_s["n"] + smooth_c(far_above)
    fixes = [get_fix(below[2], 0)] + [get_fix(above[2], j) for j in range(3)]
    a_tiles = [first_below[0] + fixes[0][0], first_above[0] + fixes[1][0], first_above[2] + fixes[2][0]]
    b_tiles = [first_below[1] + fixes[0][1], first_above[1] + fixes[1][1], first_above[3] + fixes[2][1]]
    s_tiles = [0.25 * b_tiles[0], 0.25 * b_tiles[1], first_above[4] + fixes[3][1]]
    every = list(range(1, LEVELS + 1))
    got = {}

    def keep(name, keys, tiles):
        for key, tile in zip(keys, tiles):
            got[name, key] = tile

    for kind, tiles in (("d", c_d), ("s", c_s)):
        keep(("c", kind), list(tiles), weigh_c(r_ref, spans, kind, every, list(tiles.values())))
    keys = [-1, "n-1", "n"]
    ta = weigh_tiles(r_ref, band_of(1, "d", "s"), a_tiles)
    tb = weigh_tiles(r_ref, band_of(1, "d", "d"), b_tiles)
    for j, key in enumerate(keys):
        pairs_into(zd, j, g, [ta[j], tb[j], jnp.where(lev1, got[("c", "d"), key], 0.0)])
    more_d = dot(zd[...], sd[...])
    tb = weigh_tiles(r_ref, band_of(1, "s", "d"), s_tiles)
    for j, key in enumerate([0, "n-1", "n"]):
        pairs_into(zs, j, g, [tb[j], jnp.where(lev1, got[("c", "s"), key], 0.0)])
    more_s = dot(zs[...], ss[...])
    keep(("m2", "d"), [-1, 0, "n-1", "n"], weigh_m2(r_ref, "d", [below[0], below[1], above[0], above[1]]))
    keep(("m2", "s"), [0, 1, "n-1", "n"],
         weigh_m2(r_ref, "s", [below[2], 0.25 * below[1], 0.25 * above[0], above[2]]))

    def value_of(array, kind, k, i):
        n, low = nx >> k, -1 if kind == "d" else 0
        v = w_ref[plan[array, kind] + i - low]
        for key, at in ((-1, -1), (0, 0), (1, 1), ("n-1", n - 1), ("n", n)):
            if at == i and ((array, kind), key) in got:
                v = v + got[(array, kind), key]
        return jnp.where(in_span(spans[k]), v, 0.0) if array == "c" else v

    not_last = edge_ref[1]

    def unlift(n, smooth, detail, emit):
        below, before = detail(-1), None
        for i in range(n + 1):
            here = detail(i)
            even = smooth(i) - 0.25 * (below + here)
            if i == n:
                even = even * not_last
            if i > 0:
                emit(2 * i - 1, below + 0.5 * (before + even))
            emit(2 * i, even)
            below, before = here, even

    for k in range(LEVELS, 1, -1):
        base = level_base(nx, k)

        def smooth_deep(i, k=k, base=base):
            v = value_of("c", "s", k, i)
            return v if k == LEVELS else v + rows[base + i]

        if k > 2:
            def emit(i, value, base=level_base(nx, k - 1)):
                rows[base + i] = value
        else:
            def emit(i, value):
                r = slice(i * g, (i + 1) * g)
                zdeep[r, TILE : 2 * TILE], zdeep[r, 3 * TILE : 4 * TILE] = split(value)

        unlift(nx >> k, smooth_deep, lambda i, k=k: value_of("c", "d", k, i), emit)

    def emit_m2(i, value):
        r = slice(i * g, (i + 1) * g)
        zdeep[r, 0:TILE], zdeep[r, 2 * TILE : 3 * TILE] = split(value)

    unlift(n2, lambda i: value_of("m2", "s", 2, i), lambda i: value_of("m2", "d", 2, i), emit_m2)

    extra_d = {-1: more_d[0:g], n1 - 1: more_d[g : 2 * g], n1: more_d[2 * g :]}
    extra_s = {0: more_s[0:g], n1 - 1: more_s[g : 2 * g], n1: more_s[2 * g :]}
    step = 4
    deep = {}

    def smooth_first(i):
        if i % step == 0:
            count = min(step, n1 + 1 - i)
            res = dot(zdeep[i * g : (i + count) * g], sdeep[...])
            for j in range(count):
                deep[i + j] = res[j * g : (j + 1) * g]
        v = deep[i] + vs_ref[i]
        return v + extra_s[i] if i in extra_s else v

    def detail_first(i):
        if i == n1:
            return extra_d[i]
        v = vd_ref[i + 1]
        return v + extra_d[i] if i in extra_d else v

    copies = []

    pending = {}

    def emit_out(i, value):
        if i >= nx:
            return
        pending[i] = value
        r = i - i % 8
        if all(j in pending for j in range(r, r + 8)):
            block = jnp.stack([pending.pop(j) for j in range(r, r + 8)], 0)
            ot[r // 8] = jnp.swapaxes(block, 0, 1)
            copies.append(pltpu.make_async_copy(ot.at[r // 8], out_ref.at[:, pl.ds(r, 8)], sem.at[r // 8]))
            copies[-1].start()

    unlift(n1, smooth_first, detail_first, emit_out)
    for copy in copies:
        copy.wait()


def level_base(nx, k):
    return sum((nx >> j) + 1 for j in range(max(k + 1, 3), LEVELS)) if k > 1 else 0


def swap(value, axis, first, step=1):
    count = lax.axis_size(axis)
    starts = [i for i in range(first, count - step) if (i - first) // step % 2 == 0]
    return lax.ppermute(value, axis, [p for i in starts for p in ((i, i + step), (i + step, i))])


def per_device(control, band_roots):
    vectors, m, nx, ny = control.shape
    g = vectors * m
    half = ny // 2
    gx, gy = lax.axis_size("gx"), lax.axis_size("gy")
    per = TILE // SLOT
    assert half == TILE and nx % (2 * per) == 0
    far = (nx >> LEVELS) < 2 and gx > 2
    consts = y_constants(ny, gy)
    main_mat, ehi_mat, elo_mat, s_mat, p_mat = (jnp.asarray(t) for t in consts)
    n1, n2 = nx >> 1, nx >> 2
    mains = ny + half

    ix, iy = lax.axis_index("gx"), lax.axis_index("gy")
    edge = jnp.stack([ix > 0, ix < gx - 1]).astype(F32)
    which = jnp.where(iy == 0, 0, jnp.where(iy == gy - 1, 2, 1)) if gy > 1 else jnp.zeros((), jnp.int32)
    which = jnp.stack([which, iy % 2, ix % 2, ix // 2 % 2]).astype(jnp.int32)
    r_hi = lax.reduce_precision(band_roots, 8, 7)
    r_lo = band_roots - r_hi
    roots = jnp.concatenate([r_hi.astype(BF), r_lo.astype(BF), r_hi.astype(BF)], 2)

    hbm = pl.BlockSpec(memory_space=pl.ANY)
    vmem = pl.BlockSpec(memory_space=pltpu.VMEM)

    def variant(mat):
        shape = (1,) + mat.shape[1:]
        return mat, pl.BlockSpec(shape, lambda i, e, v: (v[0], 0, 0))

    def call(kernel, ins, outs, scratches, name, out_specs=None):
        return pl.pallas_call(
            kernel,
            out_shape=tuple(jax.ShapeDtypeStruct(*s) for s in outs),
            grid_spec=pltpu.PrefetchScalarGridSpec(
                num_scalar_prefetch=2,
                grid=(1,),
                in_specs=[s for _, s in ins],
                out_specs=out_specs or (vmem,) * len(outs),
                scratch_shapes=scratches,
            ),
            name=name,
            compiler_params=pltpu.CompilerParams(vmem_limit_bytes=VMEM_LIMIT),
        )(edge, which, *[a for a, _ in ins])

    tile = (g, TILE)
    rows3 = control.reshape(g, nx, ny)
    far_hbm = pl.BlockSpec(memory_space=pltpu.HBM)
    xhl, yc, one, two = call(
        partial(first_kernel, nx),
        [(pltpu.with_memory_space_constraint(t, pltpu.HBM), far_hbm) for t in (rows3, ehi_mat, elo_mat)],
        [((nx * g, 3 * ny), BF), ((nx,) + tile, F32), ((nx // per,) + tile, F32), ((nx // per,) + tile, F32)],
        [pltpu.VMEM((nx // per, g, per, ny), F32), pltpu.VMEM((3 * ny, 2 * TILE), BF), pltpu.SemaphoreType.DMA((nx + 3,))],
        "first",
    )
    got_one = swap(one, "gy", 0)
    got_two = swap(two, "gy", 1)
    ym, one, two = call(
        partial(main_kernel, nx),
        [(xhl, vmem), variant(main_mat)],
        [((nx, g, mains), F32), ((5,) + tile, F32), ((5,) + tile, F32)],
        [pltpu.VMEM((2 * ny, mains + TILE), BF)],
        "main",
    )
    got = [(swap(one, "gx", 0), vmem), (swap(two, "gx", 1), vmem)]
    slots = 2 * n1 + 2
    sent = call(
        partial(send_kernel, nx, far),
        [(yc, vmem), (ym, vmem), (got_one, vmem), (got_two, vmem), (p_mat, vmem)],
        [((6,) + tile, F32), ((6,) + tile, F32), ((slots,) + tile, F32), ((nx * g, 4 * TILE), BF), ((nx,) + tile, F32)]
        + ([((1,) + tile, F32)] * 2 if far else []),
        [
            pltpu.VMEM((nx,) + tile, F32),
            pltpu.VMEM((4,) + tile, F32),
            pltpu.VMEM((4,) + tile, F32),
            pltpu.VMEM((4 * TILE, mains + TILE), BF),
        ],
        "send",
    )
    got += [(swap(sent[0], "gx", 0), vmem), (swap(sent[1], "gx", 1), vmem)]
    if far:
        got += [(swap(sent[5], "gx", 0, 2), vmem), (swap(sent[6], "gx", 2, 2), vmem)]

    _, count = weighted_plan(nx)
    vd, vs, w = call(
        partial(local_kernel, nx),
        [(ym, vmem), (sent[3], vmem), (sent[4], vmem), (sent[2], vmem), (p_mat, vmem), variant(s_mat), (roots, vmem)],
        [((n1 + 1, g, ny), F32), ((n1 + 1, g, ny), F32), ((count,) + tile, F32)],
        [
            pltpu.VMEM((nx, g, ny), F32),
            pltpu.VMEM((4 * TILE, ny), BF),
            pltpu.VMEM(((n1 + 1) * g, 6 * TILE), BF),
            pltpu.VMEM(((n1 + 1) * g, 4 * TILE), BF),
            pltpu.VMEM((6 * TILE, ny), BF),
            pltpu.VMEM((4 * TILE, ny), BF),
        ],
        "local",
    )
    (out,) = call(
        partial(final_kernel, nx, far),
        [(vd, vmem), (vs, vmem), (w, vmem)] + got + [variant(s_mat), (roots, vmem)],
        [((g, nx, ny), F32)],
        [
            pltpu.VMEM((6 * TILE, ny), BF),
            pltpu.VMEM((4 * TILE, ny), BF),
            pltpu.VMEM((4 * TILE, ny), BF),
            pltpu.VMEM((3 * g, 6 * TILE), BF),
            pltpu.VMEM((3 * g, 4 * TILE), BF),
            pltpu.VMEM(((n1 + 1) * g, 4 * TILE), BF),
            pltpu.VMEM((level_base(nx, 1) + sum((nx >> j) + 1 for j in range(2, LEVELS)),) + tile, F32),
            pltpu.VMEM((nx // 8, g, 8, ny), F32),
            pltpu.SemaphoreType.DMA((nx // 8,)),
        ],
        "final",
        (hbm,),
    )
    return out.reshape(control.shape)


def solution(mesh):
    in_specs = (P(None, None, "gx", "gy"), P())
    out_specs = P(None, None, "gx", "gy")
    return jax.shard_map(
        per_device, mesh=mesh, in_specs=in_specs, out_specs=out_specs, check_vma=False
    )
```

```python
from functools import lru_cache, partial

import jax
import jax.numpy as jnp
import numpy as np
from jax import lax
from jax.experimental import pallas as pl
from jax.experimental.pallas import tpu as pltpu
from jax.sharding import PartitionSpec as P

LEVELS = 5
TILE = 128
VMEM_LIMIT = 28 * 2**20
BF = jnp.bfloat16
F32 = jnp.float32


def lift_np(signal):
    even, odd = signal[0::2], signal[1::2]
    zero = np.zeros_like(even[:1])
    detail = odd - 0.5 * (even + np.concatenate([even[1:], zero]))
    return even + 0.25 * (np.concatenate([zero, detail[:-1]]) + detail), detail


def unlift_np(smooth, detail):
    zero = np.zeros_like(smooth[:1])
    even = smooth - 0.25 * (np.concatenate([zero, detail[:-1]]) + detail)
    odd = detail + 0.5 * (even + np.concatenate([even[1:], zero]))
    return np.stack([even, odd], 1).reshape(2 * even.shape[0], -1)


def lane_plan(ny):
    place, lane = {}, 0
    spans = {}
    for k in list(range(3, LEVELS + 1)) + [1, 2]:
        n = ny >> k
        first = lane
        for kind, lo in (("s", 0), ("d", -1)):
            start = lane
            for i in range(lo, n + 1):
                if k <= 2 and 0 <= i < n:
                    place[k, kind, i] = (f"m{k}", i + (n if kind == "d" else 0))
                else:
                    place[k, kind, i] = ("c", lane)
                    lane += 1
            spans[k, kind] = (start, lane)
        spans[k] = (first, lane)
    assert lane <= TILE
    return place, spans


SLOT = 16


def edge_lanes(side):
    out = []
    for k in range(1, LEVELS + 1):
        if side > 0:
            out += [(k, "d", -1)] + ([(k, "d", 0), (k, "s", 0)] if k > 1 else [])
        else:
            out += [(k, "d", -1), (k, "d", 0), (k, "s", 0)]
    assert len(out) <= SLOT
    return out


@lru_cache(None)
def y_matrices(ny, below, above):
    place, _ = lane_plan(ny)
    off = ny if below else 0
    size = off + ny + (ny if above else 0)
    width = {"m1": ny, "m2": ny // 2, "c": TILE}
    ana = {a: np.zeros((ny, w)) for a, w in width.items()}
    syn = {a: np.zeros((w, ny)) for a, w in width.items()}
    send = {side: np.zeros((ny, SLOT)) for side in (1, -1)}
    s = np.eye(size)
    for k in range(1, LEVELS + 1):
        s, d = lift_np(s)
        for kind, mat in (("s", s), ("d", d)):
            n, o, own = size >> k, off >> k, ny >> k
            for side in (1, -1):
                for lane, (level, what, i) in enumerate(edge_lanes(side)):
                    at = o + i + (own if side > 0 else 0)
                    if (level, what) == (k, kind) and 0 <= at < n:
                        send[side][:, lane] = mat[at][off : off + ny]
            for i in range(0 if kind == "s" else -1, own + 1):
                if not 0 <= o + i < n:
                    continue
                arr, lane = place[k, kind, i]
                ana[arr][:, lane] = mat[o + i][off : off + ny]
                unit = np.zeros((n, 1))
                unit[o + i] = 1.0
                zero = np.zeros_like(unit)
                back = unlift_np(unit, zero) if kind == "s" else unlift_np(zero, unit)
                for _ in range(k - 1):
                    back = unlift_np(back, np.zeros_like(back))
                syn[arr][lane] = back[off : off + ny, 0]
    return ana, syn, send


@lru_cache(None)
def y_received(ny):
    place, _ = lane_plan(ny)
    base = {"m1": 0, "m2": ny, "c": ny + ny // 2}
    mat = np.zeros((2 * SLOT, base["c"] + TILE))

    def put(row, k, kind, i, value):
        arr, lane = place[k, kind, i]
        mat[row, base[arr] + lane] += value

    for row, (k, kind, i) in enumerate(edge_lanes(1)):
        put(row, k, kind, i, 1.0)
        if kind == "d" and i == (-1 if k == 1 else 0):
            put(row, k, "s", i + 1, 0.25)
    for row, (k, kind, i) in enumerate(edge_lanes(-1)):
        n = ny >> k
        put(SLOT + row, k, kind, n + i, 1.0)
        if kind == "d" and i == -1:
            put(SLOT + row, k, "s", n - 1, 0.25)
    groups = TILE // SLOT
    return np.concatenate([np.tile(mat[:SLOT], (groups, 1)), np.tile(mat[SLOT:], (groups, 1))], 0)


def split_np(mat):
    hi = mat.astype(np.float32).astype(jnp.bfloat16)
    lo = (mat - hi.astype(np.float64)).astype(np.float32).astype(jnp.bfloat16)
    return hi, lo


@lru_cache(None)
def y_constants(ny, count):
    if count == 1:
        kinds = [(False, False)]
    else:
        kinds = [(False, True), (True, True), (True, False)]
    main, e_hi, e_lo, back = [], [], [], []
    for below, above in kinds:
        ana, syn, send = y_matrices(ny, below, above)
        hi, lo = split_np(np.concatenate([ana["m1"], ana["m2"], np.zeros((ny, TILE))], 1))
        assert not np.any(lo.astype(np.float32))
        main.append(hi)
        edge = np.tile(np.concatenate([send[1], send[-1]], 1), (1, TILE // (2 * SLOT)))
        hi, lo = split_np(np.concatenate([ana["c"], edge], 1))
        e_hi.append(hi)
        e_lo.append(lo)
        hi, lo = split_np(np.concatenate([syn["m1"], syn["m2"], syn["c"]], 0))
        assert not np.any(lo.astype(np.float32))
        back.append(hi)
    return np.stack(main), np.stack(e_hi), np.stack(e_lo), np.stack(back), split_np(y_received(ny))[0]


def split(value):
    hi = value.astype(BF)
    return hi, (value - hi.astype(F32)).astype(BF)


def dot(a, b):
    return jnp.dot(a, b, preferred_element_type=F32)


def lanes():
    return lax.broadcasted_iota(jnp.int32, (1, TILE), 1)


def in_span(span):
    lane = lanes()
    return (lane >= span[0]) & (lane < span[1])


def device_place(gx, gy):
    ix, iy = lax.axis_index("gx"), lax.axis_index("gy")
    edge = jnp.where(ix > 0, 1.0, 0.0), jnp.where(ix < gx - 1, 1.0, 0.0)
    kind = jnp.where(iy == 0, 0, jnp.where(iy == gy - 1, 2, 1)) if gy > 1 else 0
    return edge, (kind, lax.rem(iy, 2), lax.rem(ix, 2), lax.rem(ix // 2, 2))


def first_kernel(nx, edge_ref, var_ref, x_ref, ehi_ref, elo_ref, xhl, yc_ref, one_ref, two_ref, xt, e3, sems):
    g, ny = xt.shape[1], xt.shape[3]
    consts = [
        pltpu.make_async_copy(ref.at[var_ref[0]], e3.at[pl.ds(j * ny, ny)], sems.at[nx + j])
        for j, ref in enumerate((ehi_ref, ehi_ref, elo_ref))
    ]
    per = TILE // SLOT
    copies = [
        pltpu.make_async_copy(x_ref.at[:, pl.ds(r, per)], xt.at[r // per], sems.at[r // per])
        for r in range(0, nx, per)
    ]
    for copy in copies[:1] + consts + copies[1:]:
        copy.start()
    odd = var_ref[1] == 1
    for r in range(0, nx, per):
        up = down = None
        copies[r // per].wait()
        block = jnp.swapaxes(xt[r // per], 0, 1)
        for q in range(r, r + per, 4):
            for i in range(q, q + 4):
                rows = slice(i * g, (i + 1) * g)
                hi, lo = split(block[i - r])
                xhl[rows, 0:ny], xhl[rows, ny : 2 * ny], xhl[rows, 2 * ny : 3 * ny] = hi, lo, hi
            if q == 0:
                for copy in consts:
                    copy.wait()
            res = dot(xhl[q * g : (q + 4) * g], e3[...])
            for i in range(q, q + 4):
                part = res[(i - q) * g : (i - q + 1) * g]
                yc_ref[i] = part[:, 0:TILE]
                plain = part[:, TILE : 2 * TILE]
                turned = pltpu.roll(plain, SLOT, 1)
                group = lanes() // SLOT == i - r
                a, b = (plain, turned) if i % 2 == 0 else (turned, plain)
                up = jnp.where(group, a, 0.0 if up is None else up)
                down = jnp.where(group, b, 0.0 if down is None else down)
        one_ref[r // per] = jnp.where(odd, down, up)
        two_ref[r // per] = jnp.where(odd, up, down)


def main_kernel(nx, edge_ref, var_ref, xhl, a_ref, y_ref, one_ref, two_ref, a2):
    g, ny = y_ref.shape[1], a_ref.shape[1]
    a2[0:ny], a2[ny : 2 * ny] = a_ref[var_ref[0]], a_ref[var_ref[0]]
    step = 4
    for r in range(0, nx, step):
        res = dot(xhl[r * g : (r + step) * g, 0 : 2 * ny], a2[...])
        y_ref[r : r + step] = res[:, 0 : y_ref.shape[2]].reshape(step, g, y_ref.shape[2])
    lift = Lift(nx, lambda i: y_ref[i, :, 0:ny], edge_ref)
    zero = jnp.zeros((g, TILE), F32)
    top, begin, then = lift.detail(1, (nx >> 1) - 1), lift.detail(1, -1), lift.detail(1, 0)
    row = lift.smooth(1, 0)
    up = [top[:, 0:TILE], top[:, TILE:], zero, zero, zero]
    down = [begin[:, 0:TILE], begin[:, TILE:], then[:, 0:TILE], then[:, TILE:], row[:, TILE:]]
    to_pairs(var_ref[2], up, down, one_ref, two_ref)


def to_pairs(odd, up, down, one_ref, two_ref):
    for t, (a, b) in enumerate(zip(up, down)):
        one_ref[t] = jnp.where(odd == 1, b, a)
        two_ref[t] = jnp.where(odd == 1, a, b)


def from_pairs(odd, one_ref, two_ref):
    count = one_ref.shape[0]
    below = [jnp.where(odd == 1, one_ref[t], two_ref[t]) for t in range(count)]
    above = [jnp.where(odd == 1, two_ref[t], one_ref[t]) for t in range(count)]
    return below, above


class Lift:
    def __init__(self, nx, raw, edge_ref, first=0, last=None):
        self.nx, self.raw = nx, raw
        self.first, self.last = first, nx - 1 if last is None else last
        self.not_first, self.not_last = edge_ref[0], edge_ref[1]
        self.known = {}

    def smooth(self, k, i):
        if k == 0:
            if not 0 <= i < self.nx:
                return None
            assert self.first <= i <= self.last
        if (k, "s", i) not in self.known:
            self.known[k, "s", i] = self.raw(i) if k == 0 else self.new_smooth(k, i)
        return self.known[k, "s", i]

    def detail(self, k, i):
        if (k, "d", i) not in self.known:
            self.known[k, "d", i] = self.new_detail(k, i)
        return self.known[k, "d", i]

    def new_detail(self, k, i):
        if not -1 <= i <= self.nx >> k:
            return None
        even, mid, after = (self.smooth(k - 1, j) for j in (2 * i, 2 * i + 1, 2 * i + 2))
        pair = plus(even, after)
        if pair is None:
            return mid
        out = -0.5 * pair if mid is None else mid - 0.5 * pair
        return out * self.not_first if i < 0 else out

    def new_smooth(self, k, i):
        if not -1 <= i <= (self.nx >> k) + 1:
            return None
        even = self.smooth(k - 1, 2 * i)
        pair = plus(self.detail(k, i - 1), self.detail(k, i))
        if pair is None:
            return even if even is None or i < self.nx >> k else even * self.not_last
        out = 0.25 * pair if even is None else even + 0.25 * pair
        return out * self.not_last if i >= self.nx >> k else out


def plus(a, b):
    return b if a is None else a if b is None else a + b


def c_slots(lift, spans, kind, low, high, s_lanes):
    out = []
    for i in range(low, high + 1):
        tile = None
        for k in range(1, LEVELS + 1):
            if i > lift.nx >> k:
                continue
            value = lift.detail(k, i) if kind == "d" else lift.smooth(k, i)
            if value is None:
                continue
            tile = jnp.where(in_span(spans[k]), value, 0.0 if tile is None else tile)
        out.append(jnp.where(s_lanes, tile, 0.0) if kind == "s" else tile)
    return out


def smooth_lanes(spans):
    ok = in_span(spans[LEVELS])
    for k in range(1, LEVELS):
        ok = ok | in_span(spans[k, "d"])
    return ok


def send_kernel(nx, far, edge_ref, var_ref, yc_ref, ym_ref, one_ref, two_ref, p_ref, *rest):
    to_one_ref, to_two_ref, cc_ref, z, y2_ref = rest[:5]
    rest = rest[5:]
    if far:
        far_one_ref, far_two_ref = rest[:2]
        rest = rest[2:]
    yc, yl, yh, p2 = rest
    g = yc.shape[1]
    mains = ym_ref.shape[2]
    ny = mains - TILE
    half = ny // 2
    _, spans = lane_plan(ny)
    n1, n2 = nx >> 1, nx >> 2
    n = 2 * TILE
    p2[0:n], p2[n : 2 * n] = p_ref[...], p_ref[...]
    per = TILE // SLOT
    group = lanes() // SLOT
    zero = jnp.zeros((g, TILE), BF)
    odd = var_ref[1] == 1
    for t in range(nx // per):
        from_below = jnp.where(odd, one_ref[t], two_ref[t])
        from_above = jnp.where(odd, two_ref[t], one_ref[t])
        pieces = split(from_below) + split(from_above)
        for i in range(per):
            here = group == i
            rows = slice((t * per + i) * g, (t * per + i + 1) * g)
            for c, j in enumerate((0, 2, 1, 3)):
                z[rows, c * TILE : (c + 1) * TILE] = jnp.where(here, pieces[j], zero)
    step = 4
    for r in range(0, nx, step):
        res = dot(z[r * g : (r + step) * g], p2[:, ny : mains + TILE])
        y2_ref[r : r + step] = ym_ref[r : r + step, :, ny:mains] + res[:, 0:TILE].reshape(step, g, TILE)
        yc[r : r + step] = yc_ref[r : r + step] + res[:, TILE:].reshape(step, g, TILE)
    low, high = yl.shape[0], yh.shape[0]
    yl[...] = dot(z[0 : low * g], p2[:, 0:TILE]).reshape(yl.shape)
    yh[...] = dot(z[(nx - high) * g :], p2[:, 0:TILE]).reshape(yh.shape)

    def lift(ref, base):
        return Lift(nx, lambda i: ref[i - base], edge_ref, base, base + ref.shape[0] - 1)

    second = Lift(nx, lambda i: y2_ref[i], edge_ref)
    one, two = lift(yl, 0), lift(yh, nx - high)
    fix_up = [two.detail(1, n1 - 1)]
    fix_down = [one.detail(1, -1), one.detail(1, 0), one.smooth(1, 0)]
    up = [second.detail(2, n2 - 1), second.detail(2, n2), put_fixes(second.smooth(2, n2), fix_up)]
    down = [second.detail(2, -1), second.detail(2, 0), put_fixes(second.smooth(2, 0), fix_down)]

    s_lanes = smooth_lanes(spans)
    deep = Lift(nx, lambda i: yc[i], edge_ref)
    for j, tile in enumerate(c_slots(deep, spans, "d", -1, n1 - 1, s_lanes)):
        cc_ref[j] = tile
    for j, tile in enumerate(c_slots(deep, spans, "s", 0, n1, s_lanes)):
        cc_ref[n1 + 1 + j] = tile
    acc = [jnp.zeros((g, TILE), F32)] * 3
    for k in range(1, LEVELS + 1):
        n, here = nx >> k, in_span(spans[k])
        new = [deep.detail(k, n - 1)] + ([deep.detail(k, n), deep.smooth(k, n)] if k > 1 else [None] * 2)
        acc = [a if v is None else jnp.where(here, v, a) for a, v in zip(acc, new)]
    to_pairs(var_ref[2], up + acc, down + [cc_ref[0], cc_ref[1], cc_ref[n1 + 1]], to_one_ref, to_two_ref)
    if far:
        here = in_span(spans[LEVELS])
        up = jnp.where(here, deep.detail(LEVELS, nx >> LEVELS), 0.0)
        down = jnp.where(here, deep.detail(LEVELS, -1), 0.0)
        to_pairs(var_ref[3], [up], [down], far_one_ref, far_two_ref)


def put_fixes(tile, fixes):
    lane = lanes()
    for j, fix in enumerate(fixes):
        tile = jnp.where((lane >> 1) == j, pltpu.roll(fix, 1 + 2 * j, 1), tile)
    return tile


def get_fix(tile, j):
    lane = lanes()
    turned = pltpu.roll(tile, TILE - 1 - 2 * j, 1)
    a = jnp.where((lane == 0) | (lane == TILE - 1), turned, 0.0)
    return a, jnp.where(lane == TILE - 1, 4.0 * turned, 0.0)


def weigh(r_ref, bands, value):
    m = r_ref.shape[1]
    vectors = value.shape[0] // m
    hi, lo = split(value)
    out = [[] for _ in bands]
    mats = [r_ref[b] for b in bands]
    mat = mats[0] if len(mats) == 1 else jnp.concatenate(mats, 0)
    for v in range(vectors):
        part = slice(v * m, (v + 1) * m)
        rhs = jnp.concatenate([hi[part], hi[part], lo[part]], 0)
        res = dot(mat, rhs)
        for j in range(len(bands)):
            out[j].append(res[j * m : (j + 1) * m])
    return [jnp.concatenate(o, 0) for o in out]


def band_of(k, kind, y_kind):
    if kind == "s":
        return 3 * LEVELS if y_kind == "s" else 3 * (k - 1)
    return 3 * (k - 1) + (1 if y_kind == "s" else 2)


def weigh_c(r_ref, spans, kind, levels, tiles):
    which = [
        (k, y_kind)
        for k in levels
        for y_kind in ("s", "d")
        if kind == "d" or y_kind == "d" or k == LEVELS
    ]
    value = jnp.concatenate(tiles, 1) if len(tiles) > 1 else tiles[0]
    res = weigh(r_ref, [band_of(k, kind, y_kind) for k, y_kind in which], value)
    outs = []
    for t in range(len(tiles)):
        out = jnp.zeros_like(tiles[t])
        for (k, y_kind), r in zip(which, res):
            out = jnp.where(in_span(spans[k, y_kind]), r[:, t * TILE : (t + 1) * TILE], out)
        outs.append(out)
    return outs


def weigh_m2(r_ref, kind, tiles):
    lane_d = lanes() >= TILE // 2
    value = jnp.concatenate(tiles, 1) if len(tiles) > 1 else tiles[0]
    if kind == "s":
        res = [None, weigh(r_ref, [band_of(2, "s", "d")], value)[0]]
    else:
        res = weigh(r_ref, [band_of(2, "d", "s"), band_of(2, "d", "d")], value)
    outs = []
    for t in range(len(tiles)):
        a, b = (0.0 if r is None else r[:, t * TILE : (t + 1) * TILE] for r in res)
        outs.append(jnp.where(lane_d, b, a))
    return outs


def weigh_tiles(r_ref, band, tiles):
    value = jnp.concatenate(tiles, 1) if len(tiles) > 1 else tiles[0]
    res = weigh(r_ref, [band], value)[0]
    return [res[:, t * TILE : (t + 1) * TILE] for t in range(len(tiles))]


def groups(low, high, size):
    return [list(range(i, min(i + size, high + 1))) for i in range(low, high + 1, size)]


def weighted_plan(nx):
    n2 = nx >> 2
    plan, at = {}, 0
    for name, count in ((("m2", "d"), n2 + 2), (("m2", "s"), n2 + 1), (("c", "d"), n2 + 2), (("c", "s"), n2 + 1)):
        plan[name] = at
        at += count
    return plan, at


def pairs_into(ref, row, g, tiles):
    rows, width = slice(row * g, (row + 1) * g), len(tiles) * TILE
    for t, tile in enumerate(tiles):
        if tile is None:
            continue
        cols = slice(t * TILE, (t + 1) * TILE)
        ref[rows, cols], ref[rows, width + t * TILE : width + (t + 1) * TILE] = split(tile)


def stack_back(s_ref, which, out, spans_of_rows):
    at = 0
    for a, b in spans_of_rows * 2:
        out[at : at + b - a] = s_ref[which, a:b]
        at += b - a


def first_level_rows(ny):
    half, c = ny // 2, (ny + ny // 2, ny + ny // 2 + TILE)
    return [(0, ny), c], [(half, ny), c]


def local_kernel(nx, edge_ref, var_ref, ym_ref, z, y2_ref, cc_ref, p_ref, s_ref, r_ref,
                 vd_ref, vs_ref, w_ref, y, p2, zd, zs, sd, ss):
    g, ny = y.shape[1], y.shape[2]
    _, spans = lane_plan(ny)
    n1, n2 = nx >> 1, nx >> 2
    plan, _ = weighted_plan(nx)
    n = 2 * TILE
    p2[0:n], p2[n : 2 * n] = p_ref[:, 0:ny], p_ref[:, 0:ny]
    rows_d, rows_s = first_level_rows(ny)
    stack_back(s_ref, var_ref[0], sd, rows_d)
    stack_back(s_ref, var_ref[0], ss, rows_s)
    step = 4
    for r in range(0, nx, step):
        res = dot(z[r * g : (r + step) * g], p2[...])
        y[r : r + step] = ym_ref[r : r + step, :, 0:ny] + res.reshape(step, g, ny)

    def lift(columns):
        return Lift(nx, lambda i: y[i, :, columns], edge_ref)

    a, b = (lift(slice(t * TILE, (t + 1) * TILE)) for t in range(2))
    m2 = Lift(nx, lambda i: y2_ref[i], edge_ref)

    def store(name, low, some, tiles):
        for i, tile in zip(some, tiles):
            w_ref[plan[name] + i - low] = tile

    here = in_span(spans[1])

    def weighed_c(kind, low, some):
        base = 0 if kind == "d" else n1 + 1
        out = {}
        by_levels = {}
        for i in some:
            by_levels.setdefault(tuple(k for k in range(1, LEVELS + 1) if i <= nx >> k), []).append(i)
        for levels, part in by_levels.items():
            tiles = weigh_c(r_ref, spans, kind, list(levels), [cc_ref[base + i - low] for i in part])
            for i, tile in zip(part, tiles):
                if i <= n2:
                    w_ref[plan["c", kind] + i - low] = tile
                out[i] = jnp.where(here, tile, 0.0) if i <= n2 else tile
        return [out[i] for i in some]

    for some in groups(-1, n1 - 1, 4):
        ta = weigh_tiles(r_ref, band_of(1, "d", "s"), [a.detail(1, i) for i in some])
        tb = weigh_tiles(r_ref, band_of(1, "d", "d"), [b.detail(1, i) for i in some])
        tc = weighed_c("d", -1, some)
        for i, tiles in zip(some, zip(ta, tb, tc)):
            pairs_into(zd, i + 1, g, tiles)
        first, count = some[0] + 1, len(some)
        vd_ref[first : first + count] = dot(zd[first * g : (first + count) * g], sd[...]).reshape(count, g, ny)
    for some in groups(0, n1, 4):
        tb = weigh_tiles(r_ref, band_of(1, "s", "d"), [b.smooth(1, i) for i in some])
        tc = weighed_c("s", 0, some)
        for i, tiles in zip(some, zip(tb, tc)):
            pairs_into(zs, i, g, tiles)
        first, count = some[0], len(some)
        vs_ref[first : first + count] = dot(zs[first * g : (first + count) * g], ss[...]).reshape(count, g, ny)
    for some in groups(-1, n2, 4):
        store(("m2", "d"), -1, some, weigh_m2(r_ref, "d", [m2.detail(2, i) for i in some]))
    for some in groups(0, n2, 4):
        store(("m2", "s"), 0, some, weigh_m2(r_ref, "s", [m2.smooth(2, i) for i in some]))


def final_kernel(nx, far, edge_ref, var_ref, vd_ref, vs_ref, w_ref, e_one, e_two, r_one, r_two, *rest):
    if far:
        f_one, f_two = rest[:2]
        rest = rest[2:]
    s_ref, r_ref, out_ref, sd, ss, sdeep, zd, zs, zdeep, rows, ot, sem = rest
    g, ny = ot.shape[1], ot.shape[3]
    _, spans = lane_plan(ny)
    plan, _ = weighted_plan(nx)
    half = ny // 2
    n1, n2 = nx >> 1, nx >> 2
    rows_d, rows_s = first_level_rows(ny)
    stack_back(s_ref, var_ref[0], sd, rows_d)
    stack_back(s_ref, var_ref[0], ss, rows_s)
    stack_back(s_ref, var_ref[0], sdeep, [(ny, ny + half + TILE)])
    s_lanes = smooth_lanes(spans)
    lev1 = in_span(spans[1])

    def smooth_c(value):
        return jnp.where(s_lanes, 0.25 * value, 0.0)

    below, above = from_pairs(var_ref[2], r_one, r_two)
    first_below, first_above = from_pairs(var_ref[2], e_one, e_two)
    c_d = {-1: below[3], 0: below[4], "n-1": above[3], "n": above[4]}
    c_s = {
        0: below[5] + jnp.where(lev1, smooth_c(c_d[-1]), 0.0),
        1: smooth_c(c_d[0]),
        "n-1": smooth_c(c_d["n-1"]),
        "n": above[5],
    }
    if far:
        (far_below,), (far_above,) = from_pairs(var_ref[3], f_one, f_two)
        c_d[-1] = c_d[-1] + far_below
        c_s[0] = c_s[0] + smooth_c(far_below)
        c_d["n"] = c_d["n"] + far_above
        c_s["n"] = c_s["n"] + smooth_c(far_above)
    fixes = [get_fix(below[2], 0)] + [get_fix(above[2], j) for j in range(3)]
    a_tiles = [first_below[0] + fixes[0][0], first_above[0] + fixes[1][0], first_above[2] + fixes[2][0]]
    b_tiles = [first_below[1] + fixes[0][1], first_above[1] + fixes[1][1], first_above[3] + fixes[2][1]]
    s_tiles = [0.25 * b_tiles[0], 0.25 * b_tiles[1], first_above[4] + fixes[3][1]]
    every = list(range(1, LEVELS + 1))
    got = {}

    def keep(name, keys, tiles):
        for key, tile in zip(keys, tiles):
            got[name, key] = tile

    for kind, tiles in (("d", c_d), ("s", c_s)):
        keep(("c", kind), list(tiles), weigh_c(r_ref, spans, kind, every, list(tiles.values())))
    keys = [-1, "n-1", "n"]
    ta = weigh_tiles(r_ref, band_of(1, "d", "s"), a_tiles)
    tb = weigh_tiles(r_ref, band_of(1, "d", "d"), b_tiles)
    for j, key in enumerate(keys):
        pairs_into(zd, j, g, [ta[j], tb[j], jnp.where(lev1, got[("c", "d"), key], 0.0)])
    more_d = dot(zd[...], sd[...])
    tb = weigh_tiles(r_ref, band_of(1, "s", "d"), s_tiles)
    for j, key in enumerate([0, "n-1", "n"]):
        pairs_into(zs, j, g, [tb[j], jnp.where(lev1, got[("c", "s"), key], 0.0)])
    more_s = dot(zs[...], ss[...])
    keep(("m2", "d"), [-1, 0, "n-1", "n"], weigh_m2(r_ref, "d", [below[0], below[1], above[0], above[1]]))
    keep(("m2", "s"), [0, 1, "n-1", "n"],
         weigh_m2(r_ref, "s", [below[2], 0.25 * below[1], 0.25 * above[0], above[2]]))

    def value_of(array, kind, k, i):
        n, low = nx >> k, -1 if kind == "d" else 0
        v = w_ref[plan[array, kind] + i - low]
        for key, at in ((-1, -1), (0, 0), (1, 1), ("n-1", n - 1), ("n", n)):
            if at == i and ((array, kind), key) in got:
                v = v + got[(array, kind), key]
        return jnp.where(in_span(spans[k]), v, 0.0) if array == "c" else v

    not_last = edge_ref[1]

    def unlift(n, smooth, detail, emit):
        below, before = detail(-1), None
        for i in range(n + 1):
            here = detail(i)
            even = smooth(i) - 0.25 * (below + here)
            if i == n:
                even = even * not_last
            if i > 0:
                emit(2 * i - 1, below + 0.5 * (before + even))
            emit(2 * i, even)
            below, before = here, even

    for k in range(LEVELS, 1, -1):
        base = level_base(nx, k)

        def smooth_deep(i, k=k, base=base):
            v = value_of("c", "s", k, i)
            return v if k == LEVELS else v + rows[base + i]

        if k > 2:
            def emit(i, value, base=level_base(nx, k - 1)):
                rows[base + i] = value
        else:
            def emit(i, value):
                r = slice(i * g, (i + 1) * g)
                zdeep[r, TILE : 2 * TILE], zdeep[r, 3 * TILE : 4 * TILE] = split(value)

        unlift(nx >> k, smooth_deep, lambda i, k=k: value_of("c", "d", k, i), emit)

    def emit_m2(i, value):
        r = slice(i * g, (i + 1) * g)
        zdeep[r, 0:TILE], zdeep[r, 2 * TILE : 3 * TILE] = split(value)

    unlift(n2, lambda i: value_of("m2", "s", 2, i), lambda i: value_of("m2", "d", 2, i), emit_m2)

    extra_d = {-1: more_d[0:g], n1 - 1: more_d[g : 2 * g], n1: more_d[2 * g :]}
    extra_s = {0: more_s[0:g], n1 - 1: more_s[g : 2 * g], n1: more_s[2 * g :]}
    step = 4
    deep = {}

    def smooth_first(i):
        if i % step == 0:
            count = min(step, n1 + 1 - i)
            res = dot(zdeep[i * g : (i + count) * g], sdeep[...])
            for j in range(count):
                deep[i + j] = res[j * g : (j + 1) * g]
        v = deep[i] + vs_ref[i]
        return v + extra_s[i] if i in extra_s else v

    def detail_first(i):
        if i == n1:
            return extra_d[i]
        v = vd_ref[i + 1]
        return v + extra_d[i] if i in extra_d else v

    copies = []

    pending = {}

    def emit_out(i, value):
        if i >= nx:
            return
        pending[i] = value
        r = i - i % 8
        if all(j in pending for j in range(r, r + 8)):
            block = jnp.stack([pending.pop(j) for j in range(r, r + 8)], 0)
            ot[r // 8] = jnp.swapaxes(block, 0, 1)
            copies.append(pltpu.make_async_copy(ot.at[r // 8], out_ref.at[:, pl.ds(r, 8)], sem.at[r // 8]))
            copies[-1].start()

    unlift(n1, smooth_first, detail_first, emit_out)
    for copy in copies:
        copy.wait()


def level_base(nx, k):
    return sum((nx >> j) + 1 for j in range(max(k + 1, 3), LEVELS)) if k > 1 else 0


def swap(value, axis, first, step=1):
    count = lax.axis_size(axis)
    starts = [i for i in range(first, count - step) if (i - first) // step % 2 == 0]
    return lax.ppermute(value, axis, [p for i in starts for p in ((i, i + step), (i + step, i))])


def per_device(control, band_roots):
    vectors, m, nx, ny = control.shape
    g = vectors * m
    half = ny // 2
    gx, gy = lax.axis_size("gx"), lax.axis_size("gy")
    per = TILE // SLOT
    assert half == TILE and nx % (2 * per) == 0
    far = (nx >> LEVELS) < 2 and gx > 2
    consts = y_constants(ny, gy)
    main_mat, ehi_mat, elo_mat, s_mat, p_mat = (jnp.asarray(t) for t in consts)
    n1, n2 = nx >> 1, nx >> 2
    mains = ny + half

    r_hi = lax.reduce_precision(band_roots, 8, 7)
    r_lo = band_roots - r_hi
    roots = jnp.concatenate([r_hi.astype(BF), r_lo.astype(BF), r_hi.astype(BF)], 2)

    hbm = pl.BlockSpec(memory_space=pl.ANY)
    vmem = pl.BlockSpec(memory_space=pltpu.VMEM)

    def call(kernel, ins, outs, scratches, name, out_specs=None):
        def body(*refs):
            kernel(*device_place(gx, gy), *refs)

        return pl.pallas_call(
            body,
            out_shape=tuple(jax.ShapeDtypeStruct(*s) for s in outs),
            in_specs=[s for _, s in ins],
            out_specs=out_specs or (vmem,) * len(outs),
            scratch_shapes=scratches,
            name=name,
            compiler_params=pltpu.CompilerParams(vmem_limit_bytes=VMEM_LIMIT),
        )(*[a for a, _ in ins])

    tile = (g, TILE)
    rows3 = control.reshape(g, nx, ny)
    far_hbm = pl.BlockSpec(memory_space=pltpu.HBM)
    xhl, yc, one, two = call(
        partial(first_kernel, nx),
        [(pltpu.with_memory_space_constraint(t, pltpu.HBM), far_hbm) for t in (rows3, ehi_mat, elo_mat)],
        [((nx * g, 3 * ny), BF), ((nx,) + tile, F32), ((nx // per,) + tile, F32), ((nx // per,) + tile, F32)],
        [pltpu.VMEM((nx // per, g, per, ny), F32), pltpu.VMEM((3 * ny, 2 * TILE), BF), pltpu.SemaphoreType.DMA((nx + 3,))],
        "first",
    )
    got_one = swap(one, "gy", 0)
    got_two = swap(two, "gy", 1)
    ym, one, two = call(
        partial(main_kernel, nx),
        [(xhl, vmem), (main_mat, vmem)],
        [((nx, g, mains), F32), ((5,) + tile, F32), ((5,) + tile, F32)],
        [pltpu.VMEM((2 * ny, mains + TILE), BF)],
        "main",
    )
    got = [(swap(one, "gx", 0), vmem), (swap(two, "gx", 1), vmem)]
    slots = 2 * n1 + 2
    sent = call(
        partial(send_kernel, nx, far),
        [(yc, vmem), (ym, vmem), (got_one, vmem), (got_two, vmem), (p_mat, vmem)],
        [((6,) + tile, F32), ((6,) + tile, F32), ((slots,) + tile, F32), ((nx * g, 4 * TILE), BF), ((nx,) + tile, F32)]
        + ([((1,) + tile, F32)] * 2 if far else []),
        [
            pltpu.VMEM((nx,) + tile, F32),
            pltpu.VMEM((4,) + tile, F32),
            pltpu.VMEM((4,) + tile, F32),
            pltpu.VMEM((4 * TILE, mains + TILE), BF),
        ],
        "send",
    )
    got += [(swap(sent[0], "gx", 0), vmem), (swap(sent[1], "gx", 1), vmem)]
    if far:
        got += [(swap(sent[5], "gx", 0, 2), vmem), (swap(sent[6], "gx", 2, 2), vmem)]

    _, count = weighted_plan(nx)
    vd, vs, w = call(
        partial(local_kernel, nx),
        [(ym, vmem), (sent[3], vmem), (sent[4], vmem), (sent[2], vmem), (p_mat, vmem), (s_mat, vmem), (roots, vmem)],
        [((n1 + 1, g, ny), F32), ((n1 + 1, g, ny), F32), ((count,) + tile, F32)],
        [
            pltpu.VMEM((nx, g, ny), F32),
            pltpu.VMEM((4 * TILE, ny), BF),
            pltpu.VMEM(((n1 + 1) * g, 6 * TILE), BF),
            pltpu.VMEM(((n1 + 1) * g, 4 * TILE), BF),
            pltpu.VMEM((6 * TILE, ny), BF),
            pltpu.VMEM((4 * TILE, ny), BF),
        ],
        "local",
    )
    (out,) = call(
        partial(final_kernel, nx, far),
        [(vd, vmem), (vs, vmem), (w, vmem)] + got + [(s_mat, vmem), (roots, vmem)],
        [((g, nx, ny), F32)],
        [
            pltpu.VMEM((6 * TILE, ny), BF),
            pltpu.VMEM((4 * TILE, ny), BF),
            pltpu.VMEM((4 * TILE, ny), BF),
            pltpu.VMEM((3 * g, 6 * TILE), BF),
            pltpu.VMEM((3 * g, 4 * TILE), BF),
            pltpu.VMEM(((n1 + 1) * g, 4 * TILE), BF),
            pltpu.VMEM((level_base(nx, 1) + sum((nx >> j) + 1 for j in range(2, LEVELS)),) + tile, F32),
            pltpu.VMEM((nx // 8, g, 8, ny), F32),
            pltpu.SemaphoreType.DMA((nx // 8,)),
        ],
        "final",
        (hbm,),
    )
    return out.reshape(control.shape)


def solution(mesh):
    in_specs = (P(None, None, "gx", "gy"), P())
    out_specs = P(None, None, "gx", "gy")
    return jax.shard_map(
        per_device, mesh=mesh, in_specs=in_specs, out_specs=out_specs, check_vma=False
    )
```

```python
from functools import lru_cache, partial

import jax
import jax.numpy as jnp
import numpy as np
from jax import lax
from jax.experimental import pallas as pl
from jax.experimental.pallas import tpu as pltpu
from jax.sharding import PartitionSpec as P


LEVELS = 5
TILE = 128
VMEM_LIMIT = 28 * 2**20
BF = jnp.bfloat16
F32 = jnp.float32


def lift_np(signal):
    even, odd = signal[0::2], signal[1::2]
    zero = np.zeros_like(even[:1])
    detail = odd - 0.5 * (even + np.concatenate([even[1:], zero]))
    return even + 0.25 * (np.concatenate([zero, detail[:-1]]) + detail), detail


def unlift_np(smooth, detail):
    zero = np.zeros_like(smooth[:1])
    even = smooth - 0.25 * (np.concatenate([zero, detail[:-1]]) + detail)
    odd = detail + 0.5 * (even + np.concatenate([even[1:], zero]))
    return np.stack([even, odd], 1).reshape(2 * even.shape[0], -1)


def lane_plan(ny):
    place, lane = {}, 0
    spans = {}
    for k in list(range(3, LEVELS + 1)) + [1, 2]:
        n = ny >> k
        first = lane
        for kind, lo in (("s", 0), ("d", -1)):
            start = lane
            for i in range(lo, n + 1):
                if k <= 2 and 0 <= i < n:
                    place[k, kind, i] = (f"m{k}", i + (n if kind == "d" else 0))
                else:
                    place[k, kind, i] = ("c", lane)
                    lane += 1
            spans[k, kind] = (start, lane)
        spans[k] = (first, lane)
    assert lane <= TILE
    return place, spans


SLOT = 16


def edge_lanes(side):
    out = []
    for k in range(1, LEVELS + 1):
        if side > 0:
            out += [(k, "d", -1)] + ([(k, "d", 0), (k, "s", 0)] if k > 1 else [])
        else:
            out += [(k, "d", -1), (k, "d", 0), (k, "s", 0)]
    assert len(out) <= SLOT
    return out


@lru_cache(None)
def y_matrices(ny, below, above):
    place, _ = lane_plan(ny)
    off = ny if below else 0
    size = off + ny + (ny if above else 0)
    width = {"m1": ny, "m2": ny // 2, "c": TILE}
    ana = {a: np.zeros((ny, w)) for a, w in width.items()}
    syn = {a: np.zeros((w, ny)) for a, w in width.items()}
    send = {side: np.zeros((ny, SLOT)) for side in (1, -1)}
    s = np.eye(size)
    for k in range(1, LEVELS + 1):
        s, d = lift_np(s)
        for kind, mat in (("s", s), ("d", d)):
            n, o, own = size >> k, off >> k, ny >> k
            for side in (1, -1):
                for lane, (level, what, i) in enumerate(edge_lanes(side)):
                    at = o + i + (own if side > 0 else 0)
                    if (level, what) == (k, kind) and 0 <= at < n:
                        send[side][:, lane] = mat[at][off : off + ny]
            for i in range(0 if kind == "s" else -1, own + 1):
                if not 0 <= o + i < n:
                    continue
                arr, lane = place[k, kind, i]
                ana[arr][:, lane] = mat[o + i][off : off + ny]
                unit = np.zeros((n, 1))
                unit[o + i] = 1.0
                zero = np.zeros_like(unit)
                back = unlift_np(unit, zero) if kind == "s" else unlift_np(zero, unit)
                for _ in range(k - 1):
                    back = unlift_np(back, np.zeros_like(back))
                syn[arr][lane] = back[off : off + ny, 0]
    return ana, syn, send


@lru_cache(None)
def y_received(ny):
    place, _ = lane_plan(ny)
    base = {"m1": 0, "m2": ny, "c": ny + ny // 2}
    mat = np.zeros((2 * SLOT, base["c"] + TILE))

    def put(row, k, kind, i, value):
        arr, lane = place[k, kind, i]
        mat[row, base[arr] + lane] += value

    for row, (k, kind, i) in enumerate(edge_lanes(1)):
        put(row, k, kind, i, 1.0)
        if kind == "d" and i == (-1 if k == 1 else 0):
            put(row, k, "s", i + 1, 0.25)
    for row, (k, kind, i) in enumerate(edge_lanes(-1)):
        n = ny >> k
        put(SLOT + row, k, kind, n + i, 1.0)
        if kind == "d" and i == -1:
            put(SLOT + row, k, "s", n - 1, 0.25)
    groups = TILE // SLOT
    return np.concatenate([np.tile(mat[:SLOT], (groups, 1)), np.tile(mat[SLOT:], (groups, 1))], 0)


def split_np(mat):
    hi = mat.astype(np.float32).astype(jnp.bfloat16)
    lo = (mat - hi.astype(np.float64)).astype(np.float32).astype(jnp.bfloat16)
    return hi, lo


@lru_cache(None)
def y_constants(ny, count):
    if count == 1:
        kinds = [(False, False)]
    else:
        kinds = [(False, True), (True, True), (True, False)]
    main, e_hi, e_lo, back = [], [], [], []
    for below, above in kinds:
        ana, syn, send = y_matrices(ny, below, above)
        hi, lo = split_np(np.concatenate([ana["m1"], ana["m2"], np.zeros((ny, TILE))], 1))
        assert not np.any(lo.astype(np.float32))
        main.append(hi)
        edge = np.tile(np.concatenate([send[1], send[-1]], 1), (1, TILE // (2 * SLOT)))
        hi, lo = split_np(np.concatenate([ana["c"], edge], 1))
        e_hi.append(hi)
        e_lo.append(lo)
        hi, lo = split_np(np.concatenate([syn["m1"], syn["m2"], syn["c"]], 0))
        assert not np.any(lo.astype(np.float32))
        back.append(hi)
    return np.stack(main), np.stack(e_hi), np.stack(e_lo), np.stack(back), split_np(y_received(ny))[0]


def split(value):
    hi = value.astype(BF)
    return hi, (value - hi.astype(F32)).astype(BF)


def dot(a, b):
    return jnp.dot(a, b, preferred_element_type=F32)


def lanes():
    return lax.broadcasted_iota(jnp.int32, (1, TILE), 1)


def in_span(span):
    lane = lanes()
    return (lane >= span[0]) & (lane < span[1])


def device_place(gx, gy):
    ix, iy = lax.axis_index("gx"), lax.axis_index("gy")
    edge = jnp.where(ix > 0, 1.0, 0.0), jnp.where(ix < gx - 1, 1.0, 0.0)
    kind = jnp.where(iy == 0, 0, jnp.where(iy == gy - 1, 2, 1)) if gy > 1 else 0
    return edge, (kind, lax.rem(iy, 2), lax.rem(ix, 2), lax.rem(ix // 2, 2))


def first_kernel(nx, edge_ref, var_ref, x_ref, ehi_ref, elo_ref, a_ref,
                 xhl, yc_ref, one_ref, two_ref, rows_ref, xt, e3, a2, low, high, sems):
    g, ny = xt.shape[1], xt.shape[3]
    consts = [
        pltpu.make_async_copy(ref.at[var_ref[0]], e3.at[pl.ds(j * ny, ny)], sems.at[nx + j])
        for j, ref in ((0, ehi_ref), (2, elo_ref))
    ]
    late = pltpu.make_async_copy(a_ref.at[var_ref[0], :, pl.ds(0, ny)], a2.at[pl.ds(0, ny)], sems.at[nx + 3])
    per = TILE // SLOT
    copies = [
        pltpu.make_async_copy(x_ref.at[:, pl.ds(r, per)], xt.at[r // per], sems.at[r // per])
        for r in range(0, nx, per)
    ]
    for copy in copies[:1] + consts + copies[1:] + [late]:
        copy.start()
    odd = var_ref[1] == 1
    for r in range(0, nx, per):
        up = down = None
        copies[r // per].wait()
        block = jnp.swapaxes(xt[r // per], 0, 1)
        for q in range(r, r + per, 4):
            for i in range(q, q + 4):
                rows = slice(i * g, (i + 1) * g)
                hi, lo = split(block[i - r])
                xhl[rows, 0:ny], xhl[rows, ny : 2 * ny], xhl[rows, 2 * ny : 3 * ny] = hi, lo, hi
            if q == 0:
                for copy in consts:
                    copy.wait()
                e3[ny : 2 * ny] = e3[0:ny]
            res = dot(xhl[q * g : (q + 4) * g], e3[...])
            for i in range(q, q + 4):
                part = res[(i - q) * g : (i - q + 1) * g]
                yc_ref[i] = part[:, 0:TILE]
                plain = part[:, TILE : 2 * TILE]
                turned = pltpu.roll(plain, SLOT, 1)
                group = lanes() // SLOT == i - r
                a, b = (plain, turned) if i % 2 == 0 else (turned, plain)
                up = jnp.where(group, a, 0.0 if up is None else up)
                down = jnp.where(group, b, 0.0 if down is None else down)
        one_ref[r // per] = jnp.where(odd, down, up)
        two_ref[r // per] = jnp.where(odd, up, down)
    late.wait()
    a2[ny : 2 * ny] = a2[0:ny]
    count, top = low.shape[0], nx - high.shape[0]
    low[...] = dot(xhl[0 : count * g, 0 : 2 * ny], a2[...]).reshape(low.shape)
    high[...] = dot(xhl[top * g :, 0 : 2 * ny], a2[...]).reshape(high.shape)
    lift = Lift(nx, lambda i: low[i], edge_ref, 0, count - 1)
    begin, then = lift.detail(1, -1), lift.detail(1, 0)
    last = Lift(nx, lambda i: high[i - top], edge_ref, top, nx - 1).detail(1, (nx >> 1) - 1)
    for t, value in enumerate((last, begin, then)):
        rows_ref[2 * t], rows_ref[2 * t + 1] = value[:, 0:TILE], value[:, TILE:]


def main_kernel(nx, edge_ref, var_ref, xhl, a_ref, y_ref, a2):
    g, ny = y_ref.shape[1], a_ref.shape[1]
    a2[0:ny], a2[ny : 2 * ny] = a_ref[var_ref[0]], a_ref[var_ref[0]]
    step = 4
    for r in range(0, nx, step):
        res = dot(xhl[r * g : (r + step) * g, 0 : 2 * ny], a2[...])
        y_ref[r : r + step] = res[:, 0 : y_ref.shape[2]].reshape(step, g, y_ref.shape[2])


def relay_kernel(edge_ref, var_ref, rows_ref, up_ref, down_ref, one_ref, two_ref):
    up, down = [up_ref[...]], [down_ref[...]]
    zero = jnp.zeros(up_ref.shape, F32)
    up += [rows_ref[0], rows_ref[1], zero, zero]
    down += [rows_ref[t] for t in range(2, 6)]
    to_pairs(var_ref[3], up, down, one_ref, two_ref)


def to_pairs(odd, up, down, one_ref, two_ref):
    for t, (a, b) in enumerate(zip(up, down)):
        one_ref[t] = jnp.where(odd == 1, b, a)
        two_ref[t] = jnp.where(odd == 1, a, b)


def from_pairs(odd, one_ref, two_ref):
    count = one_ref.shape[0]
    below = [jnp.where(odd == 1, one_ref[t], two_ref[t]) for t in range(count)]
    above = [jnp.where(odd == 1, two_ref[t], one_ref[t]) for t in range(count)]
    return below, above


class Lift:
    def __init__(self, nx, raw, edge_ref, first=0, last=None):
        self.nx, self.raw = nx, raw
        self.first, self.last = first, nx - 1 if last is None else last
        self.not_first, self.not_last = edge_ref[0], edge_ref[1]
        self.known = {}

    def smooth(self, k, i):
        if k == 0:
            if not 0 <= i < self.nx:
                return None
            assert self.first <= i <= self.last
        if (k, "s", i) not in self.known:
            self.known[k, "s", i] = self.raw(i) if k == 0 else self.new_smooth(k, i)
        return self.known[k, "s", i]

    def detail(self, k, i):
        if (k, "d", i) not in self.known:
            self.known[k, "d", i] = self.new_detail(k, i)
        return self.known[k, "d", i]

    def new_detail(self, k, i):
        if not -1 <= i <= self.nx >> k:
            return None
        even, mid, after = (self.smooth(k - 1, j) for j in (2 * i, 2 * i + 1, 2 * i + 2))
        pair = plus(even, after)
        if pair is None:
            return mid
        out = -0.5 * pair if mid is None else mid - 0.5 * pair
        return out * self.not_first if i < 0 else out

    def new_smooth(self, k, i):
        if not -1 <= i <= (self.nx >> k) + 1:
            return None
        even = self.smooth(k - 1, 2 * i)
        pair = plus(self.detail(k, i - 1), self.detail(k, i))
        if pair is None:
            return even if even is None or i < self.nx >> k else even * self.not_last
        out = 0.25 * pair if even is None else even + 0.25 * pair
        return out * self.not_last if i >= self.nx >> k else out


def plus(a, b):
    return b if a is None else a if b is None else a + b


def c_slots(lift, spans, kind, low, high, s_lanes):
    out = []
    for i in range(low, high + 1):
        tile = None
        for k in range(1, LEVELS + 1):
            if i > lift.nx >> k:
                continue
            value = lift.detail(k, i) if kind == "d" else lift.smooth(k, i)
            if value is None:
                continue
            tile = jnp.where(in_span(spans[k]), value, 0.0 if tile is None else tile)
        out.append(jnp.where(s_lanes, tile, 0.0) if kind == "s" else tile)
    return out


def smooth_lanes(spans):
    ok = in_span(spans[LEVELS])
    for k in range(1, LEVELS):
        ok = ok | in_span(spans[k, "d"])
    return ok


def send_kernel(nx, far, edge_ref, var_ref, yc_ref, ym_ref, one_ref, two_ref, p_ref, *rest):
    to_one_ref, to_two_ref, cc_ref, z, y2_ref = rest[:5]
    far_up_ref, far_down_ref, yc, yl, yh, p2 = rest[5:]
    g = yc.shape[1]
    mains = ym_ref.shape[2]
    ny = mains - TILE
    _, spans = lane_plan(ny)
    n1, n2 = nx >> 1, nx >> 2
    n = 2 * TILE
    p2[0:n], p2[n : 2 * n] = p_ref[...], p_ref[...]
    per = TILE // SLOT
    group = lanes() // SLOT
    zero = jnp.zeros((g, TILE), BF)
    odd = var_ref[1] == 1
    for t in range(nx // per):
        from_below = jnp.where(odd, one_ref[t], two_ref[t])
        from_above = jnp.where(odd, two_ref[t], one_ref[t])
        pieces = split(from_below) + split(from_above)
        for i in range(per):
            here = group == i
            rows = slice((t * per + i) * g, (t * per + i + 1) * g)
            for c, j in enumerate((0, 2, 1, 3)):
                z[rows, c * TILE : (c + 1) * TILE] = jnp.where(here, pieces[j], zero)
    step = 4
    for r in range(0, nx, step):
        res = dot(z[r * g : (r + step) * g], p2[:, ny : mains + TILE])
        y2_ref[r : r + step] = ym_ref[r : r + step, :, ny:mains] + res[:, 0:TILE].reshape(step, g, TILE)
        yc[r : r + step] = yc_ref[r : r + step] + res[:, TILE:].reshape(step, g, TILE)
    low, high = yl.shape[0], yh.shape[0]
    yl[...] = dot(z[0 : low * g], p2[:, 0:TILE]).reshape(yl.shape)
    yh[...] = dot(z[(nx - high) * g :], p2[:, 0:TILE]).reshape(yh.shape)

    def lift(ref, base):
        return Lift(nx, lambda i: ref[i - base], edge_ref, base, base + ref.shape[0] - 1)

    second = Lift(nx, lambda i: y2_ref[i], edge_ref)
    one, two = lift(yl, 0), lift(yh, nx - high)
    fix_up = [two.detail(1, n1 - 1)]
    fix_down = [one.detail(1, -1), one.detail(1, 0)]
    up = [second.detail(2, n2 - 1), second.detail(2, n2), put_fixes(second.smooth(2, n2), fix_up)]
    down = [second.detail(2, -1), second.detail(2, 0), put_fixes(second.smooth(2, 0), fix_down)]

    s_lanes = smooth_lanes(spans)
    deep = Lift(nx, lambda i: yc[i], edge_ref)
    for j, tile in enumerate(c_slots(deep, spans, "d", -1, n1 - 1, s_lanes)):
        cc_ref[j] = tile
    for j, tile in enumerate(c_slots(deep, spans, "s", 0, n1, s_lanes)):
        cc_ref[n1 + 1 + j] = tile
    acc = [jnp.zeros((g, TILE), F32)] * 3
    for k in range(1, LEVELS + 1):
        n, here = nx >> k, in_span(spans[k])
        new = [deep.detail(k, n - 1)] + ([deep.detail(k, n), deep.smooth(k, n)] if k > 1 else [None] * 2)
        acc = [a if v is None else jnp.where(here, v, a) for a, v in zip(acc, new)]
    to_pairs(var_ref[2], up + acc, down + [cc_ref[0], cc_ref[1], cc_ref[n1 + 1]], to_one_ref, to_two_ref)
    here = in_span(spans[LEVELS]) if far else lanes() < 0
    far_up_ref[...] = jnp.where(here, deep.detail(LEVELS, nx >> LEVELS), 0.0)
    far_down_ref[...] = jnp.where(here, deep.detail(LEVELS, -1), 0.0)


def put_fixes(tile, fixes):
    lane = lanes()
    for j, fix in enumerate(fixes):
        tile = jnp.where((lane >> 1) == j, pltpu.roll(fix, 1 + 2 * j, 1), tile)
    return tile


def get_fix(tile, j):
    lane = lanes()
    turned = pltpu.roll(tile, TILE - 1 - 2 * j, 1)
    a = jnp.where((lane == 0) | (lane == TILE - 1), turned, 0.0)
    return a, jnp.where(lane == TILE - 1, 4.0 * turned, 0.0)


def weigh(r_ref, bands, value):
    m = r_ref.shape[1]
    vectors = value.shape[0] // m
    hi, lo = split(value)
    out = [[] for _ in bands]
    mats = [r_ref[b] for b in bands]
    mat = mats[0] if len(mats) == 1 else jnp.concatenate(mats, 0)
    for v in range(vectors):
        part = slice(v * m, (v + 1) * m)
        rhs = jnp.concatenate([hi[part], hi[part], lo[part]], 0)
        res = dot(mat, rhs)
        for j in range(len(bands)):
            out[j].append(res[j * m : (j + 1) * m])
    return [jnp.concatenate(o, 0) for o in out]


def band_of(k, kind, y_kind):
    if kind == "s":
        return 3 * LEVELS if y_kind == "s" else 3 * (k - 1)
    return 3 * (k - 1) + (1 if y_kind == "s" else 2)


def weigh_c(r_ref, spans, kind, levels, tiles):
    which = [
        (k, y_kind)
        for k in levels
        for y_kind in ("s", "d")
        if kind == "d" or y_kind == "d" or k == LEVELS
    ]
    value = jnp.concatenate(tiles, 1) if len(tiles) > 1 else tiles[0]
    res = weigh(r_ref, [band_of(k, kind, y_kind) for k, y_kind in which], value)
    outs = []
    for t in range(len(tiles)):
        out = jnp.zeros_like(tiles[t])
        for (k, y_kind), r in zip(which, res):
            out = jnp.where(in_span(spans[k, y_kind]), r[:, t * TILE : (t + 1) * TILE], out)
        outs.append(out)
    return outs


def weigh_m2(r_ref, kind, tiles):
    lane_d = lanes() >= TILE // 2
    value = jnp.concatenate(tiles, 1) if len(tiles) > 1 else tiles[0]
    if kind == "s":
        res = [None, weigh(r_ref, [band_of(2, "s", "d")], value)[0]]
    else:
        res = weigh(r_ref, [band_of(2, "d", "s"), band_of(2, "d", "d")], value)
    outs = []
    for t in range(len(tiles)):
        a, b = (0.0 if r is None else r[:, t * TILE : (t + 1) * TILE] for r in res)
        outs.append(jnp.where(lane_d, b, a))
    return outs


def weigh_tiles(r_ref, band, tiles):
    value = jnp.concatenate(tiles, 1) if len(tiles) > 1 else tiles[0]
    res = weigh(r_ref, [band], value)[0]
    return [res[:, t * TILE : (t + 1) * TILE] for t in range(len(tiles))]


def groups(low, high, size):
    return [list(range(i, min(i + size, high + 1))) for i in range(low, high + 1, size)]


def weighted_plan(nx):
    n2 = nx >> 2
    plan, at = {}, 0
    for name, count in ((("m2", "d"), n2 + 2), (("m2", "s"), n2 + 1), (("c", "d"), n2 + 2), (("c", "s"), n2 + 1)):
        plan[name] = at
        at += count
    return plan, at


def pairs_into(ref, row, g, tiles):
    rows, width = slice(row * g, (row + 1) * g), len(tiles) * TILE
    for t, tile in enumerate(tiles):
        if tile is None:
            continue
        cols = slice(t * TILE, (t + 1) * TILE)
        ref[rows, cols], ref[rows, width + t * TILE : width + (t + 1) * TILE] = split(tile)


def stack_back(s_ref, which, out, spans_of_rows):
    at = 0
    for a, b in spans_of_rows * 2:
        out[at : at + b - a] = s_ref[which, a:b]
        at += b - a


def first_level_rows(ny):
    half, c = ny // 2, (ny + ny // 2, ny + ny // 2 + TILE)
    return [(0, ny), c], [(half, ny), c]


def local_kernel(nx, edge_ref, var_ref, ym_ref, z, y2_ref, cc_ref, p_ref, s_ref, r_ref,
                 vd_ref, vs_ref, w_ref, y, p2, zd, zs, sd, ss):
    g, ny = y.shape[1], y.shape[2]
    _, spans = lane_plan(ny)
    n1, n2 = nx >> 1, nx >> 2
    plan, _ = weighted_plan(nx)
    n = 2 * TILE
    p2[0:n], p2[n : 2 * n] = p_ref[:, 0:ny], p_ref[:, 0:ny]
    rows_d, rows_s = first_level_rows(ny)
    stack_back(s_ref, var_ref[0], sd, rows_d)
    stack_back(s_ref, var_ref[0], ss, rows_s)
    step = 4
    for r in range(0, nx, step):
        res = dot(z[r * g : (r + step) * g], p2[...])
        y[r : r + step] = ym_ref[r : r + step, :, 0:ny] + res.reshape(step, g, ny)

    def lift(columns):
        return Lift(nx, lambda i: y[i, :, columns], edge_ref)

    a, b = (lift(slice(t * TILE, (t + 1) * TILE)) for t in range(2))
    m2 = Lift(nx, lambda i: y2_ref[i], edge_ref)

    def store(name, low, some, tiles):
        for i, tile in zip(some, tiles):
            w_ref[plan[name] + i - low] = tile

    here = in_span(spans[1])

    def weighed_c(kind, low, some):
        base = 0 if kind == "d" else n1 + 1
        out = {}
        by_levels = {}
        for i in some:
            by_levels.setdefault(tuple(k for k in range(1, LEVELS + 1) if i <= nx >> k), []).append(i)
        for levels, part in by_levels.items():
            tiles = weigh_c(r_ref, spans, kind, list(levels), [cc_ref[base + i - low] for i in part])
            for i, tile in zip(part, tiles):
                if i <= n2:
                    w_ref[plan["c", kind] + i - low] = tile
                out[i] = jnp.where(here, tile, 0.0) if i <= n2 else tile
        return [out[i] for i in some]

    for some in groups(-1, n1 - 1, 4):
        ta = weigh_tiles(r_ref, band_of(1, "d", "s"), [a.detail(1, i) for i in some])
        tb = weigh_tiles(r_ref, band_of(1, "d", "d"), [b.detail(1, i) for i in some])
        tc = weighed_c("d", -1, some)
        for i, tiles in zip(some, zip(ta, tb, tc)):
            pairs_into(zd, i + 1, g, tiles)
        first, count = some[0] + 1, len(some)
        vd_ref[first : first + count] = dot(zd[first * g : (first + count) * g], sd[...]).reshape(count, g, ny)
    for some in groups(0, n1, 4):
        tb = weigh_tiles(r_ref, band_of(1, "s", "d"), [b.smooth(1, i) for i in some])
        tc = weighed_c("s", 0, some)
        for i, tiles in zip(some, zip(tb, tc)):
            pairs_into(zs, i, g, tiles)
        first, count = some[0], len(some)
        vs_ref[first : first + count] = dot(zs[first * g : (first + count) * g], ss[...]).reshape(count, g, ny)
    for some in groups(-1, n2, 4):
        store(("m2", "d"), -1, some, weigh_m2(r_ref, "d", [m2.detail(2, i) for i in some]))
    for some in groups(0, n2, 4):
        store(("m2", "s"), 0, some, weigh_m2(r_ref, "s", [m2.smooth(2, i) for i in some]))


def final_kernel(nx, edge_ref, var_ref, vd_ref, vs_ref, w_ref, near, r_one, r_two, f_one, f_two,
                 s_ref, r_ref, out_ref, sd, ss, sdeep, zd, zs, zdeep, rows, ot, sem):
    g, ny = ot.shape[1], ot.shape[3]
    _, spans = lane_plan(ny)
    plan, _ = weighted_plan(nx)
    half = ny // 2
    n1, n2 = nx >> 1, nx >> 2
    rows_d, rows_s = first_level_rows(ny)
    stack_back(s_ref, var_ref[0], sd, rows_d)
    stack_back(s_ref, var_ref[0], ss, rows_s)
    stack_back(s_ref, var_ref[0], sdeep, [(ny, ny + half + TILE)])
    s_lanes = smooth_lanes(spans)
    lev1 = in_span(spans[1])

    def smooth_c(value):
        return jnp.where(s_lanes, 0.25 * value, 0.0)

    below, above = from_pairs(var_ref[2], r_one, r_two)
    far_below, far_above = from_pairs(var_ref[3], f_one, f_two)
    odd = var_ref[2] == 1
    first_below = [jnp.where(odd, near[t], far_below[1 + t]) for t in range(2)]
    first_above = [jnp.where(odd, far_above[1 + t], near[2 + t]) for t in range(4)]
    c_d = {-1: below[3], 0: below[4], "n-1": above[3], "n": above[4]}
    c_s = {
        0: below[5] + jnp.where(lev1, smooth_c(c_d[-1]), 0.0),
        1: smooth_c(c_d[0]),
        "n-1": smooth_c(c_d["n-1"]),
        "n": above[5],
    }
    c_d[-1] = c_d[-1] + far_below[0]
    c_s[0] = c_s[0] + smooth_c(far_below[0])
    c_d["n"] = c_d["n"] + far_above[0]
    c_s["n"] = c_s["n"] + smooth_c(far_above[0])
    fixes = [get_fix(below[2], 0)] + [get_fix(above[2], j) for j in range(2)]
    a_tiles = [first_below[0] + fixes[0][0], first_above[0] + fixes[1][0], first_above[2] + fixes[2][0]]
    b_tiles = [first_below[1] + fixes[0][1], first_above[1] + fixes[1][1], first_above[3] + fixes[2][1]]
    s_tiles = [0.25 * b_tiles[0], 0.25 * b_tiles[1], 0.25 * b_tiles[2] - 1.75 * b_tiles[1]]
    every = list(range(1, LEVELS + 1))
    got = {}

    def keep(name, keys, tiles):
        for key, tile in zip(keys, tiles):
            got[name, key] = tile

    for kind, tiles in (("d", c_d), ("s", c_s)):
        keep(("c", kind), list(tiles), weigh_c(r_ref, spans, kind, every, list(tiles.values())))
    keys = [-1, "n-1", "n"]
    ta = weigh_tiles(r_ref, band_of(1, "d", "s"), a_tiles)
    tb = weigh_tiles(r_ref, band_of(1, "d", "d"), b_tiles)
    for j, key in enumerate(keys):
        pairs_into(zd, j, g, [ta[j], tb[j], jnp.where(lev1, got[("c", "d"), key], 0.0)])
    more_d = dot(zd[...], sd[...])
    tb = weigh_tiles(r_ref, band_of(1, "s", "d"), s_tiles)
    for j, key in enumerate([0, "n-1", "n"]):
        pairs_into(zs, j, g, [tb[j], jnp.where(lev1, got[("c", "s"), key], 0.0)])
    more_s = dot(zs[...], ss[...])
    keep(("m2", "d"), [-1, 0, "n-1", "n"], weigh_m2(r_ref, "d", [below[0], below[1], above[0], above[1]]))
    keep(("m2", "s"), [0, 1, "n-1", "n"],
         weigh_m2(r_ref, "s", [below[2], 0.25 * below[1], 0.25 * above[0], above[2]]))

    def value_of(array, kind, k, i):
        n, low = nx >> k, -1 if kind == "d" else 0
        v = w_ref[plan[array, kind] + i - low]
        for key, at in ((-1, -1), (0, 0), (1, 1), ("n-1", n - 1), ("n", n)):
            if at == i and ((array, kind), key) in got:
                v = v + got[(array, kind), key]
        return jnp.where(in_span(spans[k]), v, 0.0) if array == "c" else v

    not_last = edge_ref[1]

    def unlift(n, smooth, detail, emit):
        below, before = detail(-1), None
        for i in range(n + 1):
            here = detail(i)
            even = smooth(i) - 0.25 * (below + here)
            if i == n:
                even = even * not_last
            if i > 0:
                emit(2 * i - 1, below + 0.5 * (before + even))
            emit(2 * i, even)
            below, before = here, even

    for k in range(LEVELS, 1, -1):
        base = level_base(nx, k)

        def smooth_deep(i, k=k, base=base):
            v = value_of("c", "s", k, i)
            return v if k == LEVELS else v + rows[base + i]

        if k > 2:
            def emit(i, value, base=level_base(nx, k - 1)):
                rows[base + i] = value
        else:
            def emit(i, value):
                r = slice(i * g, (i + 1) * g)
                zdeep[r, TILE : 2 * TILE], zdeep[r, 3 * TILE : 4 * TILE] = split(value)

        unlift(nx >> k, smooth_deep, lambda i, k=k: value_of("c", "d", k, i), emit)

    def emit_m2(i, value):
        r = slice(i * g, (i + 1) * g)
        zdeep[r, 0:TILE], zdeep[r, 2 * TILE : 3 * TILE] = split(value)

    unlift(n2, lambda i: value_of("m2", "s", 2, i), lambda i: value_of("m2", "d", 2, i), emit_m2)

    extra_d = {-1: more_d[0:g], n1 - 1: more_d[g : 2 * g], n1: more_d[2 * g :]}
    extra_s = {0: more_s[0:g], n1 - 1: more_s[g : 2 * g], n1: more_s[2 * g :]}
    step = 4
    deep = {}

    def smooth_first(i):
        if i % step == 0:
            count = min(step, n1 + 1 - i)
            res = dot(zdeep[i * g : (i + count) * g], sdeep[...])
            for j in range(count):
                deep[i + j] = res[j * g : (j + 1) * g]
        v = deep[i] + vs_ref[i]
        return v + extra_s[i] if i in extra_s else v

    def detail_first(i):
        if i == n1:
            return extra_d[i]
        v = vd_ref[i + 1]
        return v + extra_d[i] if i in extra_d else v

    copies = []

    pending = {}

    def emit_out(i, value):
        if i >= nx:
            return
        pending[i] = value
        r = i - i % 8
        if all(j in pending for j in range(r, r + 8)):
            block = jnp.stack([pending.pop(j) for j in range(r, r + 8)], 0)
            ot[r // 8] = jnp.swapaxes(block, 0, 1)
            copies.append(pltpu.make_async_copy(ot.at[r // 8], out_ref.at[:, pl.ds(r, 8)], sem.at[r // 8]))
            copies[-1].start()

    unlift(n1, smooth_first, detail_first, emit_out)
    for copy in copies:
        copy.wait()


def level_base(nx, k):
    return sum((nx >> j) + 1 for j in range(max(k + 1, 3), LEVELS)) if k > 1 else 0


def swap(value, axis, first, step=1):
    count = lax.axis_size(axis)
    starts = [i for i in range(first, count - step) if (i - first) // step % 2 == 0]
    return lax.ppermute(value, axis, [p for i in starts for p in ((i, i + step), (i + step, i))])


def per_device(control, band_roots):
    vectors, m, nx, ny = control.shape
    g = vectors * m
    half = ny // 2
    gx, gy = lax.axis_size("gx"), lax.axis_size("gy")
    per = TILE // SLOT
    assert half == TILE and nx % (2 * per) == 0
    far = (nx >> LEVELS) < 2 and gx > 2
    consts = y_constants(ny, gy)
    main_mat, ehi_mat, elo_mat, s_mat, p_mat = (jnp.asarray(t) for t in consts)
    n1 = nx >> 1
    mains = ny + half

    r_hi = lax.reduce_precision(band_roots, 8, 7)
    r_lo = band_roots - r_hi
    roots = jnp.concatenate([r_hi.astype(BF), r_lo.astype(BF), r_hi.astype(BF)], 2)

    hbm = pl.BlockSpec(memory_space=pl.ANY)
    vmem = pl.BlockSpec(memory_space=pltpu.VMEM)

    def call(kernel, ins, outs, scratches, out_specs=None):
        def body(*refs):
            kernel(*device_place(gx, gy), *refs)

        return pl.pallas_call(
            body,
            out_shape=tuple(jax.ShapeDtypeStruct(*s) for s in outs),
            in_specs=[s for _, s in ins],
            out_specs=out_specs or (vmem,) * len(outs),
            scratch_shapes=scratches,
            compiler_params=pltpu.CompilerParams(vmem_limit_bytes=VMEM_LIMIT),
        )(*[a for a, _ in ins])

    tile = (g, TILE)
    rows3 = control.reshape(g, nx, ny)
    far_hbm = pl.BlockSpec(memory_space=pltpu.HBM)
    xhl, yc, one, two, rows = call(
        partial(first_kernel, nx),
        [
            (pltpu.with_memory_space_constraint(t, pltpu.HBM), far_hbm)
            for t in (rows3, ehi_mat, elo_mat, main_mat)
        ],
        [((nx * g, 3 * ny), BF), ((nx,) + tile, F32), ((nx // per,) + tile, F32), ((nx // per,) + tile, F32),
         ((6,) + tile, F32)],
        [pltpu.VMEM((nx // per, g, per, ny), F32), pltpu.VMEM((3 * ny, 2 * TILE), BF),
         pltpu.VMEM((2 * ny, ny), BF), pltpu.VMEM((4, g, ny), F32), pltpu.VMEM((4, g, ny), F32),
         pltpu.SemaphoreType.DMA((nx + 4,))],
    )
    near = swap(rows, "gx", 0)
    got_one = swap(one, "gy", 0)
    got_two = swap(two, "gy", 1)
    (ym,) = call(
        partial(main_kernel, nx),
        [(xhl, vmem), (main_mat, vmem)],
        [((nx, g, mains), F32)],
        [pltpu.VMEM((2 * ny, mains + TILE), BF)],
    )
    slots = 2 * n1 + 2
    sent = call(
        partial(send_kernel, nx, far),
        [(yc, vmem), (ym, vmem), (got_one, vmem), (got_two, vmem), (p_mat, vmem)],
        [((6,) + tile, F32), ((6,) + tile, F32), ((slots,) + tile, F32), ((nx * g, 4 * TILE), BF), ((nx,) + tile, F32)]
        + [(tile, F32)] * 2,
        [
            pltpu.VMEM((nx,) + tile, F32),
            pltpu.VMEM((4,) + tile, F32),
            pltpu.VMEM((4,) + tile, F32),
            pltpu.VMEM((4 * TILE, mains + TILE), BF),
        ],
    )
    got = [near, swap(sent[0], "gx", 0), swap(sent[1], "gx", 1)]
    far_one, far_two = call(relay_kernel, [(t, vmem) for t in (near, sent[5], sent[6])], [((5,) + tile, F32)] * 2, [])
    got += [swap(far_one, "gx", 0, 2), swap(far_two, "gx", 2, 2)]

    _, count = weighted_plan(nx)
    vd, vs, w = call(
        partial(local_kernel, nx),
        [(ym, vmem), (sent[3], vmem), (sent[4], vmem), (sent[2], vmem), (p_mat, vmem), (s_mat, vmem), (roots, vmem)],
        [((n1 + 1, g, ny), F32), ((n1 + 1, g, ny), F32), ((count,) + tile, F32)],
        [
            pltpu.VMEM((nx, g, ny), F32),
            pltpu.VMEM((4 * TILE, ny), BF),
            pltpu.VMEM(((n1 + 1) * g, 6 * TILE), BF),
            pltpu.VMEM(((n1 + 1) * g, 4 * TILE), BF),
            pltpu.VMEM((6 * TILE, ny), BF),
            pltpu.VMEM((4 * TILE, ny), BF),
        ],
    )
    (out,) = call(
        partial(final_kernel, nx),
        [(t, vmem) for t in [vd, vs, w] + got + [s_mat, roots]],
        [((g, nx, ny), F32)],
        [
            pltpu.VMEM((6 * TILE, ny), BF),
            pltpu.VMEM((4 * TILE, ny), BF),
            pltpu.VMEM((4 * TILE, ny), BF),
            pltpu.VMEM((3 * g, 6 * TILE), BF),
            pltpu.VMEM((3 * g, 4 * TILE), BF),
            pltpu.VMEM(((n1 + 1) * g, 4 * TILE), BF),
            pltpu.VMEM((level_base(nx, 1) + sum((nx >> j) + 1 for j in range(2, LEVELS)),) + tile, F32),
            pltpu.VMEM((nx // 8, g, 8, ny), F32),
            pltpu.SemaphoreType.DMA((nx // 8,)),
        ],
        (hbm,),
    )
    return out.reshape(control.shape)


def solution(mesh):
    spec = P(None, None, "gx", "gy")
    return jax.shard_map(per_device, mesh=mesh, in_specs=(spec, P()), out_specs=spec, check_vma=False)
```

```python
from functools import lru_cache, partial

import jax
import jax.numpy as jnp
import numpy as np
from jax import lax
from jax.experimental import pallas as pl
from jax.experimental.pallas import tpu as pltpu
from jax.sharding import PartitionSpec as P


LEVELS = 5
TILE = 128
VMEM_LIMIT = 28 * 2**20
BF = jnp.bfloat16
F32 = jnp.float32


def lift_np(signal):
    even, odd = signal[0::2], signal[1::2]
    zero = np.zeros_like(even[:1])
    detail = odd - 0.5 * (even + np.concatenate([even[1:], zero]))
    return even + 0.25 * (np.concatenate([zero, detail[:-1]]) + detail), detail


def unlift_np(smooth, detail):
    zero = np.zeros_like(smooth[:1])
    even = smooth - 0.25 * (np.concatenate([zero, detail[:-1]]) + detail)
    odd = detail + 0.5 * (even + np.concatenate([even[1:], zero]))
    return np.stack([even, odd], 1).reshape(2 * even.shape[0], -1)


def lane_plan(ny):
    place, lane = {}, 0
    spans = {}
    for k in list(range(3, LEVELS + 1)) + [1, 2]:
        n = ny >> k
        first = lane
        for kind, lo in (("s", 0), ("d", -1)):
            start = lane
            for i in range(lo, n + 1):
                if k <= 2 and 0 <= i < n:
                    place[k, kind, i] = (f"m{k}", i + (n if kind == "d" else 0))
                else:
                    place[k, kind, i] = ("c", lane)
                    lane += 1
            spans[k, kind] = (start, lane)
        spans[k] = (first, lane)
    assert lane <= TILE
    return place, spans


SLOT = 16
REACH = 64


def edge_lanes(side):
    out = []
    for k in range(1, LEVELS + 1):
        if side > 0:
            out += [(k, "d", -1)] + ([(k, "d", 0), (k, "s", 0)] if k > 1 else [])
        else:
            out += [(k, "d", -1), (k, "d", 0), (k, "s", 0)]
    assert len(out) <= SLOT
    return out


@lru_cache(None)
def y_matrices(ny, below, above):
    place, _ = lane_plan(ny)
    off = ny if below else 0
    size = off + ny + (ny if above else 0)
    width = {"m1": ny, "m2": ny // 2, "c": TILE}
    ana = {a: np.zeros((ny, w)) for a, w in width.items()}
    syn = {a: np.zeros((w, ny)) for a, w in width.items()}
    send = {side: np.zeros((ny, SLOT)) for side in (1, -1)}
    s = np.eye(size)
    for k in range(1, LEVELS + 1):
        s, d = lift_np(s)
        for kind, mat in (("s", s), ("d", d)):
            n, o, own = size >> k, off >> k, ny >> k
            for side in (1, -1):
                for lane, (level, what, i) in enumerate(edge_lanes(side)):
                    at = o + i + (own if side > 0 else 0)
                    if (level, what) == (k, kind) and 0 <= at < n:
                        send[side][:, lane] = mat[at][off : off + ny]
            for i in range(0 if kind == "s" else -1, own + 1):
                if not 0 <= o + i < n:
                    continue
                arr, lane = place[k, kind, i]
                ana[arr][:, lane] = mat[o + i][off : off + ny]
                unit = np.zeros((n, 1))
                unit[o + i] = 1.0
                zero = np.zeros_like(unit)
                back = unlift_np(unit, zero) if kind == "s" else unlift_np(zero, unit)
                for _ in range(k - 1):
                    back = unlift_np(back, np.zeros_like(back))
                syn[arr][lane] = back[off : off + ny, 0]
    return ana, syn, send


@lru_cache(None)
def y_received(ny):
    place, _ = lane_plan(ny)
    base = {"m1": 0, "m2": ny, "c": ny + ny // 2}
    mat = np.zeros((2 * SLOT, base["c"] + TILE))

    def put(row, k, kind, i, value):
        arr, lane = place[k, kind, i]
        mat[row, base[arr] + lane] += value

    for row, (k, kind, i) in enumerate(edge_lanes(1)):
        put(row, k, kind, i, 1.0)
        if kind == "d" and i == (-1 if k == 1 else 0):
            put(row, k, "s", i + 1, 0.25)
    for row, (k, kind, i) in enumerate(edge_lanes(-1)):
        n = ny >> k
        put(SLOT + row, k, kind, n + i, 1.0)
        if kind == "d" and i == -1:
            put(SLOT + row, k, "s", n - 1, 0.25)
    groups = TILE // SLOT
    return np.concatenate([np.tile(mat[:SLOT], (groups, 1)), np.tile(mat[SLOT:], (groups, 1))], 0)


def split_np(mat):
    hi = mat.astype(np.float32).astype(jnp.bfloat16)
    lo = (mat - hi.astype(np.float64)).astype(np.float32).astype(jnp.bfloat16)
    return hi, lo


@lru_cache(None)
def y_constants(ny, count):
    if count == 1:
        kinds = [(False, False)]
    else:
        kinds = [(False, True), (True, True), (True, False)]
    main, main_lo, e_hi, e_lo, back = [], [], [], [], []
    for below, above in kinds:
        ana, syn, send = y_matrices(ny, below, above)
        hi, lo = split_np(np.concatenate([ana["m1"], ana["m2"], ana["c"]], 1))
        assert not np.any(lo[:, : ny + ny // 2].astype(np.float32))
        main.append(hi)
        main_lo.append(lo[:, ny + ny // 2 :])
        edge = np.tile(np.concatenate([send[1], send[-1]], 1), (1, TILE // (2 * SLOT)))
        assert not np.any(edge[REACH : ny - REACH])
        hi, lo = split_np(np.concatenate([edge[:REACH], edge[ny - REACH :]], 0))
        e_hi.append(hi)
        e_lo.append(lo)
        hi, lo = split_np(np.concatenate([syn["m1"], syn["m2"], syn["c"]], 0))
        assert not np.any(lo.astype(np.float32))
        back.append(hi)
    return *(np.stack(t) for t in (main, main_lo, e_hi, e_lo, back)), split_np(y_received(ny))[0]


def split(value):
    hi = value.astype(BF)
    return hi, (value - hi.astype(F32)).astype(BF)


def dot(a, b):
    return jnp.dot(a, b, preferred_element_type=F32)


def lanes():
    return lax.broadcasted_iota(jnp.int32, (1, TILE), 1)


def in_span(span):
    lane = lanes()
    return (lane >= span[0]) & (lane < span[1])


def device_place(gx, gy):
    ix, iy = lax.axis_index("gx"), lax.axis_index("gy")
    edge = jnp.where(ix > 0, 1.0, 0.0), jnp.where(ix < gx - 1, 1.0, 0.0)
    kind = jnp.where(iy == 0, 0, jnp.where(iy == gy - 1, 2, 1)) if gy > 1 else 0
    return edge, (kind, lax.rem(iy, 2), lax.rem(ix, 2), lax.rem(ix // 2, 2))


def first_kernel(nx, edge_ref, var_ref, x_ref, ehi_ref, elo_ref, a_ref,
                 xhl, one_ref, two_ref, rows_ref, xt, e3, a2, ends, low, high, sems):
    g, ny = xt.shape[1], xt.shape[3]
    consts = [
        pltpu.make_async_copy(ref.at[var_ref[0]], e3.at[pl.ds(j * TILE, TILE)], sems.at[nx + j])
        for j, ref in ((0, ehi_ref), (2, elo_ref))
    ]
    late = pltpu.make_async_copy(a_ref.at[var_ref[0], :, pl.ds(0, ny)], a2.at[pl.ds(0, ny)], sems.at[nx + 3])
    per = TILE // SLOT
    copies = [
        pltpu.make_async_copy(x_ref.at[:, pl.ds(r, per)], xt.at[r // per], sems.at[r // per])
        for r in range(0, nx, per)
    ]
    for copy in copies[:1] + consts + copies[1:] + [late]:
        copy.start()
    odd = var_ref[1] == 1
    low_half = lanes() < REACH

    def edges(r):
        up = down = None
        for q in range(r, r + per, 4):
            res = dot(ends[q * g : (q + 4) * g], e3[...])
            for i in range(q, q + 4):
                plain = res[(i - q) * g : (i - q + 1) * g]
                turned = pltpu.roll(plain, SLOT, 1)
                group = lanes() // SLOT == i - r
                a, b = (plain, turned) if i % 2 == 0 else (turned, plain)
                up = jnp.where(group, a, 0.0 if up is None else up)
                down = jnp.where(group, b, 0.0 if down is None else down)
        one_ref[r // per] = jnp.where(odd, down, up)
        two_ref[r // per] = jnp.where(odd, up, down)

    for r in range(0, nx, per):
        copies[r // per].wait()
        if r == per:
            for copy in consts:
                copy.wait()
            e3[TILE : 2 * TILE] = e3[0:TILE]
        block = jnp.swapaxes(xt[r // per], 0, 1)
        for i in range(r, r + per):
            rows = slice(i * g, (i + 1) * g)
            hi, lo = split(block[i - r])
            xhl[rows, 0:ny], xhl[rows, ny : 2 * ny] = hi, lo
            hi, lo = (jnp.where(low_half, t[:, 0:TILE], t[:, ny - TILE :]) for t in (hi, lo))
            ends[rows, 0:TILE], ends[rows, TILE : 2 * TILE], ends[rows, 2 * TILE :] = hi, lo, hi
    for r in range(0, nx, per):
        edges(r)
    late.wait()
    a2[ny : 2 * ny] = a2[0:ny]
    count, top = low.shape[0], nx - high.shape[0]
    low[...] = dot(xhl[0 : count * g, 0 : 2 * ny], a2[...]).reshape(low.shape)
    high[...] = dot(xhl[top * g :, 0 : 2 * ny], a2[...]).reshape(high.shape)
    lift = Lift(nx, lambda i: low[i], edge_ref, 0, count - 1)
    begin, then = lift.detail(1, -1), lift.detail(1, 0)
    last = Lift(nx, lambda i: high[i - top], edge_ref, top, nx - 1).detail(1, (nx >> 1) - 1)
    for t, value in enumerate((last, begin, then)):
        rows_ref[2 * t], rows_ref[2 * t + 1] = value[:, 0:TILE], value[:, TILE:]


def main_kernel(nx, edge_ref, var_ref, xhl, a_ref, lo_ref, y_ref, a2):
    g, ny = y_ref.shape[1], a_ref.shape[1]
    a2[0:ny], a2[ny : 2 * ny] = a_ref[var_ref[0]], a_ref[var_ref[0]]
    step = 4
    for r in range(0, nx, step):
        res = dot(xhl[r * g : (r + step) * g, 0 : 2 * ny], a2[...])
        more = dot(xhl[r * g : (r + step) * g, 0:ny], lo_ref[var_ref[0]])
        at = y_ref.shape[2] - TILE
        y_ref[r : r + step, :, 0:at] = res[:, 0:at].reshape(step, g, at)
        y_ref[r : r + step, :, at:] = (res[:, at:] + more).reshape(step, g, TILE)


def relay_kernel(edge_ref, var_ref, rows_ref, up_ref, down_ref, one_ref, two_ref):
    up, down = [up_ref[...]], [down_ref[...]]
    zero = jnp.zeros(up_ref.shape, F32)
    up += [rows_ref[0], rows_ref[1], zero, zero]
    down += [rows_ref[t] for t in range(2, 6)]
    to_pairs(var_ref[3], up, down, one_ref, two_ref)


def to_pairs(odd, up, down, one_ref, two_ref):
    for t, (a, b) in enumerate(zip(up, down)):
        one_ref[t] = jnp.where(odd == 1, b, a)
        two_ref[t] = jnp.where(odd == 1, a, b)


def from_pairs(odd, one_ref, two_ref):
    count = one_ref.shape[0]
    below = [jnp.where(odd == 1, one_ref[t], two_ref[t]) for t in range(count)]
    above = [jnp.where(odd == 1, two_ref[t], one_ref[t]) for t in range(count)]
    return below, above


class Lift:
    def __init__(self, nx, raw, edge_ref, first=0, last=None):
        self.nx, self.raw = nx, raw
        self.first, self.last = first, nx - 1 if last is None else last
        self.not_first, self.not_last = edge_ref[0], edge_ref[1]
        self.known = {}

    def smooth(self, k, i):
        if k == 0:
            if not 0 <= i < self.nx:
                return None
            assert self.first <= i <= self.last
        if (k, "s", i) not in self.known:
            self.known[k, "s", i] = self.raw(i) if k == 0 else self.new_smooth(k, i)
        return self.known[k, "s", i]

    def detail(self, k, i):
        if (k, "d", i) not in self.known:
            self.known[k, "d", i] = self.new_detail(k, i)
        return self.known[k, "d", i]

    def new_detail(self, k, i):
        if not -1 <= i <= self.nx >> k:
            return None
        even, mid, after = (self.smooth(k - 1, j) for j in (2 * i, 2 * i + 1, 2 * i + 2))
        pair = plus(even, after)
        if pair is None:
            return mid
        out = -0.5 * pair if mid is None else mid - 0.5 * pair
        return out * self.not_first if i < 0 else out

    def new_smooth(self, k, i):
        if not -1 <= i <= (self.nx >> k) + 1:
            return None
        even = self.smooth(k - 1, 2 * i)
        pair = plus(self.detail(k, i - 1), self.detail(k, i))
        if pair is None:
            return even if even is None or i < self.nx >> k else even * self.not_last
        out = 0.25 * pair if even is None else even + 0.25 * pair
        return out * self.not_last if i >= self.nx >> k else out


def plus(a, b):
    return b if a is None else a if b is None else a + b


def c_slots(lift, spans, kind, low, high, s_lanes):
    out = []
    for i in range(low, high + 1):
        tile = None
        for k in range(1, LEVELS + 1):
            if i > lift.nx >> k:
                continue
            value = lift.detail(k, i) if kind == "d" else lift.smooth(k, i)
            if value is None:
                continue
            tile = jnp.where(in_span(spans[k]), value, 0.0 if tile is None else tile)
        out.append(jnp.where(s_lanes, tile, 0.0) if kind == "s" else tile)
    return out


def smooth_lanes(spans):
    ok = in_span(spans[LEVELS])
    for k in range(1, LEVELS):
        ok = ok | in_span(spans[k, "d"])
    return ok


def send_kernel(nx, far, edge_ref, var_ref, ym_ref, one_ref, two_ref, p_ref, *rest):
    to_one_ref, to_two_ref, cc_ref, z, y2_ref = rest[:5]
    far_up_ref, far_down_ref, yc, yl, yh, p2 = rest[5:]
    g = yc.shape[1]
    mains = ym_ref.shape[2] - TILE
    ny = mains - TILE
    _, spans = lane_plan(ny)
    n1, n2 = nx >> 1, nx >> 2
    n = 2 * TILE
    p2[0:n], p2[n : 2 * n] = p_ref[...], p_ref[...]
    per = TILE // SLOT
    group = lanes() // SLOT
    zero = jnp.zeros((g, TILE), BF)
    odd = var_ref[1] == 1
    for t in range(nx // per):
        from_below = jnp.where(odd, one_ref[t], two_ref[t])
        from_above = jnp.where(odd, two_ref[t], one_ref[t])
        pieces = split(from_below) + split(from_above)
        for i in range(per):
            here = group == i
            rows = slice((t * per + i) * g, (t * per + i + 1) * g)
            for c, j in enumerate((0, 2, 1, 3)):
                z[rows, c * TILE : (c + 1) * TILE] = jnp.where(here, pieces[j], zero)
    step = 4
    for r in range(0, nx, step):
        res = dot(z[r * g : (r + step) * g], p2[:, ny : mains + TILE])
        y2_ref[r : r + step] = ym_ref[r : r + step, :, ny:mains] + res[:, 0:TILE].reshape(step, g, TILE)
        yc[r : r + step] = ym_ref[r : r + step, :, mains:] + res[:, TILE:].reshape(step, g, TILE)
    low, high = yl.shape[0], yh.shape[0]
    yl[...] = dot(z[0 : low * g], p2[:, 0:TILE]).reshape(yl.shape)
    yh[...] = dot(z[(nx - high) * g :], p2[:, 0:TILE]).reshape(yh.shape)

    def lift(ref, base):
        return Lift(nx, lambda i: ref[i - base], edge_ref, base, base + ref.shape[0] - 1)

    second = Lift(nx, lambda i: y2_ref[i], edge_ref)
    one, two = lift(yl, 0), lift(yh, nx - high)
    fix_up = [two.detail(1, n1 - 1)]
    fix_down = [one.detail(1, -1), one.detail(1, 0)]
    up = [second.detail(2, n2 - 1), second.detail(2, n2), put_fixes(second.smooth(2, n2), fix_up)]
    down = [second.detail(2, -1), second.detail(2, 0), put_fixes(second.smooth(2, 0), fix_down)]

    s_lanes = smooth_lanes(spans)
    deep = Lift(nx, lambda i: yc[i], edge_ref)
    for j, tile in enumerate(c_slots(deep, spans, "d", -1, n1 - 1, s_lanes)):
        cc_ref[j] = tile
    for j, tile in enumerate(c_slots(deep, spans, "s", 0, n1, s_lanes)):
        cc_ref[n1 + 1 + j] = tile
    acc = [jnp.zeros((g, TILE), F32)] * 3
    for k in range(1, LEVELS + 1):
        n, here = nx >> k, in_span(spans[k])
        new = [deep.detail(k, n - 1)] + ([deep.detail(k, n), deep.smooth(k, n)] if k > 1 else [None] * 2)
        acc = [a if v is None else jnp.where(here, v, a) for a, v in zip(acc, new)]
    to_pairs(var_ref[2], up + acc, down + [cc_ref[0], cc_ref[1], cc_ref[n1 + 1]], to_one_ref, to_two_ref)
    here = in_span(spans[LEVELS]) if far else lanes() < 0
    far_up_ref[...] = jnp.where(here, deep.detail(LEVELS, nx >> LEVELS), 0.0)
    far_down_ref[...] = jnp.where(here, deep.detail(LEVELS, -1), 0.0)


def put_fixes(tile, fixes):
    lane = lanes()
    for j, fix in enumerate(fixes):
        tile = jnp.where((lane >> 1) == j, pltpu.roll(fix, 1 + 2 * j, 1), tile)
    return tile


def get_fix(tile, j):
    lane = lanes()
    turned = pltpu.roll(tile, TILE - 1 - 2 * j, 1)
    a = jnp.where((lane == 0) | (lane == TILE - 1), turned, 0.0)
    return a, jnp.where(lane == TILE - 1, 4.0 * turned, 0.0)


def weigh(r_ref, bands, value):
    m = r_ref.shape[1]
    vectors = value.shape[0] // m
    hi, lo = split(value)
    out = [[] for _ in bands]
    mats = [r_ref[b] for b in bands]
    mat = mats[0] if len(mats) == 1 else jnp.concatenate(mats, 0)
    for v in range(vectors):
        part = slice(v * m, (v + 1) * m)
        rhs = jnp.concatenate([hi[part], hi[part], lo[part]], 0)
        res = dot(mat, rhs)
        for j in range(len(bands)):
            out[j].append(res[j * m : (j + 1) * m])
    return [jnp.concatenate(o, 0) for o in out]


def band_of(k, kind, y_kind):
    if kind == "s":
        return 3 * LEVELS if y_kind == "s" else 3 * (k - 1)
    return 3 * (k - 1) + (1 if y_kind == "s" else 2)


def weigh_c(r_ref, spans, kind, levels, tiles):
    which = [
        (k, y_kind)
        for k in levels
        for y_kind in ("s", "d")
        if kind == "d" or y_kind == "d" or k == LEVELS
    ]
    value = jnp.concatenate(tiles, 1) if len(tiles) > 1 else tiles[0]
    res = weigh(r_ref, [band_of(k, kind, y_kind) for k, y_kind in which], value)
    outs = []
    for t in range(len(tiles)):
        out = jnp.zeros_like(tiles[t])
        for (k, y_kind), r in zip(which, res):
            out = jnp.where(in_span(spans[k, y_kind]), r[:, t * TILE : (t + 1) * TILE], out)
        outs.append(out)
    return outs


def weigh_m2(r_ref, kind, tiles):
    lane_d = lanes() >= TILE // 2
    value = jnp.concatenate(tiles, 1) if len(tiles) > 1 else tiles[0]
    if kind == "s":
        res = [None, weigh(r_ref, [band_of(2, "s", "d")], value)[0]]
    else:
        res = weigh(r_ref, [band_of(2, "d", "s"), band_of(2, "d", "d")], value)
    outs = []
    for t in range(len(tiles)):
        a, b = (0.0 if r is None else r[:, t * TILE : (t + 1) * TILE] for r in res)
        outs.append(jnp.where(lane_d, b, a))
    return outs


def weigh_tiles(r_ref, band, tiles):
    value = jnp.concatenate(tiles, 1) if len(tiles) > 1 else tiles[0]
    res = weigh(r_ref, [band], value)[0]
    return [res[:, t * TILE : (t + 1) * TILE] for t in range(len(tiles))]


def groups(low, high, size):
    return [list(range(i, min(i + size, high + 1))) for i in range(low, high + 1, size)]


def weighted_plan(nx):
    n2 = nx >> 2
    plan, at = {}, 0
    for name, count in ((("m2", "d"), n2 + 2), (("m2", "s"), n2 + 1), (("c", "d"), n2 + 2), (("c", "s"), n2 + 1)):
        plan[name] = at
        at += count
    return plan, at


def pairs_into(ref, row, g, tiles):
    rows, width = slice(row * g, (row + 1) * g), len(tiles) * TILE
    for t, tile in enumerate(tiles):
        if tile is None:
            continue
        cols = slice(t * TILE, (t + 1) * TILE)
        ref[rows, cols], ref[rows, width + t * TILE : width + (t + 1) * TILE] = split(tile)


def stack_back(s_ref, which, out, spans_of_rows):
    at = 0
    for a, b in spans_of_rows * 2:
        out[at : at + b - a] = s_ref[which, a:b]
        at += b - a


def first_level_rows(ny):
    half, c = ny // 2, (ny + ny // 2, ny + ny // 2 + TILE)
    return [(0, ny), c], [(half, ny), c]


def local_kernel(nx, edge_ref, var_ref, ym_ref, z, y2_ref, cc_ref, p_ref, s_ref, r_ref,
                 vd_ref, vs_ref, w_ref, y, p2, zd, zs, sd, ss):
    g, ny = y.shape[1], y.shape[2]
    _, spans = lane_plan(ny)
    n1, n2 = nx >> 1, nx >> 2
    plan, _ = weighted_plan(nx)
    n = 2 * TILE
    p2[0:n], p2[n : 2 * n] = p_ref[:, 0:ny], p_ref[:, 0:ny]
    rows_d, rows_s = first_level_rows(ny)
    stack_back(s_ref, var_ref[0], sd, rows_d)
    stack_back(s_ref, var_ref[0], ss, rows_s)
    step = 4
    for r in range(0, nx, step):
        res = dot(z[r * g : (r + step) * g], p2[...])
        y[r : r + step] = ym_ref[r : r + step, :, 0:ny] + res.reshape(step, g, ny)

    def lift(columns):
        return Lift(nx, lambda i: y[i, :, columns], edge_ref)

    a, b = (lift(slice(t * TILE, (t + 1) * TILE)) for t in range(2))
    m2 = Lift(nx, lambda i: y2_ref[i], edge_ref)

    def store(name, low, some, tiles):
        for i, tile in zip(some, tiles):
            w_ref[plan[name] + i - low] = tile

    here = in_span(spans[1])

    def weighed_c(kind, low, some):
        base = 0 if kind == "d" else n1 + 1
        out = {}
        by_levels = {}
        for i in some:
            by_levels.setdefault(tuple(k for k in range(1, LEVELS + 1) if i <= nx >> k), []).append(i)
        for levels, part in by_levels.items():
            tiles = weigh_c(r_ref, spans, kind, list(levels), [cc_ref[base + i - low] for i in part])
            for i, tile in zip(part, tiles):
                if i <= n2:
                    w_ref[plan["c", kind] + i - low] = tile
                out[i] = jnp.where(here, tile, 0.0) if i <= n2 else tile
        return [out[i] for i in some]

    for some in groups(-1, n1 - 1, 4):
        ta = weigh_tiles(r_ref, band_of(1, "d", "s"), [a.detail(1, i) for i in some])
        tb = weigh_tiles(r_ref, band_of(1, "d", "d"), [b.detail(1, i) for i in some])
        tc = weighed_c("d", -1, some)
        for i, tiles in zip(some, zip(ta, tb, tc)):
            pairs_into(zd, i + 1, g, tiles)
        first, count = some[0] + 1, len(some)
        vd_ref[first : first + count] = dot(zd[first * g : (first + count) * g], sd[...]).reshape(count, g, ny)
    for some in groups(0, n1, 4):
        tb = weigh_tiles(r_ref, band_of(1, "s", "d"), [b.smooth(1, i) for i in some])
        tc = weighed_c("s", 0, some)
        for i, tiles in zip(some, zip(tb, tc)):
            pairs_into(zs, i, g, tiles)
        first, count = some[0], len(some)
        vs_ref[first : first + count] = dot(zs[first * g : (first + count) * g], ss[...]).reshape(count, g, ny)
    for some in groups(-1, n2, 4):
        store(("m2", "d"), -1, some, weigh_m2(r_ref, "d", [m2.detail(2, i) for i in some]))
    for some in groups(0, n2, 4):
        store(("m2", "s"), 0, some, weigh_m2(r_ref, "s", [m2.smooth(2, i) for i in some]))


def final_kernel(nx, edge_ref, var_ref, vd_ref, vs_ref, w_ref, near, r_one, r_two, f_one, f_two,
                 s_ref, r_ref, out_ref, sd, ss, sdeep, zd, zs, zdeep, rows, ot, sem):
    g, ny = ot.shape[1], ot.shape[3]
    _, spans = lane_plan(ny)
    plan, _ = weighted_plan(nx)
    half = ny // 2
    n1, n2 = nx >> 1, nx >> 2
    rows_d, rows_s = first_level_rows(ny)
    stack_back(s_ref, var_ref[0], sd, rows_d)
    stack_back(s_ref, var_ref[0], ss, rows_s)
    stack_back(s_ref, var_ref[0], sdeep, [(ny, ny + half + TILE)])
    s_lanes = smooth_lanes(spans)
    lev1 = in_span(spans[1])

    def smooth_c(value):
        return jnp.where(s_lanes, 0.25 * value, 0.0)

    below, above = from_pairs(var_ref[2], r_one, r_two)
    far_below, far_above = from_pairs(var_ref[3], f_one, f_two)
    odd = var_ref[2] == 1
    first_below = [jnp.where(odd, near[t], far_below[1 + t]) for t in range(2)]
    first_above = [jnp.where(odd, far_above[1 + t], near[2 + t]) for t in range(4)]
    c_d = {-1: below[3], 0: below[4], "n-1": above[3], "n": above[4]}
    c_s = {
        0: below[5] + jnp.where(lev1, smooth_c(c_d[-1]), 0.0),
        1: smooth_c(c_d[0]),
        "n-1": smooth_c(c_d["n-1"]),
        "n": above[5],
    }
    c_d[-1] = c_d[-1] + far_below[0]
    c_s[0] = c_s[0] + smooth_c(far_below[0])
    c_d["n"] = c_d["n"] + far_above[0]
    c_s["n"] = c_s["n"] + smooth_c(far_above[0])
    fixes = [get_fix(below[2], 0)] + [get_fix(above[2], j) for j in range(2)]
    a_tiles = [first_below[0] + fixes[0][0], first_above[0] + fixes[1][0], first_above[2] + fixes[2][0]]
    b_tiles = [first_below[1] + fixes[0][1], first_above[1] + fixes[1][1], first_above[3] + fixes[2][1]]
    s_tiles = [0.25 * b_tiles[0], 0.25 * b_tiles[1], 0.25 * b_tiles[2] - 1.75 * b_tiles[1]]
    every = list(range(1, LEVELS + 1))
    got = {}

    def keep(name, keys, tiles):
        for key, tile in zip(keys, tiles):
            got[name, key] = tile

    for kind, tiles in (("d", c_d), ("s", c_s)):
        keep(("c", kind), list(tiles), weigh_c(r_ref, spans, kind, every, list(tiles.values())))
    keys = [-1, "n-1", "n"]
    ta = weigh_tiles(r_ref, band_of(1, "d", "s"), a_tiles)
    tb = weigh_tiles(r_ref, band_of(1, "d", "d"), b_tiles)
    for j, key in enumerate(keys):
        pairs_into(zd, j, g, [ta[j], tb[j], jnp.where(lev1, got[("c", "d"), key], 0.0)])
    more_d = dot(zd[...], sd[...])
    tb = weigh_tiles(r_ref, band_of(1, "s", "d"), s_tiles)
    for j, key in enumerate([0, "n-1", "n"]):
        pairs_into(zs, j, g, [tb[j], jnp.where(lev1, got[("c", "s"), key], 0.0)])
    more_s = dot(zs[...], ss[...])
    keep(("m2", "d"), [-1, 0, "n-1", "n"], weigh_m2(r_ref, "d", [below[0], below[1], above[0], above[1]]))
    keep(("m2", "s"), [0, 1, "n-1", "n"],
         weigh_m2(r_ref, "s", [below[2], 0.25 * below[1], 0.25 * above[0], above[2]]))

    def value_of(array, kind, k, i):
        n, low = nx >> k, -1 if kind == "d" else 0
        v = w_ref[plan[array, kind] + i - low]
        for key, at in ((-1, -1), (0, 0), (1, 1), ("n-1", n - 1), ("n", n)):
            if at == i and ((array, kind), key) in got:
                v = v + got[(array, kind), key]
        return jnp.where(in_span(spans[k]), v, 0.0) if array == "c" else v

    not_last = edge_ref[1]

    def unlift(n, smooth, detail, emit):
        below, before = detail(-1), None
        for i in range(n + 1):
            here = detail(i)
            even = smooth(i) - 0.25 * (below + here)
            if i == n:
                even = even * not_last
            if i > 0:
                emit(2 * i - 1, below + 0.5 * (before + even))
            emit(2 * i, even)
            below, before = here, even

    for k in range(LEVELS, 1, -1):
        base = level_base(nx, k)

        def smooth_deep(i, k=k, base=base):
            v = value_of("c", "s", k, i)
            return v if k == LEVELS else v + rows[base + i]

        if k > 2:
            def emit(i, value, base=level_base(nx, k - 1)):
                rows[base + i] = value
        else:
            def emit(i, value):
                r = slice(i * g, (i + 1) * g)
                zdeep[r, TILE : 2 * TILE], zdeep[r, 3 * TILE : 4 * TILE] = split(value)

        unlift(nx >> k, smooth_deep, lambda i, k=k: value_of("c", "d", k, i), emit)

    def emit_m2(i, value):
        r = slice(i * g, (i + 1) * g)
        zdeep[r, 0:TILE], zdeep[r, 2 * TILE : 3 * TILE] = split(value)

    unlift(n2, lambda i: value_of("m2", "s", 2, i), lambda i: value_of("m2", "d", 2, i), emit_m2)

    extra_d = {-1: more_d[0:g], n1 - 1: more_d[g : 2 * g], n1: more_d[2 * g :]}
    extra_s = {0: more_s[0:g], n1 - 1: more_s[g : 2 * g], n1: more_s[2 * g :]}
    step = 4
    deep = {}

    def smooth_first(i):
        if i % step == 0:
            count = min(step, n1 + 1 - i)
            res = dot(zdeep[i * g : (i + count) * g], sdeep[...])
            for j in range(count):
                deep[i + j] = res[j * g : (j + 1) * g]
        v = deep[i] + vs_ref[i]
        return v + extra_s[i] if i in extra_s else v

    def detail_first(i):
        if i == n1:
            return extra_d[i]
        v = vd_ref[i + 1]
        return v + extra_d[i] if i in extra_d else v

    copies = []

    pending = {}

    def emit_out(i, value):
        if i >= nx:
            return
        pending[i] = value
        r = i - i % 8
        if all(j in pending for j in range(r, r + 8)):
            block = jnp.stack([pending.pop(j) for j in range(r, r + 8)], 0)
            ot[r // 8] = jnp.swapaxes(block, 0, 1)
            copies.append(pltpu.make_async_copy(ot.at[r // 8], out_ref.at[:, pl.ds(r, 8)], sem.at[r // 8]))
            copies[-1].start()

    unlift(n1, smooth_first, detail_first, emit_out)
    for copy in copies:
        copy.wait()


def level_base(nx, k):
    return sum((nx >> j) + 1 for j in range(max(k + 1, 3), LEVELS)) if k > 1 else 0


def swap(value, axis, first, step=1):
    count = lax.axis_size(axis)
    starts = [i for i in range(first, count - step) if (i - first) // step % 2 == 0]
    return lax.ppermute(value, axis, [p for i in starts for p in ((i, i + step), (i + step, i))])


def per_device(control, band_roots):
    vectors, m, nx, ny = control.shape
    g = vectors * m
    half = ny // 2
    gx, gy = lax.axis_size("gx"), lax.axis_size("gy")
    per = TILE // SLOT
    assert half == TILE and nx % (2 * per) == 0
    far = (nx >> LEVELS) < 2 and gx > 2
    consts = y_constants(ny, gy)
    main_mat, clo_mat, ehi_mat, elo_mat, s_mat, p_mat = (jnp.asarray(t) for t in consts)
    n1 = nx >> 1
    mains = ny + half

    r_hi = lax.reduce_precision(band_roots, 8, 7)
    r_lo = band_roots - r_hi
    roots = jnp.concatenate([r_hi.astype(BF), r_lo.astype(BF), r_hi.astype(BF)], 2)

    hbm = pl.BlockSpec(memory_space=pl.ANY)
    vmem = pl.BlockSpec(memory_space=pltpu.VMEM)

    def call(kernel, ins, outs, scratches, out_specs=None):
        def body(*refs):
            kernel(*device_place(gx, gy), *refs)

        return pl.pallas_call(
            body,
            out_shape=tuple(jax.ShapeDtypeStruct(*s) for s in outs),
            in_specs=[s for _, s in ins],
            out_specs=out_specs or (vmem,) * len(outs),
            scratch_shapes=scratches,
            compiler_params=pltpu.CompilerParams(vmem_limit_bytes=VMEM_LIMIT),
        )(*[a for a, _ in ins])

    tile = (g, TILE)
    rows3 = control.reshape(g, nx, ny)
    far_hbm = pl.BlockSpec(memory_space=pltpu.HBM)
    xhl, one, two, rows = call(
        partial(first_kernel, nx),
        [
            (pltpu.with_memory_space_constraint(t, pltpu.HBM), far_hbm)
            for t in (rows3, ehi_mat, elo_mat, main_mat)
        ],
        [((nx * g, 2 * ny), BF), ((nx // per,) + tile, F32), ((nx // per,) + tile, F32),
         ((6,) + tile, F32)],
        [pltpu.VMEM((nx // per, g, per, ny), F32), pltpu.VMEM((3 * TILE, TILE), BF),
         pltpu.VMEM((2 * ny, ny), BF), pltpu.VMEM((nx * g, 3 * TILE), BF), pltpu.VMEM((4, g, ny), F32), pltpu.VMEM((4, g, ny), F32),
         pltpu.SemaphoreType.DMA((nx + 4,))],
    )
    near = swap(rows, "gx", 0)
    got_one = swap(one, "gy", 0)
    got_two = swap(two, "gy", 1)
    (ym,) = call(
        partial(main_kernel, nx),
        [(xhl, vmem), (main_mat, vmem), (clo_mat, vmem)],
        [((nx, g, mains + TILE), F32)],
        [pltpu.VMEM((2 * ny, mains + TILE), BF)],
    )
    slots = 2 * n1 + 2
    sent = call(
        partial(send_kernel, nx, far),
        [(ym, vmem), (got_one, vmem), (got_two, vmem), (p_mat, vmem)],
        [((6,) + tile, F32), ((6,) + tile, F32), ((slots,) + tile, F32), ((nx * g, 4 * TILE), BF), ((nx,) + tile, F32)]
        + [(tile, F32)] * 2,
        [
            pltpu.VMEM((nx,) + tile, F32),
            pltpu.VMEM((4,) + tile, F32),
            pltpu.VMEM((4,) + tile, F32),
            pltpu.VMEM((4 * TILE, mains + TILE), BF),
        ],
    )
    got = [near, swap(sent[0], "gx", 0), swap(sent[1], "gx", 1)]
    far_one, far_two = call(relay_kernel, [(t, vmem) for t in (near, sent[5], sent[6])], [((5,) + tile, F32)] * 2, [])
    got += [swap(far_one, "gx", 0, 2), swap(far_two, "gx", 2, 2)]

    _, count = weighted_plan(nx)
    vd, vs, w = call(
        partial(local_kernel, nx),
        [(ym, vmem), (sent[3], vmem), (sent[4], vmem), (sent[2], vmem), (p_mat, vmem), (s_mat, vmem), (roots, vmem)],
        [((n1 + 1, g, ny), F32), ((n1 + 1, g, ny), F32), ((count,) + tile, F32)],
        [
            pltpu.VMEM((nx, g, ny), F32),
            pltpu.VMEM((4 * TILE, ny), BF),
            pltpu.VMEM(((n1 + 1) * g, 6 * TILE), BF),
            pltpu.VMEM(((n1 + 1) * g, 4 * TILE), BF),
            pltpu.VMEM((6 * TILE, ny), BF),
            pltpu.VMEM((4 * TILE, ny), BF),
        ],
    )
    (out,) = call(
        partial(final_kernel, nx),
        [(t, vmem) for t in [vd, vs, w] + got + [s_mat, roots]],
        [((g, nx, ny), F32)],
        [
            pltpu.VMEM((6 * TILE, ny), BF),
            pltpu.VMEM((4 * TILE, ny), BF),
            pltpu.VMEM((4 * TILE, ny), BF),
            pltpu.VMEM((3 * g, 6 * TILE), BF),
            pltpu.VMEM((3 * g, 4 * TILE), BF),
            pltpu.VMEM(((n1 + 1) * g, 4 * TILE), BF),
            pltpu.VMEM((level_base(nx, 1) + sum((nx >> j) + 1 for j in range(2, LEVELS)),) + tile, F32),
            pltpu.VMEM((nx // 8, g, 8, ny), F32),
            pltpu.SemaphoreType.DMA((nx // 8,)),
        ],
        (hbm,),
    )
    return out.reshape(control.shape)


def solution(mesh):
    spec = P(None, None, "gx", "gy")
    return jax.shard_map(per_device, mesh=mesh, in_specs=(spec, P()), out_specs=spec, check_vma=False)
```

```python
from functools import lru_cache, partial

import jax
import jax.numpy as jnp
import numpy as np
from jax import lax
from jax.experimental import pallas as pl
from jax.experimental.pallas import tpu as pltpu
from jax.sharding import PartitionSpec as P


LEVELS = 5
TILE = 128
VMEM_LIMIT = 28 * 2**20
BF = jnp.bfloat16
F32 = jnp.float32


def lift_np(signal):
    even, odd = signal[0::2], signal[1::2]
    zero = np.zeros_like(even[:1])
    detail = odd - 0.5 * (even + np.concatenate([even[1:], zero]))
    return even + 0.25 * (np.concatenate([zero, detail[:-1]]) + detail), detail


def unlift_np(smooth, detail):
    zero = np.zeros_like(smooth[:1])
    even = smooth - 0.25 * (np.concatenate([zero, detail[:-1]]) + detail)
    odd = detail + 0.5 * (even + np.concatenate([even[1:], zero]))
    return np.stack([even, odd], 1).reshape(2 * even.shape[0], -1)


def lane_plan(ny):
    place, lane = {}, 0
    spans = {}
    for k in list(range(3, LEVELS + 1)) + [1, 2]:
        n = ny >> k
        first = lane
        for kind, lo in (("s", 0), ("d", -1)):
            start = lane
            for i in range(lo, n + 1):
                if k <= 2 and 0 <= i < n:
                    place[k, kind, i] = (f"m{k}", i + (n if kind == "d" else 0))
                else:
                    place[k, kind, i] = ("c", lane)
                    lane += 1
            spans[k, kind] = (start, lane)
        spans[k] = (first, lane)
    assert lane <= TILE
    return place, spans


SLOT = 16
REACH = 64


def edge_lanes(side):
    out = []
    for k in range(1, LEVELS + 1):
        if side > 0:
            out += [(k, "d", -1)] + ([(k, "d", 0), (k, "s", 0)] if k > 1 else [])
        else:
            out += [(k, "d", -1), (k, "d", 0), (k, "s", 0)]
    assert len(out) <= SLOT
    return out


@lru_cache(None)
def y_matrices(ny, below, above):
    place, _ = lane_plan(ny)
    off = ny if below else 0
    size = off + ny + (ny if above else 0)
    width = {"m1": ny, "m2": ny // 2, "c": TILE}
    ana = {a: np.zeros((ny, w)) for a, w in width.items()}
    syn = {a: np.zeros((w, ny)) for a, w in width.items()}
    send = {side: np.zeros((ny, SLOT)) for side in (1, -1)}
    s = np.eye(size)
    for k in range(1, LEVELS + 1):
        s, d = lift_np(s)
        for kind, mat in (("s", s), ("d", d)):
            n, o, own = size >> k, off >> k, ny >> k
            for side in (1, -1):
                for lane, (level, what, i) in enumerate(edge_lanes(side)):
                    at = o + i + (own if side > 0 else 0)
                    if (level, what) == (k, kind) and 0 <= at < n:
                        send[side][:, lane] = mat[at][off : off + ny]
            for i in range(0 if kind == "s" else -1, own + 1):
                if not 0 <= o + i < n:
                    continue
                arr, lane = place[k, kind, i]
                ana[arr][:, lane] = mat[o + i][off : off + ny]
                unit = np.zeros((n, 1))
                unit[o + i] = 1.0
                zero = np.zeros_like(unit)
                back = unlift_np(unit, zero) if kind == "s" else unlift_np(zero, unit)
                for _ in range(k - 1):
                    back = unlift_np(back, np.zeros_like(back))
                syn[arr][lane] = back[off : off + ny, 0]
    return ana, syn, send


@lru_cache(None)
def y_received(ny):
    place, _ = lane_plan(ny)
    base = {"m1": 0, "m2": ny, "c": ny + ny // 2}
    mat = np.zeros((2 * SLOT, base["c"] + TILE))

    def put(row, k, kind, i, value):
        arr, lane = place[k, kind, i]
        mat[row, base[arr] + lane] += value

    for row, (k, kind, i) in enumerate(edge_lanes(1)):
        put(row, k, kind, i, 1.0)
        if kind == "d" and i == (-1 if k == 1 else 0):
            put(row, k, "s", i + 1, 0.25)
    for row, (k, kind, i) in enumerate(edge_lanes(-1)):
        n = ny >> k
        put(SLOT + row, k, kind, n + i, 1.0)
        if kind == "d" and i == -1:
            put(SLOT + row, k, "s", n - 1, 0.25)
    groups = TILE // SLOT
    return np.concatenate([np.tile(mat[:SLOT], (groups, 1)), np.tile(mat[SLOT:], (groups, 1))], 0)


def split_np(mat):
    hi = mat.astype(np.float32).astype(jnp.bfloat16)
    lo = (mat - hi.astype(np.float64)).astype(np.float32).astype(jnp.bfloat16)
    return hi, lo


@lru_cache(None)
def y_constants(ny, count):
    if count == 1:
        kinds = [(False, False)]
    else:
        kinds = [(False, True), (True, True), (True, False)]
    main, main_lo, e_hi, e_lo, back = [], [], [], [], []
    for below, above in kinds:
        ana, syn, send = y_matrices(ny, below, above)
        hi, lo = split_np(np.concatenate([ana["m1"], ana["m2"], ana["c"]], 1))
        assert not np.any(lo[:, : ny + ny // 2].astype(np.float32))
        main.append(hi)
        main_lo.append(lo[:, ny + ny // 2 :])
        edge = np.tile(np.concatenate([send[1], send[-1]], 1), (1, TILE // (2 * SLOT)))
        assert not np.any(edge[REACH : ny - REACH])
        hi, lo = split_np(np.concatenate([edge[:REACH], edge[ny - REACH :]], 0))
        e_hi.append(hi)
        e_lo.append(lo)
        hi, lo = split_np(np.concatenate([syn["m1"], syn["m2"], syn["c"]], 0))
        assert not np.any(lo.astype(np.float32))
        back.append(hi)
    return *(np.stack(t) for t in (main, main_lo, e_hi, e_lo, back)), split_np(y_received(ny))[0]


def split(value):
    hi = value.astype(BF)
    return hi, (value - hi.astype(F32)).astype(BF)


def dot(a, b):
    return jnp.dot(a, b, preferred_element_type=F32)


def lanes():
    return lax.broadcasted_iota(jnp.int32, (1, TILE), 1)


def in_span(span):
    lane = lanes()
    return (lane >= span[0]) & (lane < span[1])


def device_place(gx, gy):
    ix, iy = lax.axis_index("gx"), lax.axis_index("gy")
    edge = jnp.where(ix > 0, 1.0, 0.0), jnp.where(ix < gx - 1, 1.0, 0.0)
    kind = jnp.where(iy == 0, 0, jnp.where(iy == gy - 1, 2, 1)) if gy > 1 else 0
    return edge, (kind, lax.rem(iy, 2), lax.rem(ix, 2), lax.rem(ix // 2, 2))


def first_kernel(nx, edge_ref, var_ref, x_ref, ehi_ref, elo_ref, a_ref,
                 xhl, one_ref, two_ref, rows_ref, xt, e3, a2, ends, low, high, sems):
    g, ny = xt.shape[1], xt.shape[3]
    consts = [
        pltpu.make_async_copy(ref.at[var_ref[0]], e3.at[pl.ds(j * TILE, TILE)], sems.at[nx + j])
        for j, ref in ((0, ehi_ref), (2, elo_ref))
    ]
    late = pltpu.make_async_copy(a_ref.at[var_ref[0], :, pl.ds(0, ny)], a2.at[pl.ds(0, ny)], sems.at[nx + 3])
    per = TILE // SLOT
    copies = [
        pltpu.make_async_copy(x_ref.at[:, pl.ds(r, per)], xt.at[r // per], sems.at[r // per])
        for r in range(0, nx, per)
    ]
    for copy in copies[:1] + consts + copies[1:] + [late]:
        copy.start()
    odd = var_ref[1] == 1
    low_half = lanes() < REACH

    def edges(r):
        up = down = None
        for q in range(r, r + per, 4):
            res = dot(ends[q * g : (q + 4) * g], e3[...])
            for i in range(q, q + 4):
                plain = res[(i - q) * g : (i - q + 1) * g]
                turned = pltpu.roll(plain, SLOT, 1)
                group = lanes() // SLOT == i - r
                a, b = (plain, turned) if i % 2 == 0 else (turned, plain)
                up = jnp.where(group, a, 0.0 if up is None else up)
                down = jnp.where(group, b, 0.0 if down is None else down)
        one_ref[r // per] = jnp.where(odd, down, up)
        two_ref[r // per] = jnp.where(odd, up, down)

    for r in range(0, nx, per):
        copies[r // per].wait()
        if r == per:
            for copy in consts:
                copy.wait()
            e3[TILE : 2 * TILE] = e3[0:TILE]
        block = jnp.swapaxes(xt[r // per], 0, 1)
        for i in range(r, r + per):
            rows = slice(i * g, (i + 1) * g)
            hi, lo = split(block[i - r])
            xhl[rows, 0:ny], xhl[rows, ny : 2 * ny] = hi, lo
            hi, lo = (jnp.where(low_half, t[:, 0:TILE], t[:, ny - TILE :]) for t in (hi, lo))
            ends[rows, 0:TILE], ends[rows, TILE : 2 * TILE], ends[rows, 2 * TILE :] = hi, lo, hi
    for r in range(0, nx, per):
        edges(r)
    late.wait()
    a2[ny : 2 * ny] = a2[0:ny]
    count, top = low.shape[0], nx - high.shape[0]
    low[...] = dot(xhl[0 : count * g, 0 : 2 * ny], a2[...]).reshape(low.shape)
    high[...] = dot(xhl[top * g :, 0 : 2 * ny], a2[...]).reshape(high.shape)
    lift = Lift(nx, lambda i: low[i], edge_ref, 0, count - 1)
    begin, then = lift.detail(1, -1), lift.detail(1, 0)
    last = Lift(nx, lambda i: high[i - top], edge_ref, top, nx - 1).detail(1, (nx >> 1) - 1)
    for t, value in enumerate((last, begin, then)):
        rows_ref[2 * t], rows_ref[2 * t + 1] = value[:, 0:TILE], value[:, TILE:]


def main_kernel(nx, edge_ref, var_ref, xhl, a_ref, lo_ref, y_ref, a2):
    g, ny = y_ref.shape[1], a_ref.shape[1]
    a2[0:ny], a2[ny : 2 * ny] = a_ref[var_ref[0]], a_ref[var_ref[0]]
    step = 4
    for r in range(0, nx, step):
        res = dot(xhl[r * g : (r + step) * g, 0 : 2 * ny], a2[...])
        more = dot(xhl[r * g : (r + step) * g, 0:ny], lo_ref[var_ref[0]])
        at = y_ref.shape[2] - TILE
        y_ref[r : r + step, :, 0:at] = res[:, 0:at].reshape(step, g, at)
        y_ref[r : r + step, :, at:] = (res[:, at:] + more).reshape(step, g, TILE)


def relay_kernel(edge_ref, var_ref, rows_ref, up_ref, down_ref, one_ref, two_ref):
    up, down = [up_ref[...]], [down_ref[...]]
    zero = jnp.zeros(up_ref.shape, F32)
    up += [rows_ref[0], rows_ref[1], zero, zero]
    down += [rows_ref[t] for t in range(2, 6)]
    to_pairs(var_ref[3], up, down, one_ref, two_ref)


def to_pairs(odd, up, down, one_ref, two_ref):
    for t, (a, b) in enumerate(zip(up, down)):
        one_ref[t] = jnp.where(odd == 1, b, a)
        two_ref[t] = jnp.where(odd == 1, a, b)


def from_pairs(odd, one_ref, two_ref):
    count = one_ref.shape[0]
    below = [jnp.where(odd == 1, one_ref[t], two_ref[t]) for t in range(count)]
    above = [jnp.where(odd == 1, two_ref[t], one_ref[t]) for t in range(count)]
    return below, above


class Lift:
    def __init__(self, nx, raw, edge_ref, first=0, last=None):
        self.nx, self.raw = nx, raw
        self.first, self.last = first, nx - 1 if last is None else last
        self.not_first, self.not_last = edge_ref[0], edge_ref[1]
        self.known = {}

    def smooth(self, k, i):
        if k == 0:
            if not 0 <= i < self.nx:
                return None
            assert self.first <= i <= self.last
        if (k, "s", i) not in self.known:
            self.known[k, "s", i] = self.raw(i) if k == 0 else self.new_smooth(k, i)
        return self.known[k, "s", i]

    def detail(self, k, i):
        if (k, "d", i) not in self.known:
            self.known[k, "d", i] = self.new_detail(k, i)
        return self.known[k, "d", i]

    def new_detail(self, k, i):
        if not -1 <= i <= self.nx >> k:
            return None
        even, mid, after = (self.smooth(k - 1, j) for j in (2 * i, 2 * i + 1, 2 * i + 2))
        pair = plus(even, after)
        if pair is None:
            return mid
        out = -0.5 * pair if mid is None else mid - 0.5 * pair
        return out * self.not_first if i < 0 else out

    def new_smooth(self, k, i):
        if not -1 <= i <= (self.nx >> k) + 1:
            return None
        even = self.smooth(k - 1, 2 * i)
        pair = plus(self.detail(k, i - 1), self.detail(k, i))
        if pair is None:
            return even if even is None or i < self.nx >> k else even * self.not_last
        out = 0.25 * pair if even is None else even + 0.25 * pair
        return out * self.not_last if i >= self.nx >> k else out


def plus(a, b):
    return b if a is None else a if b is None else a + b


def c_slots(lift, spans, kind, low, high, s_lanes):
    out = []
    for i in range(low, high + 1):
        tile = None
        for k in range(1, LEVELS + 1):
            if i > lift.nx >> k:
                continue
            value = lift.detail(k, i) if kind == "d" else lift.smooth(k, i)
            if value is None:
                continue
            tile = jnp.where(in_span(spans[k]), value, 0.0 if tile is None else tile)
        out.append(jnp.where(s_lanes, tile, 0.0) if kind == "s" else tile)
    return out


def smooth_lanes(spans):
    ok = in_span(spans[LEVELS])
    for k in range(1, LEVELS):
        ok = ok | in_span(spans[k, "d"])
    return ok


def send_kernel(nx, far, edge_ref, var_ref, ym_ref, one_ref, two_ref, p_ref, *rest):
    to_one_ref, to_two_ref, cc_ref, z, y2_ref = rest[:5]
    far_up_ref, far_down_ref, yc, yl, yh, p2 = rest[5:]
    g = yc.shape[1]
    mains = ym_ref.shape[2] - TILE
    ny = mains - TILE
    _, spans = lane_plan(ny)
    n1, n2 = nx >> 1, nx >> 2
    n = 2 * TILE
    p2[0:n], p2[n : 2 * n] = p_ref[...], p_ref[...]
    per = TILE // SLOT
    group = lanes() // SLOT
    zero = jnp.zeros((g, TILE), BF)
    odd = var_ref[1] == 1
    for t in range(nx // per):
        from_below = jnp.where(odd, one_ref[t], two_ref[t])
        from_above = jnp.where(odd, two_ref[t], one_ref[t])
        pieces = split(from_below) + split(from_above)
        for i in range(per):
            here = group == i
            rows = slice((t * per + i) * g, (t * per + i + 1) * g)
            for c, j in enumerate((0, 2, 1, 3)):
                z[rows, c * TILE : (c + 1) * TILE] = jnp.where(here, pieces[j], zero)
    step = 4
    for r in range(0, nx, step):
        res = dot(z[r * g : (r + step) * g], p2[:, ny : mains + TILE])
        y2_ref[r : r + step] = ym_ref[r : r + step, :, ny:mains] + res[:, 0:TILE].reshape(step, g, TILE)
        yc[r : r + step] = ym_ref[r : r + step, :, mains:] + res[:, TILE:].reshape(step, g, TILE)
    low, high = yl.shape[0], yh.shape[0]
    yl[...] = dot(z[0 : low * g], p2[:, 0:TILE]).reshape(yl.shape)
    yh[...] = dot(z[(nx - high) * g :], p2[:, 0:TILE]).reshape(yh.shape)

    def lift(ref, base):
        return Lift(nx, lambda i: ref[i - base], edge_ref, base, base + ref.shape[0] - 1)

    second = Lift(nx, lambda i: y2_ref[i], edge_ref)
    one, two = lift(yl, 0), lift(yh, nx - high)
    fix_up = [two.detail(1, n1 - 1)]
    fix_down = [one.detail(1, -1), one.detail(1, 0)]
    up = [second.detail(2, n2 - 1), second.detail(2, n2), put_fixes(second.smooth(2, n2), fix_up)]
    down = [second.detail(2, -1), second.detail(2, 0), put_fixes(second.smooth(2, 0), fix_down)]

    s_lanes = smooth_lanes(spans)
    deep = Lift(nx, lambda i: yc[i], edge_ref)
    for j, tile in enumerate(c_slots(deep, spans, "d", -1, n1 - 1, s_lanes)):
        cc_ref[j] = tile
    for j, tile in enumerate(c_slots(deep, spans, "s", 0, n1, s_lanes)):
        cc_ref[n1 + 1 + j] = tile
    acc = [jnp.zeros((g, TILE), F32)] * 3
    for k in range(1, LEVELS + 1):
        n, here = nx >> k, in_span(spans[k])
        new = [deep.detail(k, n - 1)] + ([deep.detail(k, n), deep.smooth(k, n)] if k > 1 else [None] * 2)
        acc = [a if v is None else jnp.where(here, v, a) for a, v in zip(acc, new)]
    to_pairs(var_ref[2], up + acc, down + [cc_ref[0], cc_ref[1], cc_ref[n1 + 1]], to_one_ref, to_two_ref)
    here = in_span(spans[LEVELS]) if far else lanes() < 0
    far_up_ref[...] = jnp.where(here, deep.detail(LEVELS, nx >> LEVELS), 0.0)
    far_down_ref[...] = jnp.where(here, deep.detail(LEVELS, -1), 0.0)


def put_fixes(tile, fixes):
    lane = lanes()
    for j, fix in enumerate(fixes):
        tile = jnp.where((lane >> 1) == j, pltpu.roll(fix, 1 + 2 * j, 1), tile)
    return tile


def get_fix(tile, j):
    lane = lanes()
    turned = pltpu.roll(tile, TILE - 1 - 2 * j, 1)
    a = jnp.where((lane == 0) | (lane == TILE - 1), turned, 0.0)
    return a, jnp.where(lane == TILE - 1, 4.0 * turned, 0.0)


def weigh(r_ref, bands, value):
    m = r_ref.shape[1]
    vectors = value.shape[0] // m
    hi, lo = split(value)
    out = [[] for _ in bands]
    mats = [r_ref[b] for b in bands]
    mat = mats[0] if len(mats) == 1 else jnp.concatenate(mats, 0)
    for v in range(vectors):
        part = slice(v * m, (v + 1) * m)
        rhs = jnp.concatenate([hi[part], hi[part], lo[part]], 0)
        res = dot(mat, rhs)
        for j in range(len(bands)):
            out[j].append(res[j * m : (j + 1) * m])
    return [jnp.concatenate(o, 0) for o in out]


def band_of(k, kind, y_kind):
    if kind == "s":
        return 3 * LEVELS if y_kind == "s" else 3 * (k - 1)
    return 3 * (k - 1) + (1 if y_kind == "s" else 2)


def weigh_c(r_ref, spans, kind, levels, tiles):
    which = [
        (k, y_kind)
        for k in levels
        for y_kind in ("s", "d")
        if kind == "d" or y_kind == "d" or k == LEVELS
    ]
    value = jnp.concatenate(tiles, 1) if len(tiles) > 1 else tiles[0]
    res = weigh(r_ref, [band_of(k, kind, y_kind) for k, y_kind in which], value)
    outs = []
    for t in range(len(tiles)):
        out = jnp.zeros_like(tiles[t])
        for (k, y_kind), r in zip(which, res):
            out = jnp.where(in_span(spans[k, y_kind]), r[:, t * TILE : (t + 1) * TILE], out)
        outs.append(out)
    return outs


def weigh_m2(r_ref, kind, tiles):
    lane_d = lanes() >= TILE // 2
    value = jnp.concatenate(tiles, 1) if len(tiles) > 1 else tiles[0]
    if kind == "s":
        res = [None, weigh(r_ref, [band_of(2, "s", "d")], value)[0]]
    else:
        res = weigh(r_ref, [band_of(2, "d", "s"), band_of(2, "d", "d")], value)
    outs = []
    for t in range(len(tiles)):
        a, b = (0.0 if r is None else r[:, t * TILE : (t + 1) * TILE] for r in res)
        outs.append(jnp.where(lane_d, b, a))
    return outs


def weigh_tiles(r_ref, band, tiles):
    value = jnp.concatenate(tiles, 1) if len(tiles) > 1 else tiles[0]
    res = weigh(r_ref, [band], value)[0]
    return [res[:, t * TILE : (t + 1) * TILE] for t in range(len(tiles))]


def groups(low, high, size):
    return [list(range(i, min(i + size, high + 1))) for i in range(low, high + 1, size)]


def weighted_plan(nx):
    n2 = nx >> 2
    plan, at = {}, 0
    for name, count in ((("m2", "d"), n2 + 2), (("m2", "s"), n2 + 1), (("c", "d"), n2 + 2), (("c", "s"), n2 + 1)):
        plan[name] = at
        at += count
    return plan, at


def pairs_into(ref, row, g, tiles):
    rows, width = slice(row * g, (row + 1) * g), len(tiles) * TILE
    for t, tile in enumerate(tiles):
        if tile is None:
            continue
        cols = slice(t * TILE, (t + 1) * TILE)
        ref[rows, cols], ref[rows, width + t * TILE : width + (t + 1) * TILE] = split(tile)


def stack_back(s_ref, which, out, spans_of_rows):
    at = 0
    for a, b in spans_of_rows * 2:
        out[at : at + b - a] = s_ref[which, a:b]
        at += b - a


def first_level_rows(ny):
    half, c = ny // 2, (ny + ny // 2, ny + ny // 2 + TILE)
    return [(0, ny), c], [(half, ny), c]


def local_kernel(nx, edge_ref, var_ref, ym_ref, z, y2_ref, cc_ref, p_ref, s_ref, r_ref,
                 vd_ref, vs_ref, w_ref, y, p2, zd, zs, sd, ss):
    g, ny = y.shape[1], y.shape[2]
    _, spans = lane_plan(ny)
    n1, n2 = nx >> 1, nx >> 2
    plan, _ = weighted_plan(nx)
    n = 2 * TILE
    p2[0:n], p2[n : 2 * n] = p_ref[:, 0:ny], p_ref[:, 0:ny]
    rows_d, rows_s = first_level_rows(ny)
    stack_back(s_ref, var_ref[0], sd, rows_d)
    stack_back(s_ref, var_ref[0], ss, rows_s)
    step = 4
    for r in range(0, nx, step):
        res = dot(z[r * g : (r + step) * g], p2[...])
        y[r : r + step] = ym_ref[r : r + step, :, 0:ny] + res.reshape(step, g, ny)

    def lift(columns):
        return Lift(nx, lambda i: y[i, :, columns], edge_ref)

    a, b = (lift(slice(t * TILE, (t + 1) * TILE)) for t in range(2))
    m2 = Lift(nx, lambda i: y2_ref[i], edge_ref)

    def store(name, low, some, tiles):
        for i, tile in zip(some, tiles):
            w_ref[plan[name] + i - low] = tile

    here = in_span(spans[1])

    def weighed_c(kind, low, some):
        base = 0 if kind == "d" else n1 + 1
        out = {}
        by_levels = {}
        for i in some:
            by_levels.setdefault(tuple(k for k in range(1, LEVELS + 1) if i <= nx >> k), []).append(i)
        for levels, part in by_levels.items():
            tiles = weigh_c(r_ref, spans, kind, list(levels), [cc_ref[base + i - low] for i in part])
            for i, tile in zip(part, tiles):
                if i <= n2:
                    w_ref[plan["c", kind] + i - low] = tile
                out[i] = jnp.where(here, tile, 0.0) if i <= n2 else tile
        return [out[i] for i in some]

    for some in groups(-1, n1 - 1, 4):
        ta = weigh_tiles(r_ref, band_of(1, "d", "s"), [a.detail(1, i) for i in some])
        tb = weigh_tiles(r_ref, band_of(1, "d", "d"), [b.detail(1, i) for i in some])
        tc = weighed_c("d", -1, some)
        for i, tiles in zip(some, zip(ta, tb, tc)):
            pairs_into(zd, i + 1, g, tiles)
        first, count = some[0] + 1, len(some)
        vd_ref[first : first + count] = dot(zd[first * g : (first + count) * g], sd[...]).reshape(count, g, ny)
    for some in groups(0, n1, 4):
        tb = weigh_tiles(r_ref, band_of(1, "s", "d"), [b.smooth(1, i) for i in some])
        tc = weighed_c("s", 0, some)
        for i, tiles in zip(some, zip(tb, tc)):
            pairs_into(zs, i, g, tiles)
        first, count = some[0], len(some)
        vs_ref[first : first + count] = dot(zs[first * g : (first + count) * g], ss[...]).reshape(count, g, ny)
    for some in groups(-1, n2, 4):
        store(("m2", "d"), -1, some, weigh_m2(r_ref, "d", [m2.detail(2, i) for i in some]))
    for some in groups(0, n2, 4):
        store(("m2", "s"), 0, some, weigh_m2(r_ref, "s", [m2.smooth(2, i) for i in some]))


def received_keys():
    kinds = (("c", "d"), (-1, 0)), (("c", "s"), (0, 1)), (("m2", "d"), (-1, 0)), (("m2", "s"), (0, 1))
    return [(name, slot) for name, low in kinds for slot in low + ("n-1", "n")]


def received_kernel(ny, edge_ref, var_ref, r_one, r_two, r_ref, g_ref):
    _, spans = lane_plan(ny)
    s_lanes = smooth_lanes(spans)
    lev1 = in_span(spans[1])

    def smooth_c(value):
        return jnp.where(s_lanes, 0.25 * value, 0.0)

    below, above = from_pairs(var_ref[2], r_one, r_two)
    c_d = [below[3], below[4], above[3], above[4]]
    c_s = [
        below[5] + jnp.where(lev1, smooth_c(below[3]), 0.0),
        smooth_c(below[4]),
        smooth_c(above[3]),
        above[5],
    ]
    every = list(range(1, LEVELS + 1))
    tiles = weigh_c(r_ref, spans, "d", every, c_d) + weigh_c(r_ref, spans, "s", every, c_s)
    tiles += weigh_m2(r_ref, "d", [below[0], below[1], above[0], above[1]])
    tiles += weigh_m2(r_ref, "s", [below[2], 0.25 * below[1], 0.25 * above[0], above[2]])
    for j, tile in enumerate(tiles):
        g_ref[j] = tile


def final_kernel(nx, edge_ref, var_ref, vd_ref, vs_ref, w_ref, g_ref, near, r_one, r_two, f_one, f_two,
                 s_ref, r_ref, out_ref, sd, ss, sdeep, zd, zs, zdeep, rows, ot, sem):
    g, ny = ot.shape[1], ot.shape[3]
    _, spans = lane_plan(ny)
    plan, _ = weighted_plan(nx)
    half = ny // 2
    n1, n2 = nx >> 1, nx >> 2
    rows_d, rows_s = first_level_rows(ny)
    stack_back(s_ref, var_ref[0], sd, rows_d)
    stack_back(s_ref, var_ref[0], ss, rows_s)
    stack_back(s_ref, var_ref[0], sdeep, [(ny, ny + half + TILE)])
    s_lanes = smooth_lanes(spans)
    lev1 = in_span(spans[1])

    def smooth_c(value):
        return jnp.where(s_lanes, 0.25 * value, 0.0)

    below, above = from_pairs(var_ref[2], r_one, r_two)
    far_below, far_above = from_pairs(var_ref[3], f_one, f_two)
    odd = var_ref[2] == 1
    first_below = [jnp.where(odd, near[t], far_below[1 + t]) for t in range(2)]
    first_above = [jnp.where(odd, far_above[1 + t], near[2 + t]) for t in range(4)]
    fixes = [get_fix(below[2], 0)] + [get_fix(above[2], j) for j in range(2)]
    a_tiles = [first_below[0] + fixes[0][0], first_above[0] + fixes[1][0], first_above[2] + fixes[2][0]]
    b_tiles = [first_below[1] + fixes[0][1], first_above[1] + fixes[1][1], first_above[3] + fixes[2][1]]
    s_tiles = [0.25 * b_tiles[0], 0.25 * b_tiles[1], 0.25 * b_tiles[2] - 1.75 * b_tiles[1]]
    got = {key: g_ref[j] for j, key in enumerate(received_keys())}
    far_d = weigh_c(r_ref, spans, "d", [LEVELS], [far_below[0], far_above[0]])
    far_s = weigh_c(r_ref, spans, "s", [LEVELS], [smooth_c(far_below[0]), smooth_c(far_above[0])])
    got[("c", "d"), -1] += far_d[0]
    got[("c", "d"), "n"] += far_d[1]
    got[("c", "s"), 0] += far_s[0]
    got[("c", "s"), "n"] += far_s[1]
    keys = [-1, "n-1", "n"]
    ta = weigh_tiles(r_ref, band_of(1, "d", "s"), a_tiles)
    tb = weigh_tiles(r_ref, band_of(1, "d", "d"), b_tiles)
    for j, key in enumerate(keys):
        pairs_into(zd, j, g, [ta[j], tb[j], jnp.where(lev1, got[("c", "d"), key], 0.0)])
    more_d = dot(zd[...], sd[...])
    tb = weigh_tiles(r_ref, band_of(1, "s", "d"), s_tiles)
    for j, key in enumerate([0, "n-1", "n"]):
        pairs_into(zs, j, g, [tb[j], jnp.where(lev1, got[("c", "s"), key], 0.0)])
    more_s = dot(zs[...], ss[...])

    def value_of(array, kind, k, i):
        n, low = nx >> k, -1 if kind == "d" else 0
        v = w_ref[plan[array, kind] + i - low]
        for key, at in ((-1, -1), (0, 0), (1, 1), ("n-1", n - 1), ("n", n)):
            if at == i and ((array, kind), key) in got:
                v = v + got[(array, kind), key]
        return jnp.where(in_span(spans[k]), v, 0.0) if array == "c" else v

    not_last = edge_ref[1]

    def unlift(n, smooth, detail, emit):
        below, before = detail(-1), None
        for i in range(n + 1):
            here = detail(i)
            even = smooth(i) - 0.25 * (below + here)
            if i == n:
                even = even * not_last
            if i > 0:
                emit(2 * i - 1, below + 0.5 * (before + even))
            emit(2 * i, even)
            below, before = here, even

    for k in range(LEVELS, 1, -1):
        base = level_base(nx, k)

        def smooth_deep(i, k=k, base=base):
            v = value_of("c", "s", k, i)
            return v if k == LEVELS else v + rows[base + i]

        if k > 2:
            def emit(i, value, base=level_base(nx, k - 1)):
                rows[base + i] = value
        else:
            def emit(i, value):
                r = slice(i * g, (i + 1) * g)
                zdeep[r, TILE : 2 * TILE], zdeep[r, 3 * TILE : 4 * TILE] = split(value)

        unlift(nx >> k, smooth_deep, lambda i, k=k: value_of("c", "d", k, i), emit)

    def emit_m2(i, value):
        r = slice(i * g, (i + 1) * g)
        zdeep[r, 0:TILE], zdeep[r, 2 * TILE : 3 * TILE] = split(value)

    unlift(n2, lambda i: value_of("m2", "s", 2, i), lambda i: value_of("m2", "d", 2, i), emit_m2)

    extra_d = {-1: more_d[0:g], n1 - 1: more_d[g : 2 * g], n1: more_d[2 * g :]}
    extra_s = {0: more_s[0:g], n1 - 1: more_s[g : 2 * g], n1: more_s[2 * g :]}
    step = 4
    deep = {}

    def smooth_first(i):
        if i % step == 0:
            count = min(step, n1 + 1 - i)
            res = dot(zdeep[i * g : (i + count) * g], sdeep[...])
            for j in range(count):
                deep[i + j] = res[j * g : (j + 1) * g]
        v = deep[i] + vs_ref[i]
        return v + extra_s[i] if i in extra_s else v

    def detail_first(i):
        if i == n1:
            return extra_d[i]
        v = vd_ref[i + 1]
        return v + extra_d[i] if i in extra_d else v

    copies = []

    pending = {}

    def emit_out(i, value):
        if i >= nx:
            return
        pending[i] = value
        r = i - i % 8
        if all(j in pending for j in range(r, r + 8)):
            block = jnp.stack([pending.pop(j) for j in range(r, r + 8)], 0)
            ot[r // 8] = jnp.swapaxes(block, 0, 1)
            copies.append(pltpu.make_async_copy(ot.at[r // 8], out_ref.at[:, pl.ds(r, 8)], sem.at[r // 8]))
            copies[-1].start()

    unlift(n1, smooth_first, detail_first, emit_out)
    for copy in copies:
        copy.wait()


def level_base(nx, k):
    return sum((nx >> j) + 1 for j in range(max(k + 1, 3), LEVELS)) if k > 1 else 0


def swap(value, axis, first, step=1):
    count = lax.axis_size(axis)
    starts = [i for i in range(first, count - step) if (i - first) // step % 2 == 0]
    return lax.ppermute(value, axis, [p for i in starts for p in ((i, i + step), (i + step, i))])


def per_device(control, band_roots):
    vectors, m, nx, ny = control.shape
    g = vectors * m
    half = ny // 2
    gx, gy = lax.axis_size("gx"), lax.axis_size("gy")
    per = TILE // SLOT
    assert half == TILE and nx % (2 * per) == 0
    far = (nx >> LEVELS) < 2 and gx > 2
    consts = y_constants(ny, gy)
    main_mat, clo_mat, ehi_mat, elo_mat, s_mat, p_mat = (jnp.asarray(t) for t in consts)
    n1 = nx >> 1
    mains = ny + half

    r_hi = lax.reduce_precision(band_roots, 8, 7)
    r_lo = band_roots - r_hi
    roots = jnp.concatenate([r_hi.astype(BF), r_lo.astype(BF), r_hi.astype(BF)], 2)

    hbm = pl.BlockSpec(memory_space=pl.ANY)
    vmem = pl.BlockSpec(memory_space=pltpu.VMEM)

    def call(kernel, ins, outs, scratches, out_specs=None):
        def body(*refs):
            kernel(*device_place(gx, gy), *refs)

        return pl.pallas_call(
            body,
            out_shape=tuple(jax.ShapeDtypeStruct(*s) for s in outs),
            in_specs=[s for _, s in ins],
            out_specs=out_specs or (vmem,) * len(outs),
            scratch_shapes=scratches,
            compiler_params=pltpu.CompilerParams(vmem_limit_bytes=VMEM_LIMIT),
        )(*[a for a, _ in ins])

    tile = (g, TILE)
    rows3 = control.reshape(g, nx, ny)
    far_hbm = pl.BlockSpec(memory_space=pltpu.HBM)
    xhl, one, two, rows = call(
        partial(first_kernel, nx),
        [
            (pltpu.with_memory_space_constraint(t, pltpu.HBM), far_hbm)
            for t in (rows3, ehi_mat, elo_mat, main_mat)
        ],
        [((nx * g, 2 * ny), BF), ((nx // per,) + tile, F32), ((nx // per,) + tile, F32),
         ((6,) + tile, F32)],
        [pltpu.VMEM((nx // per, g, per, ny), F32), pltpu.VMEM((3 * TILE, TILE), BF),
         pltpu.VMEM((2 * ny, ny), BF), pltpu.VMEM((nx * g, 3 * TILE), BF), pltpu.VMEM((4, g, ny), F32), pltpu.VMEM((4, g, ny), F32),
         pltpu.SemaphoreType.DMA((nx + 4,))],
    )
    near = swap(rows, "gx", 0)
    got_one = swap(one, "gy", 0)
    got_two = swap(two, "gy", 1)
    (ym,) = call(
        partial(main_kernel, nx),
        [(xhl, vmem), (main_mat, vmem), (clo_mat, vmem)],
        [((nx, g, mains + TILE), F32)],
        [pltpu.VMEM((2 * ny, mains + TILE), BF)],
    )
    slots = 2 * n1 + 2
    sent = call(
        partial(send_kernel, nx, far),
        [(ym, vmem), (got_one, vmem), (got_two, vmem), (p_mat, vmem)],
        [((6,) + tile, F32), ((6,) + tile, F32), ((slots,) + tile, F32), ((nx * g, 4 * TILE), BF), ((nx,) + tile, F32)]
        + [(tile, F32)] * 2,
        [
            pltpu.VMEM((nx,) + tile, F32),
            pltpu.VMEM((4,) + tile, F32),
            pltpu.VMEM((4,) + tile, F32),
            pltpu.VMEM((4 * TILE, mains + TILE), BF),
        ],
    )
    got = [near, swap(sent[0], "gx", 0), swap(sent[1], "gx", 1)]
    far_one, far_two = call(relay_kernel, [(t, vmem) for t in (near, sent[5], sent[6])], [((5,) + tile, F32)] * 2, [])
    got += [swap(far_one, "gx", 0, 2), swap(far_two, "gx", 2, 2)]

    _, count = weighted_plan(nx)
    vd, vs, w = call(
        partial(local_kernel, nx),
        [(ym, vmem), (sent[3], vmem), (sent[4], vmem), (sent[2], vmem), (p_mat, vmem), (s_mat, vmem), (roots, vmem)],
        [((n1 + 1, g, ny), F32), ((n1 + 1, g, ny), F32), ((count,) + tile, F32)],
        [
            pltpu.VMEM((nx, g, ny), F32),
            pltpu.VMEM((4 * TILE, ny), BF),
            pltpu.VMEM(((n1 + 1) * g, 6 * TILE), BF),
            pltpu.VMEM(((n1 + 1) * g, 4 * TILE), BF),
            pltpu.VMEM((6 * TILE, ny), BF),
            pltpu.VMEM((4 * TILE, ny), BF),
        ],
    )
    (weighed,) = call(
        partial(received_kernel, ny), [(t, vmem) for t in (got[1], got[2], roots)], [((16,) + tile, F32)], []
    )
    (out,) = call(
        partial(final_kernel, nx),
        [(t, vmem) for t in [vd, vs, w, weighed] + got + [s_mat, roots]],
        [((g, nx, ny), F32)],
        [
            pltpu.VMEM((6 * TILE, ny), BF),
            pltpu.VMEM((4 * TILE, ny), BF),
            pltpu.VMEM((4 * TILE, ny), BF),
            pltpu.VMEM((3 * g, 6 * TILE), BF),
            pltpu.VMEM((3 * g, 4 * TILE), BF),
            pltpu.VMEM(((n1 + 1) * g, 4 * TILE), BF),
            pltpu.VMEM((level_base(nx, 1) + sum((nx >> j) + 1 for j in range(2, LEVELS)),) + tile, F32),
            pltpu.VMEM((nx // 8, g, 8, ny), F32),
            pltpu.SemaphoreType.DMA((nx // 8,)),
        ],
        (hbm,),
    )
    return out.reshape(control.shape)


def solution(mesh):
    spec = P(None, None, "gx", "gy")
    return jax.shard_map(per_device, mesh=mesh, in_specs=(spec, P()), out_specs=spec, check_vma=False)
```
